32 devices in a mesh: wide: 16 (over z, y, x), narrow: 2 (over core).
Axes of the slice: x: 2, y: 2, z: 4, core: 2. Of those that a mesh axis runs over, the one named last changes fastest.
Arguments:
- latent_tokens: float32 [384, 16384], P('narrow', 'wide'), may hold values from -52 to 52
- labels: int32 [64], P('wide'), may hold values from 0 to 1000
- timesteps: int32 [64], P('wide'), may hold values from 0 to 999
- class_table: bfloat16 [1001, 384], replicated, may hold values from -6 to 6
- modulation_weight: bfloat16 [384, 6, 384], P('wide', None, 'narrow'), may hold values from -0.3125 to 0.3125
- modulation_bias: float32 [6, 384], P(None, 'narrow'), may hold values from -3 to 3
- in_weight: bfloat16 [384, 3, 384], P('wide', None, 'narrow'), may hold values from -0.21875 to 0.21875
- in_bias: float32 [2, 384], P(None, 'narrow'), may hold values from -3 to 3
- out_weight: bfloat16 [384, 384], P('narrow', 'wide'), may hold values from -1.25 to 1.25
- out_bias: float32 [384], P('narrow'), may hold values from -3 to 3
- up_weight: bfloat16 [384, 1536], P('wide', 'narrow'), may hold values from -0.3125 to 0.3125
- up_bias: float32 [1536], P('narrow'), may hold values from -3 to 3
- down_weight: bfloat16 [1536, 384], P('narrow', 'wide'), may hold values from -0.3125 to 0.3125
- down_bias: float32 [384], P('narrow'), may hold values from -3 to 3
- cotangent: float32 [384, 16384], P('narrow', 'wide'), may hold values from -6 to 6
Outputs:
- block_output: float32 [384, 16384], P('narrow', 'wide')
- token_grads: float32 [384, 16384], P('narrow', 'wide')
- condition_grads: float32 [64, 384], P('wide')
- table_grads: float32 [1001, 384], replicated
- modulation_grads: float32 [384, 6, 384], P('wide', None, 'narrow')
- modulation_bias_grads: float32 [6, 384], P(None, 'narrow')
- in_grads: float32 [384, 3, 384], P('wide', None, 'narrow')
- in_bias_grads: float32 [2, 384], P(None, 'narrow')
- out_grads: float32 [384, 384], P('narrow', 'wide')
- out_bias_grads: float32 [384], P('narrow')
- up_grads: float32 [384, 1536], P('wide', 'narrow')
- up_bias_grads: float32 [1536], P('narrow')
- down_grads: float32 [1536, 384], P('narrow', 'wide')
- down_bias_grads: float32 [384], P('narrow')
The draws below stay inside these ranges and needn't reach their ends.
All inputs are finite; a program needn't handle non-finite values.
Results may differ from the reference program's by a relative error of at most 0.017.
Values may be sent and summed in bfloat16 or wider, within the bound.
A program may use at most 128 MiB of HBM per device.

```python
import math
import jax
import jax.numpy as jnp
from jax import lax

D = 384
H = 6
HD = 64
FF = 1536
SEQ = 256
NCLS = 1001
NSTEPS = 1000
LATENTS = 64
TOKENS = 16384


def draw_latent_tokens(key, part):
    noise_key, column_key, row_key = jax.random.split(key, 3)
    position = jnp.arange(D, dtype=jnp.float32) / (D - 1)
    column_scale = jnp.exp(math.log(4.0) * position + jax.random.uniform(column_key, (D,), jnp.float32, math.log(0.5), math.log(1.5)))
    noise = jnp.clip(jax.random.normal(noise_key, (TOKENS, D), jnp.float32), -4.0, 4.0)
    row_scale = jnp.exp(jax.random.uniform(row_key, (TOKENS, 1), jnp.float32, 0.0, math.log(10.0)))
    return jnp.transpose(noise * row_scale * column_scale[None, :] * 0.15)


def plant(drawn, own_key, smallest, high):
    shape = drawn.shape
    spot = [jax.random.randint(jax.random.fold_in(own_key, axis), (), 0, shape[axis]) for axis in range(len(shape))]
    drawn = drawn.at[tuple(spot)].set(smallest)
    longest = shape.index(max(shape))
    spot[longest] = (spot[longest] + 1) % shape[longest]
    return drawn.at[tuple(spot)].set(high)


def with_spikes(values, key, source, target, shards_of, factor):
    owner, partner = [(jnp.arange(values.shape[dim]) // (values.shape[dim] // shards_of)).reshape([-1 if axis == dim else 1 for axis in range(values.ndim)]) for dim in (source, target)]
    chosen = jax.random.permutation(key, shards_of)[partner]
    strong = (owner == chosen) | (owner == (partner + shards_of // 2) % shards_of)
    return jnp.where(strong, factor * values, values)


def block_levels(rng, extent, cuts, least, largest):
    level = 1.0
    for dim, blocks in cuts:
        draws = jax.random.uniform(jax.random.fold_in(jax.random.fold_in(rng, 6), dim), (blocks,), jnp.float32, least / len(cuts), largest / len(cuts))
        level = level * jnp.repeat(jnp.exp(draws), extent[dim] // blocks).reshape((-1,) + (1,) * (len(extent) - 1 - dim))
    return level


def normal_values(stream_key, shape, scale, most, shards=(), kind=jnp.bfloat16):
    values = jax.random.normal(stream_key, shape, jnp.float32) * scale
    if len(shards) > 0:
        values = block_levels(stream_key, shape, shards, -0.22, 0.18) * values
    return jnp.clip(values, min=-most, max=most).astype(kind)


def bell_draw_with(own_key, shape, deviation, reach, cuts, heavy, held_as=jnp.bfloat16):
    drawn = deviation * jax.random.normal(own_key, shape, jnp.float32)
    if cuts:
        drawn = drawn * block_levels(own_key, shape, cuts, -0.22, 0.18)
    return jnp.clip(with_spikes(drawn, jax.random.fold_in(own_key, 3), *heavy), -reach, reach).astype(held_as)


def setup_inputs(seed: int = 0) -> dict:
    key_list = jax.random.split(jax.random.key(seed), 16)
    return {
        "latent_tokens": draw_latent_tokens(jax.random.fold_in(key_list[15], 71), 0),
        "labels": plant(jax.random.randint(key_list[1], (LATENTS,), 0, NCLS), jax.random.fold_in(key_list[1], 1), 0, NCLS - 1).astype(jnp.int32),
        "timesteps": plant(jax.random.randint(key_list[2], (LATENTS,), 0, NSTEPS), jax.random.fold_in(key_list[2], 1), 0, NSTEPS - 1).astype(jnp.int32),
        "class_table": normal_values(key_list[3], (NCLS, D), 1.0, 6.0),
        "modulation_weight": normal_values(key_list[4], (D, 6, D), D ** -0.5, 0.3125, ((0, 16), (2, 2))),
        "modulation_bias": normal_values(key_list[5], (6, D), 0.5, 3.0, ((1, 2),), jnp.float32),
        "in_weight": normal_values(key_list[6], (D, 3, D), (2 * D) ** -0.5, 0.21875, ((0, 16), (2, 2))),
        "in_bias": normal_values(key_list[7], (2, D), 0.5, 3.0, ((1, 2),), jnp.float32),
        "out_weight": normal_values(key_list[8], (D, D), (D // 16) ** -0.5, 1.25, ((0, 2), (1, 16))),
        "out_bias": normal_values(key_list[9], (D,), 0.5, 3.0, ((0, 2),), jnp.float32),
        "up_weight": normal_values(key_list[10], (D, FF), D ** -0.5, 0.3125, ((0, 16), (1, 2))),
        "up_bias": normal_values(key_list[11], (FF,), 0.5, 3.0, ((0, 2),), jnp.float32),
        "down_weight": normal_values(key_list[12], (FF, D), (FF // 4) ** -0.5, 0.3125, ((0, 2), (1, 16))),
        "down_bias": normal_values(key_list[13], (D,), 0.5, 3.0, ((0, 2),), jnp.float32),
        "cotangent": bell_draw_with(key_list[14], (D, TOKENS), 1.0, 6.0, ((0, 2), (1, 16)), (1, 0, 16, 2.0), jnp.float32),
    }


EPS = 1e-06
GELU_K = 0.7978845608028654
GELU_A = 0.044715

def widen(array):
    return array.astype(jnp.float32)

def time_features(timesteps):
    half_width = D // 2
    frequencies = jnp.exp(jnp.arange(half_width, dtype=jnp.float32) * (-math.log(10000.0) / half_width))
    angles = timesteps.astype(jnp.float32)[:, None] * frequencies[None, :]
    return jnp.concatenate([jnp.cos(angles), jnp.sin(angles)], axis=1)

def gelu_value(inputs):
    inner = GELU_K * (inputs + GELU_A * inputs * inputs * inputs)
    return 0.5 * inputs * (1.0 + jnp.tanh(inner))

def gelu_slope(inputs):
    inner = GELU_K * (inputs + GELU_A * inputs * inputs * inputs)
    tangent = jnp.tanh(inner)
    return 0.5 * (1.0 + tangent) + 0.5 * inputs * (1.0 - tangent * tangent) * GELU_K * (1.0 + 3.0 * GELU_A * inputs * inputs)

def silu_slope(inputs):
    sigmoid = jax.nn.sigmoid(inputs)
    return sigmoid * (1.0 + inputs * (1.0 - sigmoid))

def norm_rows(values):
    centre = values - lax.optimization_barrier(jnp.mean(values, axis=-1, keepdims=True))
    inv_std = lax.rsqrt(lax.optimization_barrier(jnp.mean(centre * centre, axis=-1, keepdims=True)) + EPS)
    return (centre * inv_std, inv_std)

def norm_back(grad_norm, normed, inv_std):
    return inv_std * (grad_norm - lax.optimization_barrier(jnp.mean(grad_norm, axis=-1, keepdims=True)) - normed * lax.optimization_barrier(jnp.mean(grad_norm * normed, axis=-1, keepdims=True)))

def modulate_back(grad_mod, normed, scale):
    return (lax.optimization_barrier(jnp.sum(grad_mod, axis=1)), lax.optimization_barrier(jnp.sum(grad_mod * normed, axis=1)), grad_mod * (1.0 + scale))

def forward_backward(params, inputs):
    class_table, modulation_weight, modulation_bias, in_weight, in_bias, out_weight, out_bias, up_weight, up_bias, down_weight, down_bias = params
    tokens_in, cotangent, labels, timesteps = inputs
    latent_count = labels.shape[0]
    hidden_in = tokens_in.reshape(latent_count, SEQ, D)
    upstream = cotangent.reshape(latent_count, SEQ, D)
    head_shape = (latent_count, SEQ, H, HD)
    score_scale = HD ** (-0.5)
    condition = widen(class_table[labels]) + time_features(timesteps)
    activated = jax.nn.silu(condition).astype(jnp.bfloat16)
    modulation = jnp.einsum('bd,djf->bjf', widen(activated), widen(modulation_weight)) + modulation_bias
    shift_one, scale_one, gate_one, shift_two, scale_two, gate_two = [modulation[:, which][:, None, :] for which in range(6)]
    normed_one, inv_one = norm_rows(hidden_in)
    modulated_one = (normed_one * (1.0 + scale_one) + shift_one).astype(jnp.bfloat16)
    projected = jnp.einsum('bsd,djf->bsjf', widen(modulated_one), widen(in_weight))
    queries = (projected[:, :, 0] + in_bias[0]).astype(jnp.bfloat16).reshape(head_shape)
    key_rows = projected[:, :, 1].astype(jnp.bfloat16).reshape(head_shape)
    value_rows = (projected[:, :, 2] + in_bias[1]).astype(jnp.bfloat16).reshape(head_shape)
    scores = jnp.einsum('bshe,bthe->bhst', widen(queries), widen(key_rows)) * score_scale
    log_total = jnp.log(lax.optimization_barrier(jnp.sum(jnp.exp(scores), axis=-1, keepdims=True)))
    mixing = jnp.exp(scores - log_total).astype(jnp.bfloat16)
    attended = jnp.einsum('bhst,bthe->bshe', widen(mixing), widen(value_rows)).astype(jnp.bfloat16).reshape(latent_count, SEQ, D)
    attention = jnp.einsum('bsd,de->bse', widen(attended), widen(out_weight)) + out_bias
    middle = hidden_in + gate_one * attention
    normed_two, inv_two = norm_rows(middle)
    modulated_two = (normed_two * (1.0 + scale_two) + shift_two).astype(jnp.bfloat16)
    pre_act = jnp.einsum('bsd,df->bsf', widen(modulated_two), widen(up_weight)) + up_bias
    activation = gelu_value(pre_act).astype(jnp.bfloat16)
    feedforward = jnp.einsum('bsf,fd->bsd', widen(activation), widen(down_weight)) + down_bias
    block_output = middle + gate_two * feedforward
    gate_two_grad = lax.optimization_barrier(jnp.sum(upstream * feedforward, axis=1))
    grad_ff = gate_two * upstream
    grad_ff_bf = grad_ff.astype(jnp.bfloat16)
    down_total = jnp.einsum('bsf,bsd->fd', widen(activation), widen(grad_ff_bf))
    grad_pre = jnp.einsum('bsd,fd->bsf', widen(grad_ff_bf), widen(down_weight)) * gelu_slope(pre_act)
    grad_pre_bf = grad_pre.astype(jnp.bfloat16)
    up_total = jnp.einsum('bsd,bsf->df', widen(modulated_two), widen(grad_pre_bf))
    grad_mod_two = jnp.einsum('bsf,df->bsd', widen(grad_pre_bf), widen(up_weight))
    shift_two_grad, scale_two_grad, grad_norm_two = modulate_back(grad_mod_two, normed_two, scale_two)
    grad_middle = upstream + norm_back(grad_norm_two, normed_two, inv_two)
    gate_one_grad = lax.optimization_barrier(jnp.sum(grad_middle * attention, axis=1))
    grad_att = gate_one * grad_middle
    grad_att_bf = grad_att.astype(jnp.bfloat16)
    out_total = jnp.einsum('bsd,bse->de', widen(attended), widen(grad_att_bf))
    grad_attended = jnp.einsum('bse,de->bsd', widen(grad_att_bf), widen(out_weight)).astype(jnp.bfloat16).reshape(head_shape)
    weights_full = jnp.exp(scores - log_total)
    grad_mixing = jnp.einsum('bshe,bthe->bhst', widen(grad_attended), widen(value_rows))
    row_dots = lax.optimization_barrier(jnp.sum(weights_full * grad_mixing, axis=-1, keepdims=True))
    grad_scores = (weights_full * (grad_mixing - row_dots) * score_scale).astype(jnp.bfloat16)
    grad_queries = jnp.einsum('bhst,bthe->bshe', widen(grad_scores), widen(key_rows)).reshape(latent_count, SEQ, D)
    grad_keys = jnp.einsum('bhst,bshe->bthe', widen(grad_scores), widen(queries)).reshape(latent_count, SEQ, D)
    grad_values = jnp.einsum('bhst,bshe->bthe', widen(mixing), widen(grad_attended)).reshape(latent_count, SEQ, D)
    grad_proj = jnp.stack([grad_queries, grad_keys, grad_values], axis=2).astype(jnp.bfloat16)
    in_total = jnp.einsum('bsd,bsjf->djf', widen(modulated_one), widen(grad_proj))
    grad_mod_one = jnp.einsum('bsjf,djf->bsd', widen(grad_proj), widen(in_weight))
    shift_one_grad, scale_one_grad, grad_norm_one = modulate_back(grad_mod_one, normed_one, scale_one)
    token_grads = grad_middle + norm_back(grad_norm_one, normed_one, inv_one)
    grad_modulation = jnp.stack([shift_one_grad, scale_one_grad, gate_one_grad, shift_two_grad, scale_two_grad, gate_two_grad], axis=1)
    grad_modulation_bf = grad_modulation.astype(jnp.bfloat16)
    modulation_total = jnp.einsum('bd,bjf->djf', widen(activated), widen(grad_modulation_bf))
    grad_activated = jnp.einsum('bjf,djf->bd', widen(grad_modulation_bf), widen(modulation_weight))
    condition_grads = grad_activated * silu_slope(condition) * SEQ ** (-0.5)
    table_part = jax.ops.segment_sum(condition_grads, labels, num_segments=NCLS)
    in_bias_part = jnp.stack([lax.optimization_barrier(jnp.sum(grad_queries, axis=(0, 1))), lax.optimization_barrier(jnp.sum(grad_values, axis=(0, 1)))])
    grads = (table_part, modulation_total, lax.optimization_barrier(jnp.sum(grad_modulation, axis=0)), in_total, in_bias_part, out_total, lax.optimization_barrier(jnp.sum(grad_att, axis=(0, 1))), up_total, lax.optimization_barrier(jnp.sum(grad_pre, axis=(0, 1))), down_total, lax.optimization_barrier(jnp.sum(grad_ff, axis=(0, 1))))
    outputs = (block_output.reshape(-1, D), token_grads.reshape(-1, D), condition_grads)
    return (outputs, grads)

def reference(latent_tokens, labels, timesteps, class_table, modulation_weight, modulation_bias, in_weight, in_bias, out_weight, out_bias, up_weight, up_bias, down_weight, down_bias, cotangent):
    block_size = math.gcd(LATENTS, 16)
    steps_count = LATENTS // block_size
    params = (class_table, modulation_weight, modulation_bias, in_weight, in_bias, out_weight, out_bias, up_weight, up_bias, down_weight, down_bias)
    token_rows = jnp.transpose(latent_tokens)
    upstream_rows = jnp.transpose(cotangent)
    inputs = (token_rows.reshape(steps_count, block_size * SEQ, D), upstream_rows.reshape(steps_count, block_size * SEQ, D), labels.reshape(steps_count, block_size).astype(jnp.int32), timesteps.reshape(steps_count, block_size).astype(jnp.int32))
    zero_grads = (jnp.zeros((NCLS, D), jnp.float32), jnp.zeros((D, 6, D), jnp.float32), jnp.zeros((6, D), jnp.float32), jnp.zeros((D, 3, D), jnp.float32), jnp.zeros((2, D), jnp.float32), jnp.zeros((D, D), jnp.float32), jnp.zeros((D,), jnp.float32), jnp.zeros((D, FF), jnp.float32), jnp.zeros((FF,), jnp.float32), jnp.zeros((FF, D), jnp.float32), jnp.zeros((D,), jnp.float32))

    def step_block(totals, piece):
        outputs, grads = forward_backward(params, piece)
        return (jax.tree.map(jnp.add, totals, grads), outputs)
    totals, stacked = lax.scan(step_block, zero_grads, inputs)
    weight_scale = TOKENS ** (-0.5)
    block_output = jnp.transpose(stacked[0].reshape(TOKENS, D))
    token_grads = jnp.transpose(stacked[1].reshape(TOKENS, D))
    condition_grads = stacked[2].reshape(LATENTS, D)
    return (block_output, token_grads, condition_grads, totals[0], totals[1] * weight_scale, totals[2] * weight_scale, totals[3] * weight_scale, totals[4] * weight_scale, totals[5] * weight_scale, totals[6] * weight_scale, totals[7] * weight_scale, totals[8] * weight_scale, totals[9] * weight_scale, totals[10] * weight_scale)
```

```python
import functools
import math

import jax
import jax.numpy as jnp
from jax import lax
from jax.experimental import pallas as pl
from jax.experimental.pallas import tpu as pltpu
from jax.sharding import PartitionSpec as P

D = 384
HD = 64
LANES = 128
MESH = pl.DeviceIdType.MESH
VMEM_LIMIT = 60 * 1024 * 1024


EPS = 1e-06
GELU_K = 0.7978845608028654
GELU_A = 0.044715


def time_features(timesteps):
    half_width = D // 2
    frequencies = jnp.exp(
        jnp.arange(half_width, dtype=jnp.float32) * (-math.log(10000.0) / half_width)
    )
    angles = timesteps.astype(jnp.float32)[:, None] * frequencies[None, :]
    return jnp.concatenate([jnp.cos(angles), jnp.sin(angles)], axis=1)


def gelu_value(inputs):
    inner = GELU_K * (inputs + GELU_A * inputs * inputs * inputs)
    return 0.5 * inputs * (1.0 + jnp.tanh(inner))


def gelu_slope(inputs):
    inner = GELU_K * (inputs + GELU_A * inputs * inputs * inputs)
    tangent = jnp.tanh(inner)
    return 0.5 * (1.0 + tangent) + 0.5 * inputs * (1.0 - tangent * tangent) * GELU_K * (
        1.0 + 3.0 * GELU_A * inputs * inputs
    )


def silu_slope(inputs):
    sigmoid = jax.nn.sigmoid(inputs)
    return sigmoid * (1.0 + inputs * (1.0 - sigmoid))


def plane(wide):
    side = max(1, round((wide / 2) ** (1 / 3)))
    while wide % (side * side):
        side -= 1
    return wide // (side * side), side


class Place:
    def __init__(self, wide):
        self.deep, self.side = plane(wide)
        self.me = lax.axis_index("wide")
        self.core = lax.axis_index("narrow")
        self.z = self.me // (self.side * self.side)
        rest = self.me % (self.side * self.side)
        major, minor = rest // self.side, rest % self.side
        self.p = major + self.core * (minor - major)
        self.q = minor + self.core * (major - minor)
        self.p_stride = self.side + self.core * (1 - self.side)
        self.q_stride = 1 + self.core * (self.side - 1)

    def index(self, dz, dp, dq):
        return (
            ((self.z + dz) % self.deep) * (self.side * self.side)
            + ((self.p + dp) % self.side) * self.p_stride
            + ((self.q + dq) % self.side) * self.q_stride
        )

    def line_peers(self):
        return (
            [self.index(dz, 0, 0) for dz in range(1, self.deep)]
            + [self.index(0, dp, 0) for dp in range(1, self.side)]
            + [self.index(0, 0, dq) for dq in range(1, self.side)]
        )


def gather_kernel(
    wide, shard, tokens, upstream, biases,
    full, tokens_out, upstream_out, biases_out,
    send, recv, pair_send, pair_recv, swap_send, swap_recv, local,
):
    at = Place(wide)
    core, other = at.core, 1 - at.core
    barrier = pltpu.get_barrier_semaphore()
    peers = at.line_peers()
    for peer in peers:
        pl.semaphore_signal(barrier, 1, device_id=(peer, core), device_id_type=MESH)
    pl.semaphore_signal(barrier, 1, device_id=(at.me, other), device_id_type=MESH)
    pl.semaphore_wait(barrier, len(peers) + 1)
    waits = []
    count = 0

    def push(src, block, target):
        nonlocal count
        copy = pltpu.make_async_remote_copy(
            src, full.at[core, block], send.at[count], recv.at[block],
            device_id=(target, core), device_id_type=MESH,
        )
        copy.start()
        waits.append(copy)
        count += 1

    def share(src, block):
        copy = pltpu.make_async_remote_copy(
            src, full.at[core, block], pair_send.at[block], pair_recv.at[block],
            device_id=(at.me, other), device_id_type=MESH,
        )
        copy.start()
        waits.append(copy)

    def arrived(block):
        pltpu.make_async_copy(full.at[core, block], full.at[core, block], recv.at[block]).wait()

    for dz in range(1, at.deep):
        push(shard, at.me, at.index(dz, 0, 0))
    for dp in range(1, at.side):
        push(shard, at.me, at.index(0, dp, 0))
    for dq in range(1, at.side):
        push(shard, at.me, at.index(0, 0, dq))
    share(shard, at.me)
    half = tokens_out.shape[2]
    mine = pl.ds(pl.multiple_of(core * half, LANES), half)
    theirs = pl.ds(pl.multiple_of(other * half, LANES), half)
    for which, (src, dst) in enumerate(
        [(tokens.at[:, theirs], tokens_out), (upstream.at[:, theirs], upstream_out), (biases, biases_out)]
    ):
        copy = pltpu.make_async_remote_copy(
            src, dst.at[core], swap_send.at[which], swap_recv.at[which],
            device_id=(at.me, other), device_id_type=MESH,
        )
        copy.start()
        waits.append(copy)
    keeps = [
        pltpu.make_async_copy(src, dst, local.at[which])
        for which, (src, dst) in enumerate(
            [
                (tokens.at[:, mine], tokens_out.at[core]),
                (upstream.at[:, mine], upstream_out.at[core]),
                (biases, biases_out.at[core]),
                (shard, full.at[core, at.me]),
            ]
        )
    ]
    for keep in keeps:
        keep.start()
    for dz in range(1, at.deep):
        block = at.index(dz, 0, 0)
        arrived(block)
        for dp in range(1, at.side):
            push(full.at[core, block], block, at.index(0, dp, 0))
        for dq in range(1, at.side):
            push(full.at[core, block], block, at.index(0, 0, dq))
        share(full.at[core, block], block)
    for dz in range(at.deep):
        for dp in range(1, at.side):
            block = at.index(dz, dp, 0)
            arrived(block)
            for dq in range(1, at.side):
                push(full.at[core, block], block, at.index(0, 0, dq))
            share(full.at[core, block], block)
    for dz in range(at.deep):
        for dq in range(1, at.side):
            for dp in range(at.side):
                block = at.index(dz, dp, dq)
                arrived(block)
                share(full.at[core, block], block)
    for keep in keeps:
        keep.wait()
    for copy in waits:
        copy.wait_send()
    for block in range(wide):
        pltpu.make_async_copy(full.at[core, block], full.at[core, block], pair_recv.at[block]).wait()
    for which, (src, dst) in enumerate(
        [(tokens_out.at[core], None), (upstream_out.at[core], None), (biases_out.at[core], None)]
    ):
        pltpu.make_async_copy(src, src, swap_recv.at[which]).wait()


def gather_all(wide, shard, tokens, upstream, biases):
    rows, columns = shard.shape
    features, count = tokens.shape
    deep, side = plane(wide)
    sends = wide * (deep + 2 * side)
    vmem = pl.BlockSpec(memory_space=pltpu.VMEM)
    return pl.pallas_call(
        functools.partial(gather_kernel, wide),
        name="gather",
        out_shape=(
            jax.ShapeDtypeStruct((2, wide, rows, columns), shard.dtype),
            jax.ShapeDtypeStruct((2, features, count // 2), tokens.dtype),
            jax.ShapeDtypeStruct((2, features, count // 2), tokens.dtype),
            jax.ShapeDtypeStruct((2,) + biases.shape, biases.dtype),
        ),
        in_specs=[vmem] * 4,
        out_specs=(vmem,) * 4,
        scratch_shapes=[
            pltpu.SemaphoreType.DMA((sends,)),
            pltpu.SemaphoreType.DMA((wide,)),
            pltpu.SemaphoreType.DMA((wide,)),
            pltpu.SemaphoreType.DMA((wide,)),
            pltpu.SemaphoreType.DMA((3,)),
            pltpu.SemaphoreType.DMA((3,)),
            pltpu.SemaphoreType.DMA((4,)),
        ],
        compiler_params=pltpu.CompilerParams(
            collective_id=0, has_side_effects=True, vmem_limit_bytes=VMEM_LIMIT
        ),
    )(shard, tokens, upstream, biases)


def scatter_kernel(
    wide, parts, message, block_out, token_out,
    total, messages, block_half, token_half,
    from_pair, from_q, from_p, from_z, sums,
    send, pair_send, pair_recv, q_recv, p_recv, z_recv,
    note_send, note_recv, swap_send, swap_recv, local,
):
    at = Place(wide)
    core, other = at.core, 1 - at.core
    barrier = pltpu.get_barrier_semaphore()
    for step in range(wide):
        peer = (at.me + step) % wide
        if step:
            pl.semaphore_signal(barrier, 1, device_id=(peer, core), device_id_type=MESH)
        pl.semaphore_signal(barrier, 1, device_id=(peer, other), device_id_type=MESH)
    pl.semaphore_wait(barrier, 2 * wide - 1)
    waits = []

    deep, side = at.deep, at.side
    order = (
        [(dz, dp, dq) for dq in range(1, side) for dp in range(side) for dz in range(deep)]
        + [(dz, dp, 0) for dp in range(1, side) for dz in range(deep)]
        + [(dz, 0, 0) for dz in range(1, deep)]
        + [(0, 0, 0)]
    )
    for dz, dp, dq in order:
        block = at.index(dz, dp, dq)
        copy = pltpu.make_async_remote_copy(
            parts.at[other, block], from_pair.at[block], pair_send.at[block], pair_recv.at[block],
            device_id=(at.me, other), device_id_type=MESH,
        )
        copy.start()
        waits.append(copy)
    for step in range(wide):
        peer = (at.me + step) % wide
        for flip in range(2):
            if step == 0 and flip == 0:
                continue
            seat = core if flip == 0 else other
            copy = pltpu.make_async_remote_copy(
                message.at[seat], messages.at[at.me, core],
                note_send.at[step, flip], note_recv.at[at.me, core],
                device_id=(peer, seat), device_id_type=MESH,
            )
            copy.start()
            waits.append(copy)
    half = block_out.shape[0] // 2
    span = block_out.shape[1]
    columns = pl.ds(pl.multiple_of(core * span, LANES), span)
    mine = pl.ds(pl.multiple_of(core * half, 8), half)
    theirs = pl.ds(pl.multiple_of(other * half, 8), half)
    keeps = [pltpu.make_async_copy(message.at[core], messages.at[at.me, core], local.at[2])]
    for which, (src, dst) in enumerate([(block_out, block_half), (token_out, token_half)]):
        copy = pltpu.make_async_remote_copy(
            src.at[theirs], dst.at[:, columns], swap_send.at[which], swap_recv.at[which],
            device_id=(at.me, other), device_id_type=MESH,
        )
        copy.start()
        waits.append(copy)
        keeps.append(pltpu.make_async_copy(src.at[mine], dst.at[:, columns], local.at[which]))
    for keep in keeps:
        keep.start()

    def landed(ref, sem):
        pltpu.make_async_copy(ref, ref, sem).wait()

    f32 = jnp.float32
    for number, (dz, dp, dq) in enumerate(order):
        block = at.index(dz, dp, dq)
        landed(from_pair.at[block], pair_recv.at[block])
        value = parts[core, block].astype(f32) + from_pair[block].astype(f32)
        zs, ps = (at.z + dz) % deep, (at.p + dp) % side
        if dq == 0:
            for s in range(side - 1):
                landed(from_q.at[s, zs, ps], q_recv.at[s, zs, ps])
                value += from_q[s, zs, ps].astype(f32)
            if dp == 0:
                for s in range(side - 1):
                    landed(from_p.at[s, zs], p_recv.at[s, zs])
                    value += from_p[s, zs].astype(f32)
        if dq:
            target, slot, sem = (
                at.index(0, 0, dq), from_q.at[side - 1 - dq, zs, ps], q_recv.at[side - 1 - dq, zs, ps]
            )
        elif dp:
            target, slot, sem = (
                at.index(0, dp, 0), from_p.at[side - 1 - dp, zs], p_recv.at[side - 1 - dp, zs]
            )
        elif dz:
            target, slot, sem = at.index(dz, 0, 0), from_z.at[deep - 1 - dz], z_recv.at[deep - 1 - dz]
        else:
            for s in range(deep - 1):
                landed(from_z.at[s], z_recv.at[s])
                value += from_z[s].astype(f32)
            total[...] = value
            continue
        sums[block] = value.astype(jnp.bfloat16)
        copy = pltpu.make_async_remote_copy(
            sums.at[block], slot, send.at[number], sem,
            device_id=(target, core), device_id_type=MESH,
        )
        copy.start()
        waits.append(copy)
    for keep in keeps:
        keep.wait()
    for copy in waits:
        copy.wait_send()
    for step in range(wide):
        peer = (at.me + step) % wide
        if step:
            landed(messages.at[peer, core], note_recv.at[peer, core])
        landed(messages.at[peer, other], note_recv.at[peer, other])
    spare = pl.ds(pl.multiple_of(other * span, LANES), span)
    landed(block_half.at[:, spare], swap_recv.at[0])
    landed(token_half.at[:, spare], swap_recv.at[1])


def scatter_all(wide, parts, message, block_out, token_out):
    rows, columns = parts.shape[2:]
    features, count = block_out.shape
    deep, side = plane(wide)
    vmem = pl.BlockSpec(memory_space=pltpu.VMEM)
    bf, f32 = jnp.bfloat16, jnp.float32
    dma = pltpu.SemaphoreType.DMA
    return pl.pallas_call(
        functools.partial(scatter_kernel, wide),
        name="scatter",
        out_shape=(
            jax.ShapeDtypeStruct((rows, columns), f32),
            jax.ShapeDtypeStruct((wide,) + message.shape, bf),
            jax.ShapeDtypeStruct((features // 2, 2 * count), f32),
            jax.ShapeDtypeStruct((features // 2, 2 * count), f32),
        ),
        in_specs=[vmem] * 4,
        out_specs=(vmem,) * 4,
        scratch_shapes=[
            pltpu.VMEM((wide, rows, columns), bf),
            pltpu.VMEM((max(side - 1, 1), deep, side, rows, columns), bf),
            pltpu.VMEM((max(side - 1, 1), deep, rows, columns), bf),
            pltpu.VMEM((max(deep - 1, 1), rows, columns), bf),
            pltpu.VMEM((wide, rows, columns), bf),
            dma((wide,)),
            dma((wide,)),
            dma((wide,)),
            dma((max(side - 1, 1), deep, side)),
            dma((max(side - 1, 1), deep)),
            dma((max(deep - 1, 1),)),
            dma((wide, 2)),
            dma((wide, 2)),
            dma((2,)),
            dma((2,)),
            dma((3,)),
        ],
        compiler_params=pltpu.CompilerParams(
            collective_id=1, has_side_effects=True, vmem_limit_bytes=VMEM_LIMIT
        ),
    )(parts, message, block_out, token_out)


def norm_forward(values):
    average = jnp.mean(values, axis=-1, keepdims=True)
    centred = values - average
    inv_std = lax.rsqrt(jnp.mean(centred * centred, axis=-1, keepdims=True) + EPS)
    return centred * inv_std, inv_std


def norm_backward(grad_norm, normed, inv_std):
    first = jnp.mean(grad_norm, axis=-1, keepdims=True)
    second = jnp.mean(grad_norm * normed, axis=-1, keepdims=True)
    return inv_std * (grad_norm - first - normed * second)


def block_kernel(
    own, sequence, width, hidden,
    tokens, upstream, full, modulation, bias_in, bias_out, bias_up, bias_down,
    block_out, token_out, parts, grad_mod, sum_heads, sum_out, sum_up, sum_down,
    hid, upg, normed, inv, mod_bf, normed_two, inv_two, mod_two, gff, attention, feed, gmod,
    qkv, att_heads, att, weights, gatt_heads, gatt, gproj_heads, gproj,
):
    bf, f32 = jnp.bfloat16, jnp.float32
    features = 2 * width
    heads = features // HD
    per_half = heads // 2
    count = own * sequence
    score_scale = HD ** (-0.5)
    rows = LANES if sequence % LANES == 0 else sequence
    blocks = count // rows
    chunk = 256 if hidden % 256 == 0 else hidden
    chunks = hidden // chunk
    in_at, out_at = 2 * hidden, 2 * hidden + 3 * width

    def dot(a, b, left, right):
        return lax.dot_general(a, b, (((left,), (right,)), ((), ())), preferred_element_type=f32)

    def total(value):
        return jnp.sum(value, axis=0, keepdims=True)

    grad_mod[...] = jnp.zeros_like(grad_mod)
    sum_heads[...] = jnp.zeros_like(sum_heads)
    sum_out[...] = jnp.zeros_like(sum_out)
    sum_down[...] = jnp.zeros_like(sum_down)
    feed[...] = jnp.zeros_like(feed)
    gmod[...] = jnp.zeros_like(gmod)

    def span(r):
        return pl.ds(pl.multiple_of(r * rows, rows), rows), (r * rows) // sequence

    @pl.loop(0, blocks)
    def _(r):
        at, b = span(r)
        values = jnp.transpose(tokens[:, at])
        hid[at, :] = values
        unit, scale = norm_forward(values)
        normed[at, :] = unit
        inv[at, :] = scale
        mod_bf[at, :] = (unit * (1.0 + modulation[b, 1:2, :]) + modulation[b, 0:1, :]).astype(bf)
        up = jnp.transpose(upstream[:, at])
        upg[at, :] = up
        grad = modulation[b, 5:6, :] * up
        gff[at, :] = grad.astype(bf)
        sum_down[...] += total(grad)

    @pl.loop(0, blocks)
    def _(r):
        at, b = span(r)
        for n in range(2):
            out = dot(mod_bf[at, :], full[n, :, in_at:out_at], 1, 0)
            for j in range(3):
                for h in range(per_half):
                    low = j * width + h * HD
                    piece = out[:, low : low + HD]
                    if j != 1:
                        piece = piece + bias_in[j // 2, n * per_half + h]
                    qkv[j, n * per_half + h, at, :] = piece.astype(bf)

    @pl.loop(0, own * heads)
    def _(i):
        b, h = i // heads, i % heads
        at = pl.ds(pl.multiple_of(b * sequence, sequence), sequence)
        scores = dot(qkv[0, h, at, :], qkv[1, h, at, :], 1, 1) * score_scale
        log_total = jnp.log(jnp.sum(jnp.exp(scores), axis=-1, keepdims=True))
        mix = jnp.exp(scores - log_total)
        weights[i] = mix
        att_heads[h, at, :] = dot(mix.astype(bf), qkv[2, h, at, :], 1, 0).astype(bf)

    for n in range(2):
        att[n] = jnp.concatenate([att_heads[n * per_half + h] for h in range(per_half)], axis=1)

    @pl.loop(0, blocks)
    def _(r):
        at, b = span(r)
        result = bias_out[...] + sum(
            dot(att[n, at, :], full[n, :, out_at : out_at + width], 1, 1) for n in range(2)
        )
        attention[at, :] = result
        middle = hid[at, :] + modulation[b, 2:3, :] * result
        hid[at, :] = middle
        unit, scale = norm_forward(middle)
        normed_two[at, :] = unit
        inv_two[at, :] = scale
        mod_two[at, :] = (unit * (1.0 + modulation[b, 4:5, :]) + modulation[b, 3:4, :]).astype(bf)

    @pl.loop(0, 2 * chunks)
    def _(i):
        n, c = i // chunks, i % chunks
        at = pl.ds(pl.multiple_of(c * chunk, chunk), chunk)
        down_at = pl.ds(pl.multiple_of(hidden + c * chunk, chunk), chunk)
        up_w, down_w = full[n, :, at], full[n, :, down_at]
        pre = dot(mod_two[...], up_w, 1, 0) + bias_up[n, :, at]
        tangent = jnp.tanh(GELU_K * (pre + GELU_A * pre * pre * pre))
        act = (0.5 * pre * (1.0 + tangent)).astype(bf)
        slope = 0.5 * (1.0 + tangent) + 0.5 * pre * (1.0 - tangent * tangent) * GELU_K * (
            1.0 + 3.0 * GELU_A * pre * pre
        )
        feed[...] += dot(act, down_w, 1, 1)
        parts[n, :, down_at] = dot(gff[...], act, 0, 0).astype(bf)
        grad = dot(gff[...], down_w, 1, 0) * slope
        sum_up[n, :, at] = total(grad)
        grad_bf = grad.astype(bf)
        parts[n, :, at] = dot(mod_two[...], grad_bf, 0, 0).astype(bf)
        gmod[...] += dot(grad_bf, up_w, 1, 1)

    @pl.loop(0, blocks)
    def _(r):
        at, b = span(r)
        ff = feed[at, :] + bias_down[...]
        up = upg[at, :]
        block_out[:, at] = jnp.transpose(hid[at, :] + modulation[b, 5:6, :] * ff)
        grad_mod[b, 5:6, :] += total(up * ff)
        grad, unit = gmod[at, :], normed_two[at, :]
        grad_mod[b, 3:4, :] += total(grad)
        grad_mod[b, 4:5, :] += total(grad * unit)
        middle = up + norm_backward(grad * (1.0 + modulation[b, 4:5, :]), unit, inv_two[at, :])
        upg[at, :] = middle
        grad_mod[b, 2:3, :] += total(middle * attention[at, :])
        grad_att = modulation[b, 2:3, :] * middle
        sum_out[...] += total(grad_att)
        grad_bf = grad_att.astype(bf)
        gatt[at, :] = grad_bf
        for n in range(2):
            out = dot(grad_bf, full[n, :, out_at : out_at + width], 1, 0).astype(bf)
            for h in range(per_half):
                gatt_heads[n * per_half + h, at, :] = out[:, h * HD : (h + 1) * HD]

    @pl.loop(0, own * heads)
    def _(i):
        b, h = i // heads, i % heads
        at = pl.ds(pl.multiple_of(b * sequence, sequence), sequence)
        mix, grad_out = weights[i], gatt_heads[h, at, :]
        grad_mix = dot(grad_out, qkv[2, h, at, :], 1, 1)
        dots = jnp.sum(mix * grad_mix, axis=-1, keepdims=True)
        grad_scores = (mix * (grad_mix - dots) * score_scale).astype(bf)
        grad_q = dot(grad_scores, qkv[1, h, at, :], 1, 0)
        grad_k = dot(grad_scores, qkv[0, h, at, :], 0, 0)
        grad_v = dot(mix.astype(bf), grad_out, 0, 0)
        gproj_heads[0, h, at, :] = grad_q.astype(bf)
        gproj_heads[1, h, at, :] = grad_k.astype(bf)
        gproj_heads[2, h, at, :] = grad_v.astype(bf)
        sum_heads[0, h] += total(grad_q)
        sum_heads[1, h] += total(grad_v)

    for n in range(2):
        gproj[n] = jnp.concatenate(
            [gproj_heads[j, n * per_half + h] for j in range(3) for h in range(per_half)], axis=1
        )
        parts[n, :, in_at:] = jnp.concatenate(
            [dot(mod_bf[...], gproj[n], 0, 0), dot(gatt[...], att[n], 0, 0)], axis=1
        ).astype(bf)

    @pl.loop(0, blocks)
    def _(r):
        at, b = span(r)
        grad = sum(dot(gproj[n, at, :], full[n, :, in_at:out_at], 1, 1) for n in range(2))
        unit = normed[at, :]
        grad_mod[b, 0:1, :] += total(grad)
        grad_mod[b, 1:2, :] += total(grad * unit)
        back = norm_backward(grad * (1.0 + modulation[b, 1:2, :]), unit, inv[at, :])
        token_out[:, at] = jnp.transpose(upg[at, :] + back)


def block_pass(
    tokens, upstream, full, modulation, bias_in, bias_out, bias_up, bias_down, own, sequence, width, hidden
):
    bf, f32 = jnp.bfloat16, jnp.float32
    features = 2 * width
    heads = features // HD
    count = own * sequence
    bias_in = jnp.transpose(bias_in.reshape(2, 2, width), (1, 0, 2)).reshape(2, heads, 1, HD)
    vmem = pl.BlockSpec(memory_space=pltpu.VMEM)
    sds = jax.ShapeDtypeStruct
    wide_f32, wide_bf = pltpu.VMEM((count, features), f32), pltpu.VMEM((count, features), bf)
    column = pltpu.VMEM((count, 1), f32)
    by_head = pltpu.VMEM((heads, count, HD), bf)
    by_head_three = pltpu.VMEM((3, heads, count, HD), bf)
    block_out, token_out, parts, grad_mod, sum_heads, sum_out, sum_up, sum_down = pl.pallas_call(
        functools.partial(block_kernel, own, sequence, width, hidden),
        name="block",
        out_shape=(
            sds((features, count), f32),
            sds((features, count), f32),
            sds((2, features, 2 * hidden + 4 * width), bf),
            sds((own, 6, features), f32),
            sds((2, heads, 1, HD), f32),
            sds((1, features), f32),
            sds((2, 1, hidden), f32),
            sds((1, features), f32),
        ),
        in_specs=[vmem] * 8,
        out_specs=(vmem,) * 8,
        scratch_shapes=[
            wide_f32, wide_f32, wide_f32, column, wide_bf, wide_f32, column, wide_bf, wide_bf, wide_f32,
            wide_f32, wide_f32,
            by_head_three, by_head, pltpu.VMEM((2, count, width), bf),
            pltpu.VMEM((own * heads, sequence, sequence), f32),
            by_head, wide_bf, by_head_three, pltpu.VMEM((2, count, 3 * width), bf),
        ],
        compiler_params=pltpu.CompilerParams(vmem_limit_bytes=VMEM_LIMIT),
    )(
        tokens, upstream, full, modulation, bias_in, bias_out.reshape(1, -1),
        bias_up.reshape(2, 1, hidden), bias_down.reshape(1, -1),
    )
    by_half = lambda value: value.reshape(2, -1)
    bias_sums = jnp.concatenate(
        [
            by_half(sum_heads[0]), by_half(sum_heads[1]), by_half(sum_out), by_half(sum_up), by_half(sum_down),
        ],
        axis=1,
    )
    return block_out, token_out, parts, grad_mod, bias_sums


def codes(values):
    return jnp.concatenate([values // 256, values % 256]).astype(jnp.bfloat16)


def shards(
    latent_tokens,
    labels,
    timesteps,
    class_table,
    modulation_weight,
    modulation_bias,
    in_weight,
    in_bias,
    out_weight,
    out_bias,
    up_weight,
    up_bias,
    down_weight,
    down_bias,
    cotangent,
):
    bf, f32 = jnp.bfloat16, jnp.float32
    wide = lax.axis_size("wide")
    me, core = lax.axis_index("wide"), lax.axis_index("narrow")
    latent_count = labels.shape[0]
    own = latent_count // 2
    width = latent_tokens.shape[0]
    hidden = up_weight.shape[1]
    local_tokens = latent_tokens.shape[1]
    sequence = local_tokens // latent_count
    weight_scale = (local_tokens * wide) ** (-0.5)
    rows = up_weight.shape[0]

    ids = jnp.concatenate([codes(labels), codes(timesteps)])
    ids = jnp.pad(ids[None, :], ((0, rows - 1), (0, LANES - ids.shape[0])))
    shard = jnp.concatenate(
        [
            up_weight,
            jnp.transpose(down_weight),
            in_weight.reshape(rows, 3 * width),
            jnp.transpose(out_weight),
            modulation_weight.reshape(rows, 6 * width),
            ids,
        ],
        axis=1,
    )
    bias_parts = [in_bias.reshape(-1), out_bias, up_bias, down_bias, modulation_bias.reshape(-1)]
    biases = jnp.concatenate(bias_parts)
    pad = -biases.shape[0] % (8 * LANES)
    biases = jnp.pad(biases, (0, pad)).reshape(-1, LANES)
    full, tokens, upstream, both = gather_all(wide, shard, latent_tokens, cotangent, biases)
    ids_all = full[0, :, 0, -LANES:].astype(jnp.int32)
    pick = lambda n: ids_all[:, n * latent_count : (n + 1) * latent_count].reshape(-1)
    labels_all = pick(0) * 256 + pick(1)
    times_all = pick(2) * 256 + pick(3)
    class_ids = jnp.arange(class_table.shape[0], dtype=jnp.int32)
    every_hot = (labels_all[:, None] == class_ids[None, :]).astype(bf)
    condition_all = jnp.dot(every_hot, class_table, preferred_element_type=f32) + time_features(
        times_all
    )
    activated_all = jax.nn.silu(condition_all).astype(bf)
    first = me * latent_count + core * own
    condition = lax.dynamic_slice_in_dim(condition_all, first, own, 0)
    activated = lax.dynamic_slice_in_dim(activated_all, first, own, 0)

    full = full.reshape(2, rows * wide, -1)
    flat = both.reshape(2, -1)
    offset = 0
    halves = []
    for part in bias_parts:
        halves.append(flat[:, offset : offset + part.shape[0]])
        offset += part.shape[0]
    bias_in, bias_out, bias_up, bias_down, bias_mod = halves
    mod_at = 2 * hidden + 4 * width
    mod_full = full[:, :, mod_at : mod_at + 6 * width]
    modulation = jnp.einsum("bd,ndf->nbf", activated, mod_full, preferred_element_type=f32) + bias_mod[:, None]
    modulation = jnp.transpose(modulation.reshape(2, own, 6, width), (1, 2, 0, 3)).reshape(own, 6, 2 * width)

    block_output, token_grads, parts, grad_modulation, bias_sums = block_pass(
        tokens.reshape(2 * width, -1), upstream.reshape(2 * width, -1), full, modulation,
        bias_in, bias_out, bias_up, bias_down, own, sequence, width, hidden,
    )

    grad_modulation_bf = grad_modulation.astype(bf)
    by_half = jnp.transpose(grad_modulation_bf.reshape(own, 6, 2, width), (2, 0, 1, 3)).reshape(2, own, 6 * width)
    grad_activated = jnp.einsum("nbf,ndf->bd", by_half, mod_full, preferred_element_type=f32)
    condition_rows = (grad_activated * silu_slope(condition) * sequence ** (-0.5)).astype(bf)
    message = jnp.concatenate(
        [
            by_half.reshape(2, -1),
            jnp.broadcast_to(condition_rows.reshape(1, -1), (2, own * 2 * width)),
            bias_sums.astype(bf),
        ],
        axis=1,
    )
    used = message.shape[1]
    message = jnp.pad(message, ((0, 0), (0, -used % (16 * LANES)))).reshape(2, -1, LANES)
    total, messages, block_half, token_half = scatter_all(
        wide, parts.reshape(2, wide, rows, -1), message, block_output, token_grads
    )
    flat_notes = messages.reshape(wide * 2, -1)
    gm_all = flat_notes[:, : own * 6 * width].reshape(wide * latent_count, 6 * width)
    cond_all = flat_notes[:, own * 6 * width : own * 8 * width].reshape(wide * latent_count, 2 * width)
    sums = jnp.sum(flat_notes[:, own * 8 * width : used].astype(f32), axis=0) * weight_scale
    act_mine = lax.dynamic_slice_in_dim(activated_all, me * rows, rows, 1)
    mod_grads = jnp.einsum("bd,bf->df", act_mine, gm_all, preferred_element_type=f32) * weight_scale
    mod_bias_grads = jnp.sum(gm_all.astype(f32), axis=0) * weight_scale
    table_grads = jnp.einsum("bc,bd->cd", every_hot, cond_all, preferred_element_type=f32)
    condition_grads = lax.dynamic_slice_in_dim(cond_all, me * latent_count, latent_count, 0).astype(f32)
    total = total * weight_scale
    up_part = total[:, :hidden]
    down_part = jnp.transpose(total[:, hidden : 2 * hidden])
    in_part = total[:, 2 * hidden : 2 * hidden + 3 * width].reshape(rows, 3, width)
    out_part = jnp.transpose(total[:, 2 * hidden + 3 * width :])
    return (
        block_half,
        token_half,
        condition_grads,
        table_grads,
        mod_grads.reshape(rows, 6, width),
        mod_bias_grads.reshape(6, width),
        in_part,
        sums[: 2 * width].reshape(2, width),
        out_part,
        sums[2 * width : 3 * width],
        up_part,
        sums[3 * width : 3 * width + hidden],
        down_part,
        sums[3 * width + hidden :],
    )


ROLE_ROWS = 16
EARLY_ROWS, LATE_ROWS = 64, 32


class Spot:
    def __init__(self, wide):
        self.deep, self.side = plane(wide)
        self.me = lax.axis_index("wide")
        self.core = lax.axis_index("narrow")
        self.other = 1 - self.core
        self.z = self.me // 4
        rest = self.me % 4
        major, minor = rest // 2, rest % 2
        self.p = major + self.core * (minor - major)
        self.q = minor + self.core * (major - minor)
        self.xy = rest
        self.waits = []

    def line(self, dp, dq):
        p, q = (self.p + dp) % 2, (self.q + dq) % 2
        return p * (2 - self.core) + q * (1 + self.core)

    def depth(self, dz):
        return (self.z + dz) % self.deep

    def device(self, dz, dp, dq):
        return self.depth(dz) * 4 + self.line(dp, dq)

    def push(self, src, dst, send, recv, target, seat):
        copy = pltpu.make_async_remote_copy(
            src, dst, send, recv, device_id=(target, seat), device_id_type=MESH
        )
        copy.start()
        self.waits.append(copy)

    def p_peer(self):
        return self.device(0, 1, 0)

    def q_peer(self):
        return self.device(0, 0, 1)

    def enter(self):
        barrier = pltpu.get_barrier_semaphore()
        peers = [self.device(dz, 0, 0) for dz in range(1, self.deep)] + [self.p_peer(), self.q_peer()]
        for peer in peers:
            pl.semaphore_signal(barrier, 1, device_id=(peer, self.core), device_id_type=MESH)
        pl.semaphore_signal(barrier, 1, device_id=(self.me, self.other), device_id_type=MESH)
        pl.semaphore_wait(barrier, len(peers) + 1)


def landed(ref, sem):
    pltpu.make_async_copy(ref, ref, sem).wait()


class Gather:
    def __init__(self, spot, buf, send, recv, number):
        self.spot, self.buf = spot, buf
        self.send = lambda n: send.at[number, n]
        self.recv = lambda n: recv.at[number, n]
        self.base = spot.deep - 1

    def mine(self):
        s = self.spot
        return self.buf.at[s.core, s.xy, s.z]

    def share(self, line, send, recv, target, seat):
        ref = self.buf.at[self.spot.core, line]
        self.spot.push(ref, ref, self.send(send), self.recv(recv), target, seat)

    def one(self):
        s = self.spot
        for dz in range(1, s.deep):
            s.push(self.mine(), self.mine(), self.send(dz - 1), self.recv(dz - 1), s.device(dz, 0, 0), s.core)

    def two(self):
        s, base = self.spot, self.base
        for dz in range(1, s.deep):
            landed(self.buf.at[s.core, s.xy, s.depth(-dz)], self.recv(dz - 1))
        line = s.line(0, 0)
        self.share(line, base, base, s.p_peer(), s.core)
        self.share(line, base + 1, base + 1, s.q_peer(), s.core)
        self.share(line, base + 2, base + 3, s.me, s.other)

    def three(self):
        s, base = self.spot, self.base
        line = s.line(1, 0)
        landed(self.buf.at[s.core, line], self.recv(base))
        self.share(line, base + 3, base + 2, s.q_peer(), s.core)
        self.share(line, base + 4, base + 4, s.me, s.other)

    def four(self):
        s, base = self.spot, self.base
        for dp in range(2):
            line = s.line(dp, 1)
            landed(self.buf.at[s.core, line], self.recv(base + 1 + dp))
            self.share(line, base + 5 + dp, base + 5 + dp, s.me, s.other)

    def five(self):
        s, base = self.spot, self.base
        for slot, (dp, dq) in enumerate([(0, 0), (0, 1), (1, 0), (1, 1)]):
            landed(self.buf.at[s.other, s.line(dp, dq)], self.recv(base + 3 + slot))


class Scatter:
    def __init__(self, spot, parts, bufs, send, recv, number):
        self.spot, self.parts = spot, parts
        self.from_pair, self.to_q, self.from_q, self.to_p, self.from_p, self.to_z, self.from_z, self.total = bufs
        self.send = lambda n: send.at[number, n]
        self.recv = lambda n: recv.at[number, n]

    def pair(self, line):
        f32 = jnp.float32
        return self.parts[self.spot.core, line].astype(f32) + self.from_pair[line].astype(f32)

    def one(self):
        s = self.spot
        s.push(self.parts.at[s.other], self.from_pair, self.send(0), self.recv(0), s.me, s.other)

    def two(self):
        s = self.spot
        landed(self.from_pair, self.recv(0))
        for dp in (1, 0):
            self.to_q[dp] = self.pair(s.line(dp, 1)).astype(jnp.bfloat16)
            s.push(self.to_q.at[dp], self.from_q.at[dp], self.send(1 + dp), self.recv(1 + dp), s.q_peer(), s.core)

    def three(self):
        s = self.spot
        landed(self.from_q.at[1], self.recv(2))
        value = self.pair(s.line(1, 0)) + self.from_q[1].astype(jnp.float32)
        self.to_p[...] = value.astype(jnp.bfloat16)
        s.push(self.to_p, self.from_p, self.send(3), self.recv(3), s.p_peer(), s.core)

    def four(self):
        s, f32 = self.spot, jnp.float32
        landed(self.from_q.at[0], self.recv(1))
        landed(self.from_p, self.recv(3))
        for dz in list(range(1, s.deep)) + [0]:
            z = s.depth(dz)
            value = self.parts[s.core, s.xy, z].astype(f32) + self.from_pair[s.xy, z].astype(f32)
            value = value + self.from_q[0, z].astype(f32) + self.from_p[z].astype(f32)
            if dz:
                self.to_z[dz - 1] = value.astype(jnp.bfloat16)
                s.push(
                    self.to_z.at[dz - 1], self.from_z.at[dz - 1], self.send(3 + dz), self.recv(3 + dz),
                    s.device(dz, 0, 0), s.core,
                )
            else:
                self.total[...] = value

    def five(self):
        s = self.spot
        for dz in range(1, s.deep):
            landed(self.from_z.at[dz - 1], self.recv(3 + dz))
        value = self.total[...]
        for dz in range(1, s.deep):
            value = value + self.from_z[dz - 1].astype(jnp.float32)
        self.total[...] = value


def scatter_shapes(deep, rows, columns):
    bf = jnp.bfloat16
    return [
        pltpu.VMEM((2, 4, deep, rows, columns), bf),
        pltpu.VMEM((4, deep, rows, columns), bf),
        pltpu.VMEM((2, deep, rows, columns), bf),
        pltpu.VMEM((2, deep, rows, columns), bf),
        pltpu.VMEM((deep, rows, columns), bf),
        pltpu.VMEM((deep, rows, columns), bf),
        pltpu.VMEM((deep - 1, rows, columns), bf),
        pltpu.VMEM((deep - 1, rows, columns), bf),
    ]


def main_kernel(
    wide, sequence,
    tokens, upstream, labels, timesteps, class_table,
    mod_w, in_w, out_w, up_w, down_w, mod_b, in_b, out_b, up_b, down_b,
    block_half, token_half, early, late, tot_up, tot_down, tot_out, tot_in,
    tok, ups, table, bias_pack, bias_full, bias_up,
    g_one, g_two, g_up, g_down, square, w_up, w_down,
    hid, upg, normed, inv, mod_bf, normed_two, inv_two, mod_two, gff, attention, feed, gmod,
    qkv, att, weights, gatt, gattended, gproj,
    modv, gm, act, slope, sum_heads, sum_out, sum_up, sum_down, early_rows, late_rows, bout, tout,
    *rest,
):
    bf, f32 = jnp.bfloat16, jnp.float32
    up_bufs, down_bufs, out_bufs, in_bufs = [rest[8 * n : 8 * n + 8] for n in range(4)]
    g_send, g_recv, s_send, s_recv, swap_send, swap_recv, local = rest[32:]
    width, hidden = in_w.shape[2], up_w.shape[1]
    features, count = tok.shape
    shard_rows = up_w.shape[0]
    own = count // sequence
    pairs = features // LANES
    spot = Spot(wide)
    core, other, deep = spot.core, spot.other, spot.deep
    score_scale = HD ** (-0.5)
    cond_scale = sequence ** (-0.5)
    rows = LANES
    blocks = count // rows
    chunk = 256
    chunks = hidden // chunk
    thirds = features // LANES

    def dot(a, b, left, right):
        return lax.dot_general(a, b, (((left,), (right,)), ((), ())), preferred_element_type=f32)

    def total(value):
        return jnp.sum(value, axis=0, keepdims=True)

    def span(r):
        return pl.ds(pl.multiple_of(r * rows, rows), rows), (r * rows) // sequence

    mine = pl.ds(pl.multiple_of(core * count, LANES), count)
    theirs = pl.ds(pl.multiple_of(other * count, LANES), count)
    my_rows = pl.ds(pl.multiple_of(core * width, 8), width)
    their_rows = pl.ds(pl.multiple_of(other * width, 8), width)
    keeps = [
        pltpu.make_async_copy(class_table, table, local.at[0]),
        pltpu.make_async_copy(tokens.at[:, mine], tok.at[my_rows], local.at[1]),
        pltpu.make_async_copy(upstream.at[:, mine], ups.at[my_rows], local.at[2]),
    ]
    for keep in keeps:
        keep.start()

    xy, z = spot.xy, spot.z
    g_one[core, xy, z] = jnp.concatenate(
        [in_w[j].astype(f32) for j in range(3)]
        + [mod_w[j].astype(f32) for j in range(2)]
        + [out_w[...].astype(f32)],
        axis=1,
    ).astype(bf)
    g_two[core, xy, z] = jnp.concatenate([mod_w[j].astype(f32) for j in range(2, 6)], axis=1).astype(bf)
    g_up[core, xy, z] = up_w[...]
    g_down[core, xy, z] = down_w[...]
    bias_pack[core] = jnp.zeros(bias_pack.shape[1:], f32)
    bias_pack[core, 0:1, :] = up_b[...]
    bias_pack[core, 1:2, :width] = out_b[...]
    bias_pack[core, 2:3, :width] = down_b[...]
    bias_pack[core, 3:5, :width] = in_b[...]
    bias_pack[core, 5:11, :width] = mod_b[...]

    gather = [
        Gather(spot, buf, g_send, g_recv, n)
        for n, buf in enumerate([g_one, g_two, g_up, g_down, early, late])
    ]
    scatter = [
        Scatter(spot, bufs[0], tuple(bufs[1:]) + (out,), s_send, s_recv, n)
        for n, (bufs, out) in enumerate(
            [(up_bufs, tot_up), (down_bufs, tot_down), (out_bufs, tot_out), (in_bufs, tot_in)]
        )
    ]
    one, two, up_g, down_g, early_g, late_g = gather
    up_s, down_s, out_s, in_s = scatter

    spot.enter()
    one.one()
    spot.push(bias_pack.at[core], bias_pack.at[core], swap_send.at[0], swap_recv.at[0], spot.me, other)
    spot.push(tokens.at[:, theirs], tok.at[my_rows], swap_send.at[1], swap_recv.at[1], spot.me, other)
    spot.push(upstream.at[:, theirs], ups.at[my_rows], swap_send.at[2], swap_recv.at[2], spot.me, other)
    two.one()

    gm[...] = jnp.zeros_like(gm)
    sum_heads[...] = jnp.zeros_like(sum_heads)
    sum_out[...] = jnp.zeros_like(sum_out)
    sum_down[...] = jnp.zeros_like(sum_down)
    feed[...] = jnp.zeros_like(feed)
    gmod[...] = jnp.zeros_like(gmod)
    early_rows[...] = jnp.zeros_like(early_rows)
    late_rows[...] = jnp.zeros_like(late_rows)

    my_labels = [labels[core * own + l] for l in range(own)]
    my_times = [timesteps[core * own + l] for l in range(own)]

    def by_row(scalars, shape):
        row = lax.broadcasted_iota(jnp.int32, shape, 0)
        value = jnp.full(shape, -1, jnp.int32)
        for l, scalar in enumerate(scalars):
            value = jnp.where(row == l, scalar, value)
        return value

    keeps[0].wait()
    classes = class_table.shape[0]
    hot = by_row(my_labels, (8, classes)) == lax.broadcasted_iota(jnp.int32, (8, classes), 1)
    half_width = features // 2
    power = lax.broadcasted_iota(jnp.int32, (8, half_width), 1).astype(f32)
    angles = by_row(my_times, (8, half_width)).astype(f32) * jnp.exp(power * (-math.log(10000.0) / half_width))
    condition = dot(hot.astype(f32).astype(bf), table[...], 1, 0) + jnp.concatenate(
        [jnp.cos(angles), jnp.sin(angles)], axis=1
    )
    sigmoid = 1.0 / (1.0 + jnp.exp(-condition))
    act[...] = condition * sigmoid
    slope[...] = sigmoid * (1.0 + condition * (1.0 - sigmoid)) * cond_scale

    keeps[1].wait()
    keeps[2].wait()
    landed(tok.at[their_rows], swap_recv.at[1])
    landed(ups.at[their_rows], swap_recv.at[2])

    @pl.loop(0, blocks)
    def _(r):
        at, _ = span(r)
        values = jnp.transpose(tok[:, at])
        hid[at, :] = values
        unit, scale = norm_forward(values)
        normed[at, :] = unit
        inv[at, :] = scale
        upg[at, :] = jnp.transpose(ups[:, at])

    landed(bias_pack.at[other], swap_recv.at[0])
    bias_full[...] = jnp.concatenate([bias_pack[n, :, :width] for n in range(2)], axis=1)
    bias_up[...] = jnp.concatenate([bias_pack[n, 0:1, :] for n in range(2)], axis=1)

    one.two()
    up_g.one()
    down_g.one()
    one.three()
    two.two()
    one.four()
    two.three()
    up_g.two()
    one.five()

    def regroup(buf, places):
        @pl.loop(0, 2 * deep)
        def _(k):
            depth, pair = k // 2, k % 2
            at = pl.ds(pl.multiple_of(k * 2 * shard_rows, 16), 2 * shard_rows)
            halves = [
                jnp.concatenate([buf[n, 2 * pair + m, depth].astype(f32) for m in range(2)], axis=0)
                for n in range(2)
            ]
            for write, low, size in places:
                write(at, jnp.concatenate([half[:, low : low + size] for half in halves], axis=1).astype(bf))

    def to_square(j):
        def write(at, value):
            square[j, at, :] = value
        return write

    def to_hidden(ref):
        def write(at, value):
            ref[at, :] = value
        return write

    regroup(
        g_one,
        [(to_square(6 + j), j * width, width) for j in range(3)]
        + [(to_square(j), (3 + j) * width, width) for j in range(2)]
        + [(to_square(9), 5 * width, width)],
    )

    act_bf = act[...].astype(bf)

    def modulate(j):
        value = dot(act_bf, square[j], 1, 0) + bias_full[5 + j : 6 + j, :]
        for l in range(own):
            modv[l, j : j + 1, :] = value[l : l + 1, :]

    modulate(0)
    modulate(1)

    @pl.loop(0, blocks)
    def _(r):
        at, b = span(r)
        value = (normed[at, :] * (1.0 + modv[b, 1:2, :]) + modv[b, 0:1, :]).astype(bf)
        mod_bf[at, :] = value
        qkv[0, at, :] = (dot(value, square[6], 1, 0) + bias_full[3:4, :]).astype(bf)
        qkv[1, at, :] = dot(value, square[7], 1, 0).astype(bf)
        qkv[2, at, :] = (dot(value, square[8], 1, 0) + bias_full[4:5, :]).astype(bf)

    two.four()
    up_g.three()
    down_g.two()

    lane = lax.broadcasted_iota(jnp.int32, (1, LANES), 1)
    masks = [(lane // HD == h).astype(f32).astype(bf) for h in range(LANES // HD)]

    def split(value):
        return jnp.concatenate([value * mask for mask in masks], axis=0)

    def side_by_side(value):
        return jnp.concatenate([value[h * sequence : (h + 1) * sequence] for h in range(len(masks))], axis=1)

    def attend(b):
        at = pl.ds(b * sequence, sequence)

        @pl.loop(0, pairs)
        def _(g):
            col = pl.ds(pl.multiple_of(g * LANES, LANES), LANES)
            scores = dot(split(qkv[0, at, col]), qkv[1, at, col], 1, 1) * score_scale
            log_total = jnp.log(jnp.sum(jnp.exp(scores), axis=-1, keepdims=True))
            mix = jnp.exp(scores - log_total)
            weights[b * pairs + g] = mix
            att[at, col] = dot(side_by_side(mix.astype(bf)), split(qkv[2, at, col]), 1, 0).astype(bf)

    attend(0)
    two.five()
    up_g.four()
    down_g.three()
    regroup(g_two, [(to_square(2 + j), j * width, width) for j in range(4)])
    for j in range(2, 6):
        modulate(j)
    for b in range(1, own):
        attend(b)
    up_g.five()
    down_g.four()
    regroup(g_up, [(to_hidden(w_up), 0, hidden)])

    @pl.loop(0, blocks)
    def _(r):
        at, b = span(r)
        result = bias_full[1:2, :] + dot(att[at, :], square[9], 1, 1)
        attention[at, :] = result
        middle = hid[at, :] + modv[b, 2:3, :] * result
        hid[at, :] = middle
        unit, scale = norm_forward(middle)
        normed_two[at, :] = unit
        inv_two[at, :] = scale
        mod_two[at, :] = (unit * (1.0 + modv[b, 4:5, :]) + modv[b, 3:4, :]).astype(bf)
        grad = modv[b, 5:6, :] * upg[at, :]
        gff[at, :] = grad.astype(bf)
        sum_down[...] += total(grad)

    down_g.five()
    regroup(g_down, [(to_hidden(w_down), 0, hidden)])

    up_parts, down_parts, out_parts, in_parts = up_bufs[0], down_bufs[0], out_bufs[0], in_bufs[0]

    def put(parts, n, columns, value):
        for w in range(wide):
            piece = value[w * shard_rows : (w + 1) * shard_rows].astype(bf)
            parts[n, w % 4, w // 4, :, columns] = piece

    def forward_and_back(n):
        @pl.loop(0, chunks)
        def _(c):
            at = pl.ds(pl.multiple_of(n * hidden + c * chunk, chunk), chunk)
            columns = pl.ds(pl.multiple_of(c * chunk, chunk), chunk)
            up_at, down_at = w_up[:, at], w_down[:, at]
            pre = dot(mod_two[...], up_at, 1, 0) + bias_up[:, at]
            tangent = jnp.tanh(GELU_K * (pre + GELU_A * pre * pre * pre))
            value = (0.5 * pre * (1.0 + tangent)).astype(bf)
            steep = 0.5 * (1.0 + tangent) + 0.5 * pre * (1.0 - tangent * tangent) * GELU_K * (
                1.0 + 3.0 * GELU_A * pre * pre
            )
            feed[...] += dot(value, down_at, 1, 1)
            put(down_parts, n, columns, dot(gff[...], value, 0, 0))
            grad = dot(gff[...], down_at, 1, 0) * steep
            sum_up[:, at] = total(grad)
            grad_bf = grad.astype(bf)
            put(up_parts, n, columns, dot(mod_two[...], grad_bf, 0, 0))
            gmod[...] += dot(grad_bf, up_at, 1, 1)

    forward_and_back(other)
    down_s.one()
    up_s.one()
    forward_and_back(core)
    down_s.two()
    up_s.two()

    @pl.loop(0, blocks)
    def _(r):
        at, b = span(r)
        ff = feed[at, :] + bias_full[2:3, :]
        up = upg[at, :]
        bout[:, at] = jnp.transpose(hid[at, :] + modv[b, 5:6, :] * ff)
        gm[b, 5:6, :] += total(up * ff)
        grad, unit = gmod[at, :], normed_two[at, :]
        gm[b, 3:4, :] += total(grad)
        gm[b, 4:5, :] += total(grad * unit)
        middle = up + norm_backward(grad * (1.0 + modv[b, 4:5, :]), unit, inv_two[at, :])
        upg[at, :] = middle
        gm[b, 2:3, :] += total(middle * attention[at, :])
        grad_att = modv[b, 2:3, :] * middle
        sum_out[...] += total(grad_att)
        grad_bf = grad_att.astype(bf)
        gatt[at, :] = grad_bf
        gattended[at, :] = dot(grad_bf, square[9], 1, 0).astype(bf)

    def swap_out(src, dst, which):
        spot.push(src.at[their_rows], dst.at[:, mine], swap_send.at[which], swap_recv.at[which], spot.me, other)
        keep = pltpu.make_async_copy(src.at[my_rows], dst.at[:, mine], local.at[which])
        keep.start()
        keeps.append(keep)

    swap_out(bout, block_half, 3)

    def row_pieces(ref, low, value):
        for k in range(value.shape[1] // LANES):
            ref[low + k : low + k + 1, :] = value[:, k * LANES : (k + 1) * LANES]

    for l in range(own):
        for j in range(4):
            row_pieces(early_rows, (l * 4 + j) * thirds, gm[l, 2 + j : 3 + j, :])
        row_pieces(early_rows, (own * 4 + l) * thirds, act[l : l + 1, :])
        code = jnp.full((1, LANES), my_labels[l], jnp.int32)
        low = own * 5 * thirds
        early_rows[low + l : low + l + 1, :] = (code // 256).astype(f32)
        early_rows[low + own + l : low + own + l + 1, :] = (code % 256).astype(f32)
    low = own * 5 * thirds + 2 * own
    row_pieces(early_rows, low, sum_out[...])
    row_pieces(early_rows, low + thirds, sum_down[...])
    row_pieces(early_rows, low + 2 * thirds, sum_up[...])
    early[core, xy, z] = early_rows[...].astype(bf)
    early_g.one()

    value = dot(gatt[...], att[...], 0, 0)
    for n in range(2):
        put(out_parts, n, slice(None), value[:, n * width : (n + 1) * width])
    out_s.one()
    down_s.three()
    up_s.three()
    early_g.two()

    gact = jnp.zeros((8, features), f32)

    def stack_gm(j):
        return jnp.concatenate([gm[l, j : j + 1, :] for l in range(own)] * (8 // own), axis=0).astype(bf)

    def attend_back(b):
        at = pl.ds(b * sequence, sequence)

        @pl.loop(0, pairs)
        def _(g):
            col = pl.ds(pl.multiple_of(g * LANES, LANES), LANES)
            mix = weights[b * pairs + g]
            grad_out = split(gattended[at, col])
            grad_mix = dot(grad_out, qkv[2, at, col], 1, 1)
            dots = jnp.sum(mix * grad_mix, axis=-1, keepdims=True)
            grad_scores = (mix * (grad_mix - dots) * score_scale).astype(bf)
            grad_q = dot(side_by_side(grad_scores), split(qkv[1, at, col]), 1, 0)
            grad_k = dot(grad_scores, split(qkv[0, at, col]), 0, 0)
            grad_v = dot(mix.astype(bf), grad_out, 0, 0)
            gproj[0, at, col] = grad_q.astype(bf)
            gproj[1, at, col] = grad_k.astype(bf)
            gproj[2, at, col] = grad_v.astype(bf)
            sum_heads[0, :, col] += total(grad_q)
            sum_heads[1, :, col] += total(grad_v)

    attend_back(0)
    down_s.four()
    up_s.four()
    early_g.three()
    out_s.two()
    for b in range(1, own):
        attend_back(b)
    early_g.four()
    out_s.three()

    pieces = [dot(mod_bf[...], gproj[j], 0, 0) for j in range(3)]
    for n in range(2):
        value = jnp.concatenate([piece[:, n * width : (n + 1) * width] for piece in pieces], axis=1)
        put(in_parts, n, slice(None), value)
    in_s.one()
    down_s.five()
    up_s.five()
    for j in range(2, 6):
        gact += dot(stack_gm(j), square[j], 1, 1)

    @pl.loop(0, blocks)
    def _(r):
        at, b = span(r)
        grad = sum(dot(gproj[j, at, :], square[6 + j], 1, 1) for j in range(3))
        unit = normed[at, :]
        gm[b, 0:1, :] += total(grad)
        gm[b, 1:2, :] += total(grad * unit)
        back = norm_backward(grad * (1.0 + modv[b, 1:2, :]), unit, inv[at, :])
        tout[:, at] = jnp.transpose(upg[at, :] + back)

    swap_out(tout, token_half, 4)
    in_s.two()
    out_s.four()
    for j in range(2):
        gact += dot(stack_gm(j), square[j], 1, 1)
    grad_condition = gact * slope[...]
    for l in range(own):
        for j in range(2):
            row_pieces(late_rows, (l * 2 + j) * thirds, gm[l, j : j + 1, :])
        row_pieces(late_rows, (own * 2 + l) * thirds, grad_condition[l : l + 1, :])
    for which in range(2):
        row_pieces(late_rows, (own * 3 + which) * thirds, sum_heads[which])
    late[core, xy, z] = late_rows[...].astype(bf)
    late_g.one()
    in_s.three()
    late_g.two()
    early_g.five()
    out_s.five()
    late_g.three()
    in_s.four()
    late_g.four()
    late_g.five()
    in_s.five()

    for keep in keeps[3:]:
        keep.wait()
    landed(block_half.at[:, theirs], swap_recv.at[3])
    landed(token_half.at[:, theirs], swap_recv.at[4])
    for copy in spot.waits:
        copy.wait_send()


def main_pass(
    wide, sequence, own, tokens, upstream, labels, timesteps, class_table,
    mod_w, in_w, out_w, up_w, down_w, mod_b, in_b, out_b, up_b, down_b,
):
    bf, f32 = jnp.bfloat16, jnp.float32
    deep = plane(wide)[0]
    width, both = tokens.shape
    count, features = both // 2, 2 * width
    rows, hidden = up_w.shape
    vmem = pl.BlockSpec(memory_space=pltpu.VMEM)
    anywhere = pl.BlockSpec(memory_space=pl.ANY)
    smem = pl.BlockSpec(memory_space=pltpu.SMEM)
    sds, dma, ram = jax.ShapeDtypeStruct, pltpu.SemaphoreType.DMA, pltpu.VMEM
    wide_f32, wide_bf = ram((count, features), f32), ram((count, features), bf)
    flipped = ram((features, count), f32)
    column = ram((count, 1), f32)
    three = ram((3, count, features), bf)
    gathered = lambda columns: ram((2, 4, deep, rows, columns), bf)
    scratch = [
        flipped, flipped, ram(class_table.shape, bf), ram((2, ROLE_ROWS, hidden), f32),
        ram((ROLE_ROWS, features), f32), ram((1, 2 * hidden), f32),
        gathered(6 * width), gathered(4 * width), gathered(hidden), gathered(hidden),
        ram((10, features, features), bf), ram((features, 2 * hidden), bf), ram((features, 2 * hidden), bf),
        wide_f32, wide_f32, wide_f32, column, wide_bf, wide_f32, column, wide_bf, wide_bf, wide_f32,
        wide_f32, wide_f32,
        three, wide_bf, ram((own * features // LANES, sequence * LANES // HD, sequence), f32),
        wide_bf, wide_bf, three,
        ram((own, 8, features), f32), ram((own, 8, features), f32), ram((8, features), f32),
        ram((8, features), f32), ram((2, 1, features), f32), ram((1, features), f32),
        ram((1, 2 * hidden), f32), ram((1, features), f32),
        ram((EARLY_ROWS, LANES), f32), ram((LATE_ROWS, LANES), f32), flipped, flipped,
    ]
    for columns in (hidden, hidden, width, 3 * width):
        scratch += scatter_shapes(deep, rows, columns)
    scratch += [
        dma((6, deep - 1 + 7)), dma((6, deep - 1 + 7)), dma((4, deep + 3)), dma((4, deep + 3)),
        dma((5,)), dma((5,)), dma((5,)),
    ]
    return pl.pallas_call(
        functools.partial(main_kernel, wide, sequence),
        name="everything",
        out_shape=(
            sds((width, both), f32),
            sds((width, both), f32),
            sds((2, 4, deep, EARLY_ROWS, LANES), bf),
            sds((2, 4, deep, LATE_ROWS, LANES), bf),
            sds((rows, hidden), f32),
            sds((rows, hidden), f32),
            sds((rows, width), f32),
            sds((rows, 3 * width), f32),
        ),
        in_specs=[anywhere] * 2 + [smem] * 2 + [anywhere] + [vmem] * 10,
        out_specs=(anywhere,) * 2 + (vmem,) * 6,
        scratch_shapes=scratch,
        compiler_params=pltpu.CompilerParams(
            collective_id=0, has_side_effects=True, vmem_limit_bytes=VMEM_LIMIT
        ),
    )(
        tokens, upstream, labels, timesteps, class_table,
        mod_w, in_w, out_w, up_w, down_w, mod_b, in_b, out_b, up_b, down_b,
    )


def finish_kernel(
    wide, own, weight_scale,
    block_half, token_half, early, late, tot_up, tot_down, tot_out, tot_in,
    block_out, token_out, cond_out, table_out, mod_out, mod_bias_out, in_out, in_bias_out,
    out_out, out_bias_out, up_out, up_bias_out, down_out, down_bias_out,
    early_f, late_f, act_t, local,
):
    bf, f32 = jnp.bfloat16, jnp.float32
    deep = plane(wide)[0]
    copies = [
        pltpu.make_async_copy(block_half, block_out, local.at[0]),
        pltpu.make_async_copy(token_half, token_out, local.at[1]),
    ]
    for copy in copies:
        copy.start()
    me, core = lax.axis_index("wide"), lax.axis_index("narrow")
    rows, hidden = up_out.shape
    width = out_out.shape[1]
    features = 2 * width
    thirds = features // LANES
    devices = 2 * wide

    def dot(a, b, left, right):
        return lax.dot_general(a, b, (((left,), (right,)), ((), ())), preferred_element_type=f32)

    up_out[...] = tot_up[...] * weight_scale
    down_out[...] = tot_down[...] * weight_scale
    out_out[...] = tot_out[...] * weight_scale
    for j in range(3):
        in_out[j] = tot_in[:, j * width : (j + 1) * width] * weight_scale

    early_f[...] = early[...].astype(f32)
    late_f[...] = late[...].astype(f32)

    def everyone(ref, size, row):
        return ref[pl.ds(row, devices, stride=size), :]

    def latents(ref, size, first, step):
        return jnp.concatenate(
            [
                jnp.concatenate(
                    [everyone(ref, size, first + l * step + k) for k in range(thirds)], axis=1
                )
                for l in range(own)
            ],
            axis=0,
        )

    def half(value):
        return jnp.where(core == 0, value[:, :width], value[:, width:])

    act_t[...] = jnp.transpose(latents(early_f, EARLY_ROWS, own * 4 * thirds, thirds))
    act_mine = act_t[pl.ds(pl.multiple_of(me * rows, 8), rows), :].astype(bf)
    for j in range(6):
        if j < 2:
            grads = latents(late_f, LATE_ROWS, j * thirds, 2 * thirds)
        else:
            grads = latents(early_f, EARLY_ROWS, (j - 2) * thirds, 4 * thirds)
        grads = half(grads)
        mod_bias_out[j : j + 1, :] = jnp.sum(grads, axis=0, keepdims=True) * weight_scale
        mod_out[j] = dot(act_mine, grads.astype(bf), 1, 0) * weight_scale

    cond = latents(late_f, LATE_ROWS, own * 2 * thirds, thirds).astype(bf)
    low = own * 5 * thirds
    code = jnp.concatenate(
        [
            everyone(early_f, EARLY_ROWS, low + l) * 256.0 + everyone(early_f, EARLY_ROWS, low + own + l)
            for l in range(own)
        ],
        axis=0,
    )
    classes = table_out.shape[0]
    for first in range(0, classes, LANES):
        size = min(LANES, classes - first)
        names = lax.broadcasted_iota(jnp.int32, code.shape, 1).astype(f32) + float(first)
        hot = jnp.where(code == names, 1.0, 0.0).astype(bf)
        table_out[first : first + size, :] = dot(hot, cond, 0, 0)[:size]

    spot_xy, spot_z = me % 4, me // 4
    for n in range(2):
        seat = (n * 4 + spot_xy) * deep + spot_z
        for l in range(own):
            first = seat * LATE_ROWS + (own * 2 + l) * thirds
            for k in range(thirds):
                cond_out[n * own + l : n * own + l + 1, k * LANES : (k + 1) * LANES] = late_f[
                    pl.ds(first + k, 1), :
                ]

    def sums(ref, size, low, many):
        return [
            jnp.sum(everyone(ref, size, low + k), axis=0, keepdims=True) * weight_scale for k in range(many)
        ]

    low = own * 5 * thirds + 2 * own
    out_bias_out[...] = half(jnp.concatenate(sums(early_f, EARLY_ROWS, low, thirds), axis=1))
    down_bias_out[...] = half(jnp.concatenate(sums(early_f, EARLY_ROWS, low + thirds, thirds), axis=1))
    pieces = sums(early_f, EARLY_ROWS, low + 2 * thirds, 2 * hidden // LANES)
    many = len(pieces) // 2
    up_bias_out[...] = jnp.concatenate(
        [jnp.where(core == 0, pieces[k], pieces[many + k]) for k in range(many)], axis=1
    )
    for which in range(2):
        pieces = sums(late_f, LATE_ROWS, (own * 3 + which) * thirds, thirds)
        in_bias_out[which : which + 1, :] = half(jnp.concatenate(pieces, axis=1))
    for copy in copies:
        copy.wait()


def finish_pass(wide, own, weight_scale, classes, results):
    f32 = jnp.float32
    block_half, token_half, early, late, tot_up, tot_down, tot_out, tot_in = results
    rows, hidden = tot_up.shape
    width = tot_out.shape[1]
    vmem = pl.BlockSpec(memory_space=pltpu.VMEM)
    anywhere = pl.BlockSpec(memory_space=pl.ANY)
    sds, ram = jax.ShapeDtypeStruct, pltpu.VMEM
    early, late = early.reshape(-1, LANES), late.reshape(-1, LANES)
    return pl.pallas_call(
        functools.partial(finish_kernel, wide, own, weight_scale),
        name="finish",
        out_shape=(
            sds(block_half.shape, f32),
            sds(token_half.shape, f32),
            sds((2 * own, 2 * width), f32),
            sds((classes, 2 * width), f32),
            sds((6, rows, width), f32),
            sds((6, width), f32),
            sds((3, rows, width), f32),
            sds((2, width), f32),
            sds((rows, width), f32),
            sds((1, width), f32),
            sds((rows, hidden), f32),
            sds((1, hidden), f32),
            sds((rows, hidden), f32),
            sds((1, width), f32),
        ),
        in_specs=[anywhere] * 2 + [vmem] * 6,
        out_specs=(anywhere,) * 2 + (vmem,) * 12,
        scratch_shapes=[
            ram(early.shape, f32), ram(late.shape, f32), ram((2 * width, 2 * own * wide), f32),
            pltpu.SemaphoreType.DMA((2,)),
        ],
        compiler_params=pltpu.CompilerParams(vmem_limit_bytes=VMEM_LIMIT),
    )(block_half, token_half, early, late, tot_up, tot_down, tot_out, tot_in)


def fused_shards(
    latent_tokens, labels, timesteps, class_table, modulation_weight, modulation_bias, in_weight, in_bias,
    out_weight, out_bias, up_weight, up_bias, down_weight, down_bias, cotangent,
):
    wide = lax.axis_size("wide")
    own = labels.shape[0] // 2
    sequence = latent_tokens.shape[1] // labels.shape[0]
    weight_scale = (latent_tokens.shape[1] * wide) ** (-0.5)
    results = main_pass(
        wide, sequence, own, latent_tokens, cotangent, labels, timesteps, class_table,
        jnp.transpose(modulation_weight, (1, 0, 2)), jnp.transpose(in_weight, (1, 0, 2)),
        jnp.transpose(out_weight), up_weight, jnp.transpose(down_weight),
        modulation_bias, in_bias, out_bias.reshape(1, -1), up_bias.reshape(1, -1), down_bias.reshape(1, -1),
    )
    outs = list(finish_pass(wide, own, weight_scale, class_table.shape[0], results))
    outs[4] = jnp.transpose(outs[4], (1, 0, 2))
    outs[6] = jnp.transpose(outs[6], (1, 0, 2))
    for n in (9, 11, 13):
        outs[n] = outs[n].reshape(-1)
    outs[8] = jnp.transpose(outs[8])
    outs[12] = jnp.transpose(outs[12])
    return tuple(outs)


def fits(wide, features, latents):
    deep, side = plane(wide)
    rows = features // wide
    return side == 2 and deep > 1 and features % wide == 0 and rows % 8 == 0 and latents == 4 * wide


def pick(wide):
    def run(*args):
        chosen = fused_shards if fits(wide, args[3].shape[1], args[1].shape[0] * wide) else shards
        return chosen(*args)

    return run


def solution(mesh):
    return jax.shard_map(
        pick(mesh.shape["wide"]),
        mesh=mesh,
        in_specs=(
            P("narrow", "wide"),
            P("wide"),
            P("wide"),
            P(),
            P("wide", None, "narrow"),
            P(None, "narrow"),
            P("wide", None, "narrow"),
            P(None, "narrow"),
            P("narrow", "wide"),
            P("narrow"),
            P("wide", "narrow"),
            P("narrow"),
            P("narrow", "wide"),
            P("narrow"),
            P("narrow", "wide"),
        ),
        out_specs=(
            P("narrow", "wide"),
            P("narrow", "wide"),
            P("wide", None),
            P(),
            P("wide", None, "narrow"),
            P(None, "narrow"),
            P("wide", None, "narrow"),
            P(None, "narrow"),
            P("narrow", "wide"),
            P("narrow"),
            P("wide", "narrow"),
            P("narrow"),
            P("narrow", "wide"),
            P("narrow"),
        ),
        check_vma=False,
    )
```

```python
import functools
import math

import jax
import jax.numpy as jnp
from jax import lax
from jax.experimental import pallas as pl
from jax.experimental.pallas import tpu as pltpu
from jax.sharding import PartitionSpec as P

D = 384
HD = 64
LANES = 128
MESH = pl.DeviceIdType.MESH
VMEM_LIMIT = 60 * 1024 * 1024


EPS = 1e-06
GELU_K = 0.7978845608028654
GELU_A = 0.044715


def time_features(timesteps):
    half_width = D // 2
    frequencies = jnp.exp(
        jnp.arange(half_width, dtype=jnp.float32) * (-math.log(10000.0) / half_width)
    )
    angles = timesteps.astype(jnp.float32)[:, None] * frequencies[None, :]
    return jnp.concatenate([jnp.cos(angles), jnp.sin(angles)], axis=1)


def gelu_value(inputs):
    inner = GELU_K * (inputs + GELU_A * inputs * inputs * inputs)
    return 0.5 * inputs * (1.0 + jnp.tanh(inner))


def gelu_slope(inputs):
    inner = GELU_K * (inputs + GELU_A * inputs * inputs * inputs)
    tangent = jnp.tanh(inner)
    return 0.5 * (1.0 + tangent) + 0.5 * inputs * (1.0 - tangent * tangent) * GELU_K * (
        1.0 + 3.0 * GELU_A * inputs * inputs
    )


def silu_slope(inputs):
    sigmoid = jax.nn.sigmoid(inputs)
    return sigmoid * (1.0 + inputs * (1.0 - sigmoid))


def plane(wide):
    side = max(1, round((wide / 2) ** (1 / 3)))
    while wide % (side * side):
        side -= 1
    return wide // (side * side), side


class Place:
    def __init__(self, wide):
        self.deep, self.side = plane(wide)
        self.me = lax.axis_index("wide")
        self.core = lax.axis_index("narrow")
        self.z = self.me // (self.side * self.side)
        rest = self.me % (self.side * self.side)
        major, minor = rest // self.side, rest % self.side
        self.p = major + self.core * (minor - major)
        self.q = minor + self.core * (major - minor)
        self.p_stride = self.side + self.core * (1 - self.side)
        self.q_stride = 1 + self.core * (self.side - 1)

    def index(self, dz, dp, dq):
        return (
            ((self.z + dz) % self.deep) * (self.side * self.side)
            + ((self.p + dp) % self.side) * self.p_stride
            + ((self.q + dq) % self.side) * self.q_stride
        )

    def line_peers(self):
        return (
            [self.index(dz, 0, 0) for dz in range(1, self.deep)]
            + [self.index(0, dp, 0) for dp in range(1, self.side)]
            + [self.index(0, 0, dq) for dq in range(1, self.side)]
        )


def gather_kernel(
    wide, shard, tokens, upstream, biases,
    full, tokens_out, upstream_out, biases_out,
    send, recv, pair_send, pair_recv, swap_send, swap_recv, local,
):
    at = Place(wide)
    core, other = at.core, 1 - at.core
    barrier = pltpu.get_barrier_semaphore()
    peers = at.line_peers()
    for peer in peers:
        pl.semaphore_signal(barrier, 1, device_id=(peer, core), device_id_type=MESH)
    pl.semaphore_signal(barrier, 1, device_id=(at.me, other), device_id_type=MESH)
    pl.semaphore_wait(barrier, len(peers) + 1)
    waits = []
    count = 0

    def push(src, block, target):
        nonlocal count
        copy = pltpu.make_async_remote_copy(
            src, full.at[core, block], send.at[count], recv.at[block],
            device_id=(target, core), device_id_type=MESH,
        )
        copy.start()
        waits.append(copy)
        count += 1

    def share(src, block):
        copy = pltpu.make_async_remote_copy(
            src, full.at[core, block], pair_send.at[block], pair_recv.at[block],
            device_id=(at.me, other), device_id_type=MESH,
        )
        copy.start()
        waits.append(copy)

    def arrived(block):
        pltpu.make_async_copy(full.at[core, block], full.at[core, block], recv.at[block]).wait()

    for dz in range(1, at.deep):
        push(shard, at.me, at.index(dz, 0, 0))
    for dp in range(1, at.side):
        push(shard, at.me, at.index(0, dp, 0))
    for dq in range(1, at.side):
        push(shard, at.me, at.index(0, 0, dq))
    share(shard, at.me)
    half = tokens_out.shape[2]
    mine = pl.ds(pl.multiple_of(core * half, LANES), half)
    theirs = pl.ds(pl.multiple_of(other * half, LANES), half)
    for which, (src, dst) in enumerate(
        [(tokens.at[:, theirs], tokens_out), (upstream.at[:, theirs], upstream_out), (biases, biases_out)]
    ):
        copy = pltpu.make_async_remote_copy(
            src, dst.at[core], swap_send.at[which], swap_recv.at[which],
            device_id=(at.me, other), device_id_type=MESH,
        )
        copy.start()
        waits.append(copy)
    keeps = [
        pltpu.make_async_copy(src, dst, local.at[which])
        for which, (src, dst) in enumerate(
            [
                (tokens.at[:, mine], tokens_out.at[core]),
                (upstream.at[:, mine], upstream_out.at[core]),
                (biases, biases_out.at[core]),
                (shard, full.at[core, at.me]),
            ]
        )
    ]
    for keep in keeps:
        keep.start()
    for dz in range(1, at.deep):
        block = at.index(dz, 0, 0)
        arrived(block)
        for dp in range(1, at.side):
            push(full.at[core, block], block, at.index(0, dp, 0))
        for dq in range(1, at.side):
            push(full.at[core, block], block, at.index(0, 0, dq))
        share(full.at[core, block], block)
    for dz in range(at.deep):
        for dp in range(1, at.side):
            block = at.index(dz, dp, 0)
            arrived(block)
            for dq in range(1, at.side):
                push(full.at[core, block], block, at.index(0, 0, dq))
            share(full.at[core, block], block)
    for dz in range(at.deep):
        for dq in range(1, at.side):
            for dp in range(at.side):
                block = at.index(dz, dp, dq)
                arrived(block)
                share(full.at[core, block], block)
    for keep in keeps:
        keep.wait()
    for copy in waits:
        copy.wait_send()
    for block in range(wide):
        pltpu.make_async_copy(full.at[core, block], full.at[core, block], pair_recv.at[block]).wait()
    for which, (src, dst) in enumerate(
        [(tokens_out.at[core], None), (upstream_out.at[core], None), (biases_out.at[core], None)]
    ):
        pltpu.make_async_copy(src, src, swap_recv.at[which]).wait()


def gather_all(wide, shard, tokens, upstream, biases):
    rows, columns = shard.shape
    features, count = tokens.shape
    deep, side = plane(wide)
    sends = wide * (deep + 2 * side)
    vmem = pl.BlockSpec(memory_space=pltpu.VMEM)
    return pl.pallas_call(
        functools.partial(gather_kernel, wide),
        name="gather",
        out_shape=(
            jax.ShapeDtypeStruct((2, wide, rows, columns), shard.dtype),
            jax.ShapeDtypeStruct((2, features, count // 2), tokens.dtype),
            jax.ShapeDtypeStruct((2, features, count // 2), tokens.dtype),
            jax.ShapeDtypeStruct((2,) + biases.shape, biases.dtype),
        ),
        in_specs=[vmem] * 4,
        out_specs=(vmem,) * 4,
        scratch_shapes=[
            pltpu.SemaphoreType.DMA((sends,)),
            pltpu.SemaphoreType.DMA((wide,)),
            pltpu.SemaphoreType.DMA((wide,)),
            pltpu.SemaphoreType.DMA((wide,)),
            pltpu.SemaphoreType.DMA((3,)),
            pltpu.SemaphoreType.DMA((3,)),
            pltpu.SemaphoreType.DMA((4,)),
        ],
        compiler_params=pltpu.CompilerParams(
            collective_id=0, has_side_effects=True, vmem_limit_bytes=VMEM_LIMIT
        ),
    )(shard, tokens, upstream, biases)


def scatter_kernel(
    wide, parts, message, block_out, token_out,
    total, messages, block_half, token_half,
    from_pair, from_q, from_p, from_z, sums,
    send, pair_send, pair_recv, q_recv, p_recv, z_recv,
    note_send, note_recv, swap_send, swap_recv, local,
):
    at = Place(wide)
    core, other = at.core, 1 - at.core
    barrier = pltpu.get_barrier_semaphore()
    for step in range(wide):
        peer = (at.me + step) % wide
        if step:
            pl.semaphore_signal(barrier, 1, device_id=(peer, core), device_id_type=MESH)
        pl.semaphore_signal(barrier, 1, device_id=(peer, other), device_id_type=MESH)
    pl.semaphore_wait(barrier, 2 * wide - 1)
    waits = []

    deep, side = at.deep, at.side
    order = (
        [(dz, dp, dq) for dq in range(1, side) for dp in range(side) for dz in range(deep)]
        + [(dz, dp, 0) for dp in range(1, side) for dz in range(deep)]
        + [(dz, 0, 0) for dz in range(1, deep)]
        + [(0, 0, 0)]
    )
    for dz, dp, dq in order:
        block = at.index(dz, dp, dq)
        copy = pltpu.make_async_remote_copy(
            parts.at[other, block], from_pair.at[block], pair_send.at[block], pair_recv.at[block],
            device_id=(at.me, other), device_id_type=MESH,
        )
        copy.start()
        waits.append(copy)
    for step in range(wide):
        peer = (at.me + step) % wide
        for flip in range(2):
            if step == 0 and flip == 0:
                continue
            seat = core if flip == 0 else other
            copy = pltpu.make_async_remote_copy(
                message.at[seat], messages.at[at.me, core],
                note_send.at[step, flip], note_recv.at[at.me, core],
                device_id=(peer, seat), device_id_type=MESH,
            )
            copy.start()
            waits.append(copy)
    half = block_out.shape[0] // 2
    span = block_out.shape[1]
    columns = pl.ds(pl.multiple_of(core * span, LANES), span)
    mine = pl.ds(pl.multiple_of(core * half, 8), half)
    theirs = pl.ds(pl.multiple_of(other * half, 8), half)
    keeps = [pltpu.make_async_copy(message.at[core], messages.at[at.me, core], local.at[2])]
    for which, (src, dst) in enumerate([(block_out, block_half), (token_out, token_half)]):
        copy = pltpu.make_async_remote_copy(
            src.at[theirs], dst.at[:, columns], swap_send.at[which], swap_recv.at[which],
            device_id=(at.me, other), device_id_type=MESH,
        )
        copy.start()
        waits.append(copy)
        keeps.append(pltpu.make_async_copy(src.at[mine], dst.at[:, columns], local.at[which]))
    for keep in keeps:
        keep.start()

    def landed(ref, sem):
        pltpu.make_async_copy(ref, ref, sem).wait()

    f32 = jnp.float32
    for number, (dz, dp, dq) in enumerate(order):
        block = at.index(dz, dp, dq)
        landed(from_pair.at[block], pair_recv.at[block])
        value = parts[core, block].astype(f32) + from_pair[block].astype(f32)
        zs, ps = (at.z + dz) % deep, (at.p + dp) % side
        if dq == 0:
            for s in range(side - 1):
                landed(from_q.at[s, zs, ps], q_recv.at[s, zs, ps])
                value += from_q[s, zs, ps].astype(f32)
            if dp == 0:
                for s in range(side - 1):
                    landed(from_p.at[s, zs], p_recv.at[s, zs])
                    value += from_p[s, zs].astype(f32)
        if dq:
            target, slot, sem = (
                at.index(0, 0, dq), from_q.at[side - 1 - dq, zs, ps], q_recv.at[side - 1 - dq, zs, ps]
            )
        elif dp:
            target, slot, sem = (
                at.index(0, dp, 0), from_p.at[side - 1 - dp, zs], p_recv.at[side - 1 - dp, zs]
            )
        elif dz:
            target, slot, sem = at.index(dz, 0, 0), from_z.at[deep - 1 - dz], z_recv.at[deep - 1 - dz]
        else:
            for s in range(deep - 1):
                landed(from_z.at[s], z_recv.at[s])
                value += from_z[s].astype(f32)
            total[...] = value
            continue
        sums[block] = value.astype(jnp.bfloat16)
        copy = pltpu.make_async_remote_copy(
            sums.at[block], slot, send.at[number], sem,
            device_id=(target, core), device_id_type=MESH,
        )
        copy.start()
        waits.append(copy)
    for keep in keeps:
        keep.wait()
    for copy in waits:
        copy.wait_send()
    for step in range(wide):
        peer = (at.me + step) % wide
        if step:
            landed(messages.at[peer, core], note_recv.at[peer, core])
        landed(messages.at[peer, other], note_recv.at[peer, other])
    spare = pl.ds(pl.multiple_of(other * span, LANES), span)
    landed(block_half.at[:, spare], swap_recv.at[0])
    landed(token_half.at[:, spare], swap_recv.at[1])


def scatter_all(wide, parts, message, block_out, token_out):
    rows, columns = parts.shape[2:]
    features, count = block_out.shape
    deep, side = plane(wide)
    vmem = pl.BlockSpec(memory_space=pltpu.VMEM)
    bf, f32 = jnp.bfloat16, jnp.float32
    dma = pltpu.SemaphoreType.DMA
    return pl.pallas_call(
        functools.partial(scatter_kernel, wide),
        name="scatter",
        out_shape=(
            jax.ShapeDtypeStruct((rows, columns), f32),
            jax.ShapeDtypeStruct((wide,) + message.shape, bf),
            jax.ShapeDtypeStruct((features // 2, 2 * count), f32),
            jax.ShapeDtypeStruct((features // 2, 2 * count), f32),
        ),
        in_specs=[vmem] * 4,
        out_specs=(vmem,) * 4,
        scratch_shapes=[
            pltpu.VMEM((wide, rows, columns), bf),
            pltpu.VMEM((max(side - 1, 1), deep, side, rows, columns), bf),
            pltpu.VMEM((max(side - 1, 1), deep, rows, columns), bf),
            pltpu.VMEM((max(deep - 1, 1), rows, columns), bf),
            pltpu.VMEM((wide, rows, columns), bf),
            dma((wide,)),
            dma((wide,)),
            dma((wide,)),
            dma((max(side - 1, 1), deep, side)),
            dma((max(side - 1, 1), deep)),
            dma((max(deep - 1, 1),)),
            dma((wide, 2)),
            dma((wide, 2)),
            dma((2,)),
            dma((2,)),
            dma((3,)),
        ],
        compiler_params=pltpu.CompilerParams(
            collective_id=1, has_side_effects=True, vmem_limit_bytes=VMEM_LIMIT
        ),
    )(parts, message, block_out, token_out)


def norm_forward(values):
    average = jnp.mean(values, axis=-1, keepdims=True)
    centred = values - average
    inv_std = lax.rsqrt(jnp.mean(centred * centred, axis=-1, keepdims=True) + EPS)
    return centred * inv_std, inv_std


def norm_backward(grad_norm, normed, inv_std):
    first = jnp.mean(grad_norm, axis=-1, keepdims=True)
    second = jnp.mean(grad_norm * normed, axis=-1, keepdims=True)
    return inv_std * (grad_norm - first - normed * second)


def block_kernel(
    own, sequence, width, hidden,
    tokens, upstream, full, modulation, bias_in, bias_out, bias_up, bias_down,
    block_out, token_out, parts, grad_mod, sum_heads, sum_out, sum_up, sum_down,
    hid, upg, normed, inv, mod_bf, normed_two, inv_two, mod_two, gff, attention, feed, gmod,
    qkv, att_heads, att, weights, gatt_heads, gatt, gproj_heads, gproj,
):
    bf, f32 = jnp.bfloat16, jnp.float32
    features = 2 * width
    heads = features // HD
    per_half = heads // 2
    count = own * sequence
    score_scale = HD ** (-0.5)
    rows = LANES if sequence % LANES == 0 else sequence
    blocks = count // rows
    chunk = 256 if hidden % 256 == 0 else hidden
    chunks = hidden // chunk
    in_at, out_at = 2 * hidden, 2 * hidden + 3 * width

    def dot(a, b, left, right):
        return lax.dot_general(a, b, (((left,), (right,)), ((), ())), preferred_element_type=f32)

    def total(value):
        return jnp.sum(value, axis=0, keepdims=True)

    grad_mod[...] = jnp.zeros_like(grad_mod)
    sum_heads[...] = jnp.zeros_like(sum_heads)
    sum_out[...] = jnp.zeros_like(sum_out)
    sum_down[...] = jnp.zeros_like(sum_down)
    feed[...] = jnp.zeros_like(feed)
    gmod[...] = jnp.zeros_like(gmod)

    def span(r):
        return pl.ds(pl.multiple_of(r * rows, rows), rows), (r * rows) // sequence

    @pl.loop(0, blocks)
    def _(r):
        at, b = span(r)
        values = jnp.transpose(tokens[:, at])
        hid[at, :] = values
        unit, scale = norm_forward(values)
        normed[at, :] = unit
        inv[at, :] = scale
        mod_bf[at, :] = (unit * (1.0 + modulation[b, 1:2, :]) + modulation[b, 0:1, :]).astype(bf)
        up = jnp.transpose(upstream[:, at])
        upg[at, :] = up
        grad = modulation[b, 5:6, :] * up
        gff[at, :] = grad.astype(bf)
        sum_down[...] += total(grad)

    @pl.loop(0, blocks)
    def _(r):
        at, b = span(r)
        for n in range(2):
            out = dot(mod_bf[at, :], full[n, :, in_at:out_at], 1, 0)
            for j in range(3):
                for h in range(per_half):
                    low = j * width + h * HD
                    piece = out[:, low : low + HD]
                    if j != 1:
                        piece = piece + bias_in[j // 2, n * per_half + h]
                    qkv[j, n * per_half + h, at, :] = piece.astype(bf)

    @pl.loop(0, own * heads)
    def _(i):
        b, h = i // heads, i % heads
        at = pl.ds(pl.multiple_of(b * sequence, sequence), sequence)
        scores = dot(qkv[0, h, at, :], qkv[1, h, at, :], 1, 1) * score_scale
        log_total = jnp.log(jnp.sum(jnp.exp(scores), axis=-1, keepdims=True))
        mix = jnp.exp(scores - log_total)
        weights[i] = mix
        att_heads[h, at, :] = dot(mix.astype(bf), qkv[2, h, at, :], 1, 0).astype(bf)

    for n in range(2):
        att[n] = jnp.concatenate([att_heads[n * per_half + h] for h in range(per_half)], axis=1)

    @pl.loop(0, blocks)
    def _(r):
        at, b = span(r)
        result = bias_out[...] + sum(
            dot(att[n, at, :], full[n, :, out_at : out_at + width], 1, 1) for n in range(2)
        )
        attention[at, :] = result
        middle = hid[at, :] + modulation[b, 2:3, :] * result
        hid[at, :] = middle
        unit, scale = norm_forward(middle)
        normed_two[at, :] = unit
        inv_two[at, :] = scale
        mod_two[at, :] = (unit * (1.0 + modulation[b, 4:5, :]) + modulation[b, 3:4, :]).astype(bf)

    @pl.loop(0, 2 * chunks)
    def _(i):
        n, c = i // chunks, i % chunks
        at = pl.ds(pl.multiple_of(c * chunk, chunk), chunk)
        down_at = pl.ds(pl.multiple_of(hidden + c * chunk, chunk), chunk)
        up_w, down_w = full[n, :, at], full[n, :, down_at]
        pre = dot(mod_two[...], up_w, 1, 0) + bias_up[n, :, at]
        tangent = jnp.tanh(GELU_K * (pre + GELU_A * pre * pre * pre))
        act = (0.5 * pre * (1.0 + tangent)).astype(bf)
        slope = 0.5 * (1.0 + tangent) + 0.5 * pre * (1.0 - tangent * tangent) * GELU_K * (
            1.0 + 3.0 * GELU_A * pre * pre
        )
        feed[...] += dot(act, down_w, 1, 1)
        parts[n, :, down_at] = dot(gff[...], act, 0, 0).astype(bf)
        grad = dot(gff[...], down_w, 1, 0) * slope
        sum_up[n, :, at] = total(grad)
        grad_bf = grad.astype(bf)
        parts[n, :, at] = dot(mod_two[...], grad_bf, 0, 0).astype(bf)
        gmod[...] += dot(grad_bf, up_w, 1, 1)

    @pl.loop(0, blocks)
    def _(r):
        at, b = span(r)
        ff = feed[at, :] + bias_down[...]
        up = upg[at, :]
        block_out[:, at] = jnp.transpose(hid[at, :] + modulation[b, 5:6, :] * ff)
        grad_mod[b, 5:6, :] += total(up * ff)
        grad, unit = gmod[at, :], normed_two[at, :]
        grad_mod[b, 3:4, :] += total(grad)
        grad_mod[b, 4:5, :] += total(grad * unit)
        middle = up + norm_backward(grad * (1.0 + modulation[b, 4:5, :]), unit, inv_two[at, :])
        upg[at, :] = middle
        grad_mod[b, 2:3, :] += total(middle * attention[at, :])
        grad_att = modulation[b, 2:3, :] * middle
        sum_out[...] += total(grad_att)
        grad_bf = grad_att.astype(bf)
        gatt[at, :] = grad_bf
        for n in range(2):
            out = dot(grad_bf, full[n, :, out_at : out_at + width], 1, 0).astype(bf)
            for h in range(per_half):
                gatt_heads[n * per_half + h, at, :] = out[:, h * HD : (h + 1) * HD]

    @pl.loop(0, own * heads)
    def _(i):
        b, h = i // heads, i % heads
        at = pl.ds(pl.multiple_of(b * sequence, sequence), sequence)
        mix, grad_out = weights[i], gatt_heads[h, at, :]
        grad_mix = dot(grad_out, qkv[2, h, at, :], 1, 1)
        dots = jnp.sum(mix * grad_mix, axis=-1, keepdims=True)
        grad_scores = (mix * (grad_mix - dots) * score_scale).astype(bf)
        grad_q = dot(grad_scores, qkv[1, h, at, :], 1, 0)
        grad_k = dot(grad_scores, qkv[0, h, at, :], 0, 0)
        grad_v = dot(mix.astype(bf), grad_out, 0, 0)
        gproj_heads[0, h, at, :] = grad_q.astype(bf)
        gproj_heads[1, h, at, :] = grad_k.astype(bf)
        gproj_heads[2, h, at, :] = grad_v.astype(bf)
        sum_heads[0, h] += total(grad_q)
        sum_heads[1, h] += total(grad_v)

    for n in range(2):
        gproj[n] = jnp.concatenate(
            [gproj_heads[j, n * per_half + h] for j in range(3) for h in range(per_half)], axis=1
        )
        parts[n, :, in_at:] = jnp.concatenate(
            [dot(mod_bf[...], gproj[n], 0, 0), dot(gatt[...], att[n], 0, 0)], axis=1
        ).astype(bf)

    @pl.loop(0, blocks)
    def _(r):
        at, b = span(r)
        grad = sum(dot(gproj[n, at, :], full[n, :, in_at:out_at], 1, 1) for n in range(2))
        unit = normed[at, :]
        grad_mod[b, 0:1, :] += total(grad)
        grad_mod[b, 1:2, :] += total(grad * unit)
        back = norm_backward(grad * (1.0 + modulation[b, 1:2, :]), unit, inv[at, :])
        token_out[:, at] = jnp.transpose(upg[at, :] + back)


def block_pass(
    tokens, upstream, full, modulation, bias_in, bias_out, bias_up, bias_down, own, sequence, width, hidden
):
    bf, f32 = jnp.bfloat16, jnp.float32
    features = 2 * width
    heads = features // HD
    count = own * sequence
    bias_in = jnp.transpose(bias_in.reshape(2, 2, width), (1, 0, 2)).reshape(2, heads, 1, HD)
    vmem = pl.BlockSpec(memory_space=pltpu.VMEM)
    sds = jax.ShapeDtypeStruct
    wide_f32, wide_bf = pltpu.VMEM((count, features), f32), pltpu.VMEM((count, features), bf)
    column = pltpu.VMEM((count, 1), f32)
    by_head = pltpu.VMEM((heads, count, HD), bf)
    by_head_three = pltpu.VMEM((3, heads, count, HD), bf)
    block_out, token_out, parts, grad_mod, sum_heads, sum_out, sum_up, sum_down = pl.pallas_call(
        functools.partial(block_kernel, own, sequence, width, hidden),
        name="block",
        out_shape=(
            sds((features, count), f32),
            sds((features, count), f32),
            sds((2, features, 2 * hidden + 4 * width), bf),
            sds((own, 6, features), f32),
            sds((2, heads, 1, HD), f32),
            sds((1, features), f32),
            sds((2, 1, hidden), f32),
            sds((1, features), f32),
        ),
        in_specs=[vmem] * 8,
        out_specs=(vmem,) * 8,
        scratch_shapes=[
            wide_f32, wide_f32, wide_f32, column, wide_bf, wide_f32, column, wide_bf, wide_bf, wide_f32,
            wide_f32, wide_f32,
            by_head_three, by_head, pltpu.VMEM((2, count, width), bf),
            pltpu.VMEM((own * heads, sequence, sequence), f32),
            by_head, wide_bf, by_head_three, pltpu.VMEM((2, count, 3 * width), bf),
        ],
        compiler_params=pltpu.CompilerParams(vmem_limit_bytes=VMEM_LIMIT),
    )(
        tokens, upstream, full, modulation, bias_in, bias_out.reshape(1, -1),
        bias_up.reshape(2, 1, hidden), bias_down.reshape(1, -1),
    )
    by_half = lambda value: value.reshape(2, -1)
    bias_sums = jnp.concatenate(
        [
            by_half(sum_heads[0]), by_half(sum_heads[1]), by_half(sum_out), by_half(sum_up), by_half(sum_down),
        ],
        axis=1,
    )
    return block_out, token_out, parts, grad_mod, bias_sums


def codes(values):
    return jnp.concatenate([values // 256, values % 256]).astype(jnp.bfloat16)


def shards(
    latent_tokens,
    labels,
    timesteps,
    class_table,
    modulation_weight,
    modulation_bias,
    in_weight,
    in_bias,
    out_weight,
    out_bias,
    up_weight,
    up_bias,
    down_weight,
    down_bias,
    cotangent,
):
    bf, f32 = jnp.bfloat16, jnp.float32
    wide = lax.axis_size("wide")
    me, core = lax.axis_index("wide"), lax.axis_index("narrow")
    latent_count = labels.shape[0]
    own = latent_count // 2
    width = latent_tokens.shape[0]
    hidden = up_weight.shape[1]
    local_tokens = latent_tokens.shape[1]
    sequence = local_tokens // latent_count
    weight_scale = (local_tokens * wide) ** (-0.5)
    rows = up_weight.shape[0]

    ids = jnp.concatenate([codes(labels), codes(timesteps)])
    ids = jnp.pad(ids[None, :], ((0, rows - 1), (0, LANES - ids.shape[0])))
    shard = jnp.concatenate(
        [
            up_weight,
            jnp.transpose(down_weight),
            in_weight.reshape(rows, 3 * width),
            jnp.transpose(out_weight),
            modulation_weight.reshape(rows, 6 * width),
            ids,
        ],
        axis=1,
    )
    bias_parts = [in_bias.reshape(-1), out_bias, up_bias, down_bias, modulation_bias.reshape(-1)]
    biases = jnp.concatenate(bias_parts)
    pad = -biases.shape[0] % (8 * LANES)
    biases = jnp.pad(biases, (0, pad)).reshape(-1, LANES)
    full, tokens, upstream, both = gather_all(wide, shard, latent_tokens, cotangent, biases)
    ids_all = full[0, :, 0, -LANES:].astype(jnp.int32)
    pick = lambda n: ids_all[:, n * latent_count : (n + 1) * latent_count].reshape(-1)
    labels_all = pick(0) * 256 + pick(1)
    times_all = pick(2) * 256 + pick(3)
    class_ids = jnp.arange(class_table.shape[0], dtype=jnp.int32)
    every_hot = (labels_all[:, None] == class_ids[None, :]).astype(bf)
    condition_all = jnp.dot(every_hot, class_table, preferred_element_type=f32) + time_features(
        times_all
    )
    activated_all = jax.nn.silu(condition_all).astype(bf)
    first = me * latent_count + core * own
    condition = lax.dynamic_slice_in_dim(condition_all, first, own, 0)
    activated = lax.dynamic_slice_in_dim(activated_all, first, own, 0)

    full = full.reshape(2, rows * wide, -1)
    flat = both.reshape(2, -1)
    offset = 0
    halves = []
    for part in bias_parts:
        halves.append(flat[:, offset : offset + part.shape[0]])
        offset += part.shape[0]
    bias_in, bias_out, bias_up, bias_down, bias_mod = halves
    mod_at = 2 * hidden + 4 * width
    mod_full = full[:, :, mod_at : mod_at + 6 * width]
    modulation = jnp.einsum("bd,ndf->nbf", activated, mod_full, preferred_element_type=f32) + bias_mod[:, None]
    modulation = jnp.transpose(modulation.reshape(2, own, 6, width), (1, 2, 0, 3)).reshape(own, 6, 2 * width)

    block_output, token_grads, parts, grad_modulation, bias_sums = block_pass(
        tokens.reshape(2 * width, -1), upstream.reshape(2 * width, -1), full, modulation,
        bias_in, bias_out, bias_up, bias_down, own, sequence, width, hidden,
    )

    grad_modulation_bf = grad_modulation.astype(bf)
    by_half = jnp.transpose(grad_modulation_bf.reshape(own, 6, 2, width), (2, 0, 1, 3)).reshape(2, own, 6 * width)
    grad_activated = jnp.einsum("nbf,ndf->bd", by_half, mod_full, preferred_element_type=f32)
    condition_rows = (grad_activated * silu_slope(condition) * sequence ** (-0.5)).astype(bf)
    message = jnp.concatenate(
        [
            by_half.reshape(2, -1),
            jnp.broadcast_to(condition_rows.reshape(1, -1), (2, own * 2 * width)),
            bias_sums.astype(bf),
        ],
        axis=1,
    )
    used = message.shape[1]
    message = jnp.pad(message, ((0, 0), (0, -used % (16 * LANES)))).reshape(2, -1, LANES)
    total, messages, block_half, token_half = scatter_all(
        wide, parts.reshape(2, wide, rows, -1), message, block_output, token_grads
    )
    flat_notes = messages.reshape(wide * 2, -1)
    gm_all = flat_notes[:, : own * 6 * width].reshape(wide * latent_count, 6 * width)
    cond_all = flat_notes[:, own * 6 * width : own * 8 * width].reshape(wide * latent_count, 2 * width)
    sums = jnp.sum(flat_notes[:, own * 8 * width : used].astype(f32), axis=0) * weight_scale
    act_mine = lax.dynamic_slice_in_dim(activated_all, me * rows, rows, 1)
    mod_grads = jnp.einsum("bd,bf->df", act_mine, gm_all, preferred_element_type=f32) * weight_scale
    mod_bias_grads = jnp.sum(gm_all.astype(f32), axis=0) * weight_scale
    table_grads = jnp.einsum("bc,bd->cd", every_hot, cond_all, preferred_element_type=f32)
    condition_grads = lax.dynamic_slice_in_dim(cond_all, me * latent_count, latent_count, 0).astype(f32)
    total = total * weight_scale
    up_part = total[:, :hidden]
    down_part = jnp.transpose(total[:, hidden : 2 * hidden])
    in_part = total[:, 2 * hidden : 2 * hidden + 3 * width].reshape(rows, 3, width)
    out_part = jnp.transpose(total[:, 2 * hidden + 3 * width :])
    return (
        block_half,
        token_half,
        condition_grads,
        table_grads,
        mod_grads.reshape(rows, 6, width),
        mod_bias_grads.reshape(6, width),
        in_part,
        sums[: 2 * width].reshape(2, width),
        out_part,
        sums[2 * width : 3 * width],
        up_part,
        sums[3 * width : 3 * width + hidden],
        down_part,
        sums[3 * width + hidden :],
    )


ROLE_ROWS = 16
EARLY_ROWS, LATE_ROWS = 64, 32


class Spot:
    def __init__(self, wide):
        self.deep, self.side = plane(wide)
        self.me = lax.axis_index("wide")
        self.core = lax.axis_index("narrow")
        self.other = 1 - self.core
        self.z = self.me // 4
        rest = self.me % 4
        major, minor = rest // 2, rest % 2
        self.p = major + self.core * (minor - major)
        self.q = minor + self.core * (major - minor)
        self.xy = rest
        self.waits = []

    def line(self, dp, dq):
        p, q = (self.p + dp) % 2, (self.q + dq) % 2
        return p * (2 - self.core) + q * (1 + self.core)

    def depth(self, dz):
        return (self.z + dz) % self.deep

    def device(self, dz, dp, dq):
        return self.depth(dz) * 4 + self.line(dp, dq)

    def push(self, src, dst, send, recv, target, seat):
        copy = pltpu.make_async_remote_copy(
            src, dst, send, recv, device_id=(target, seat), device_id_type=MESH
        )
        copy.start()
        self.waits.append(copy)

    def p_peer(self):
        return self.device(0, 1, 0)

    def q_peer(self):
        return self.device(0, 0, 1)

    def enter(self):
        barrier = pltpu.get_barrier_semaphore()
        peers = [self.device(dz, 0, 0) for dz in range(1, self.deep)] + [self.p_peer(), self.q_peer(), self.device(0, 1, 1)]
        for peer in peers:
            pl.semaphore_signal(barrier, 1, device_id=(peer, self.core), device_id_type=MESH)
        pl.semaphore_signal(barrier, 1, device_id=(self.me, self.other), device_id_type=MESH)
        pl.semaphore_wait(barrier, len(peers) + 1)


def landed(ref, sem):
    pltpu.make_async_copy(ref, ref, sem).wait()


class Gather:
    def __init__(self, spot, buf, send, recv, number, direct=False):
        self.spot, self.buf, self.direct = spot, buf, direct
        self.send = lambda n: send.at[number, n]
        self.recv = lambda n: recv.at[number, n]
        self.base = spot.deep - 1

    def mine(self):
        s = self.spot
        return self.buf.at[s.core, s.xy, s.z]

    def share(self, line, send, recv, target, seat):
        ref = self.buf.at[self.spot.core, line]
        self.spot.push(ref, ref, self.send(send), self.recv(recv), target, seat)

    def one(self):
        s = self.spot
        for dz in range(1, s.deep):
            s.push(self.mine(), self.mine(), self.send(dz - 1), self.recv(dz - 1), s.device(dz, 0, 0), s.core)

    def two(self):
        s, base = self.spot, self.base
        for dz in range(1, s.deep):
            landed(self.buf.at[s.core, s.xy, s.depth(-dz)], self.recv(dz - 1))
        line = s.line(0, 0)
        self.share(line, base, base, s.p_peer(), s.core)
        self.share(line, base + 1, base + 1, s.q_peer(), s.core)
        if self.direct:
            self.share(line, base + 3, base + 2, s.device(0, 1, 1), s.core)
        self.share(line, base + 2, base + 3, s.me, s.other)

    def three(self):
        s, base = self.spot, self.base
        line = s.line(1, 0)
        landed(self.buf.at[s.core, line], self.recv(base))
        if not self.direct:
            self.share(line, base + 3, base + 2, s.q_peer(), s.core)
        self.share(line, base + 4, base + 4, s.me, s.other)

    def four(self):
        s, base = self.spot, self.base
        for dp in range(2):
            line = s.line(dp, 1)
            landed(self.buf.at[s.core, line], self.recv(base + 1 + dp))
            self.share(line, base + 5 + dp, base + 5 + dp, s.me, s.other)

    def five(self):
        s, base = self.spot, self.base
        for slot, (dp, dq) in enumerate([(0, 0), (0, 1), (1, 0), (1, 1)]):
            landed(self.buf.at[s.other, s.line(dp, dq)], self.recv(base + 3 + slot))


class Scatter:
    def __init__(self, spot, parts, bufs, send, recv, number, direct=False):
        self.spot, self.parts, self.direct = spot, parts, direct
        self.from_pair, self.to_q, self.from_q, self.to_p, self.from_p, self.to_z, self.from_z, self.total = bufs
        self.send = lambda n: send.at[number, n]
        self.recv = lambda n: recv.at[number, n]

    def pair(self, line):
        f32 = jnp.float32
        return self.parts[self.spot.core, line].astype(f32) + self.from_pair[line].astype(f32)

    def one(self):
        s = self.spot
        s.push(self.parts.at[s.other], self.from_pair, self.send(0), self.recv(0), s.me, s.other)

    def two(self):
        s, bf = self.spot, jnp.bfloat16
        landed(self.from_pair, self.recv(0))
        for dp in (1, 0):
            self.to_q[dp] = self.pair(s.line(dp, 1)).astype(bf)
            target = s.device(0, dp, 1) if self.direct else s.q_peer()
            s.push(self.to_q.at[dp], self.from_q.at[dp], self.send(1 + dp), self.recv(1 + dp), target, s.core)
        if self.direct:
            self.to_p[...] = self.pair(s.line(1, 0)).astype(bf)
            s.push(self.to_p, self.from_p, self.send(3), self.recv(3), s.p_peer(), s.core)

    def three(self):
        s = self.spot
        landed(self.from_q.at[1], self.recv(2))
        if not self.direct:
            value = self.pair(s.line(1, 0)) + self.from_q[1].astype(jnp.float32)
            self.to_p[...] = value.astype(jnp.bfloat16)
            s.push(self.to_p, self.from_p, self.send(3), self.recv(3), s.p_peer(), s.core)

    def four(self):
        s, f32 = self.spot, jnp.float32
        landed(self.from_q.at[0], self.recv(1))
        landed(self.from_p, self.recv(3))
        for dz in list(range(1, s.deep)) + [0]:
            z = s.depth(dz)
            value = self.parts[s.core, s.xy, z].astype(f32) + self.from_pair[s.xy, z].astype(f32)
            value = value + self.from_q[0, z].astype(f32) + self.from_p[z].astype(f32)
            if self.direct:
                value = value + self.from_q[1, z].astype(f32)
            if dz:
                self.to_z[dz - 1] = value.astype(jnp.bfloat16)
                s.push(
                    self.to_z.at[dz - 1], self.from_z.at[dz - 1], self.send(3 + dz), self.recv(3 + dz),
                    s.device(dz, 0, 0), s.core,
                )
            else:
                self.total[...] = value

    def five(self):
        s = self.spot
        for dz in range(1, s.deep):
            landed(self.from_z.at[dz - 1], self.recv(3 + dz))
        value = self.total[...]
        for dz in range(1, s.deep):
            value = value + self.from_z[dz - 1].astype(jnp.float32)
        self.total[...] = value


def scatter_shapes(deep, rows, columns):
    bf = jnp.bfloat16
    return [
        pltpu.VMEM((2, 4, deep, rows, columns), bf),
        pltpu.VMEM((4, deep, rows, columns), bf),
        pltpu.VMEM((2, deep, rows, columns), bf),
        pltpu.VMEM((2, deep, rows, columns), bf),
        pltpu.VMEM((deep, rows, columns), bf),
        pltpu.VMEM((deep, rows, columns), bf),
        pltpu.VMEM((deep - 1, rows, columns), bf),
        pltpu.VMEM((deep - 1, rows, columns), bf),
    ]


def main_kernel(
    wide, sequence,
    tokens, upstream, labels, timesteps, class_table,
    mod_w, in_w, out_w, up_w, down_w, mod_b, in_b, out_b, up_b, down_b,
    block_half, token_half, early, late, tot_a, tot_b, tot_c, tot_out, tot_in,
    tok, ups, table, bias_pack, bias_full, bias_up,
    g_one, g_two, g_a, g_b, g_c, square, w_up, w_down,
    hid, upg, normed, inv, mod_bf, normed_two, inv_two, mod_two, gff, attention, feed, gmod,
    qkv, att, weights, gatt, gattended, gproj,
    modv, gm, act, slope, sum_heads, sum_out, sum_up, sum_down, early_rows, late_rows, bout, tout,
    *rest,
):
    bf, f32 = jnp.bfloat16, jnp.float32
    groups = [rest[8 * n : 8 * n + 8] for n in range(5)]
    out_parts, in_parts = groups[3][0], groups[4][0]
    g_send, g_recv, s_send, s_recv, swap_send, swap_recv, local = rest[40:]
    width, hidden = in_w.shape[2], up_w.shape[1]
    features, count = tok.shape
    shard_rows = up_w.shape[0]
    own = count // sequence
    pairs = features // LANES
    spot = Spot(wide)
    core, other, deep = spot.core, spot.other, spot.deep
    score_scale = HD ** (-0.5)
    cond_scale = sequence ** (-0.5)
    rows = LANES
    blocks = count // rows
    chunks = 3
    chunk = hidden // chunks
    thirds = features // LANES

    def dot(a, b, left, right):
        return lax.dot_general(a, b, (((left,), (right,)), ((), ())), preferred_element_type=f32)

    def total(value):
        return jnp.sum(value, axis=0, keepdims=True)

    def span(r):
        return pl.ds(pl.multiple_of(r * rows, rows), rows), (r * rows) // sequence

    mine = pl.ds(pl.multiple_of(core * count, LANES), count)
    theirs = pl.ds(pl.multiple_of(other * count, LANES), count)
    my_rows = pl.ds(pl.multiple_of(core * width, 8), width)
    their_rows = pl.ds(pl.multiple_of(other * width, 8), width)
    keeps = [
        pltpu.make_async_copy(class_table, table, local.at[0]),
        pltpu.make_async_copy(tokens.at[:, mine], tok.at[my_rows], local.at[1]),
        pltpu.make_async_copy(upstream.at[:, mine], ups.at[my_rows], local.at[2]),
    ]
    for keep in keeps:
        keep.start()

    xy, z = spot.xy, spot.z
    g_one[core, xy, z] = jnp.concatenate(
        [in_w[j].astype(f32) for j in range(3)]
        + [mod_w[j].astype(f32) for j in range(2)],
        axis=1,
    ).astype(bf)
    g_two[core, xy, z] = jnp.concatenate(
        [mod_w[j].astype(f32) for j in range(2, 6)] + [out_w[...].astype(f32)], axis=1
    ).astype(bf)
    for c, buf in enumerate([g_a, g_b, g_c]):
        buf[core, xy, z, :, :chunk] = up_w[:, c * chunk : (c + 1) * chunk]
        buf[core, xy, z, :, chunk:] = down_w[:, c * chunk : (c + 1) * chunk]
    bias_pack[core] = jnp.zeros(bias_pack.shape[1:], f32)
    bias_pack[core, 0:1, :] = up_b[...].reshape(1, -1)
    bias_pack[core, 1:2, :width] = out_b[...]
    bias_pack[core, 2:3, :width] = down_b[...]
    bias_pack[core, 3:5, :width] = in_b[...]
    bias_pack[core, 5:11, :width] = mod_b[...]

    gather = [
        Gather(spot, buf, g_send, g_recv, n, direct=n > 4)
        for n, buf in enumerate([g_one, g_two, g_a, g_b, g_c, early, late])
    ]
    scatter = [
        Scatter(spot, bufs[0], tuple(bufs[1:]) + (out,), s_send, s_recv, n, direct=n == 4)
        for n, (bufs, out) in enumerate(
            zip(groups, [tot_a, tot_b, tot_c, tot_out, tot_in])
        )
    ]
    one, two, a_g, b_g, c_g, early_g, late_g = gather
    a_s, b_s, c_s, out_s, in_s = scatter

    spot.enter()
    one.one()
    spot.push(bias_pack.at[core], bias_pack.at[core], swap_send.at[0], swap_recv.at[0], spot.me, other)
    spot.push(tokens.at[:, theirs], tok.at[my_rows], swap_send.at[1], swap_recv.at[1], spot.me, other)
    spot.push(upstream.at[:, theirs], ups.at[my_rows], swap_send.at[2], swap_recv.at[2], spot.me, other)
    gm[...] = jnp.zeros_like(gm)
    sum_heads[...] = jnp.zeros_like(sum_heads)
    sum_out[...] = jnp.zeros_like(sum_out)
    sum_down[...] = jnp.zeros_like(sum_down)
    feed[...] = jnp.zeros_like(feed)
    gmod[...] = jnp.zeros_like(gmod)
    early_rows[...] = jnp.zeros_like(early_rows)
    late_rows[...] = jnp.zeros_like(late_rows)

    my_labels = [labels[core * own + l] for l in range(own)]
    my_times = [timesteps[core * own + l] for l in range(own)]

    def by_row(scalars, shape):
        row = lax.broadcasted_iota(jnp.int32, shape, 0)
        value = jnp.full(shape, -1, jnp.int32)
        for l, scalar in enumerate(scalars):
            value = jnp.where(row == l, scalar, value)
        return value

    keeps[0].wait()
    classes = class_table.shape[0]
    hot = by_row(my_labels, (8, classes)) == lax.broadcasted_iota(jnp.int32, (8, classes), 1)
    half_width = features // 2
    power = lax.broadcasted_iota(jnp.int32, (8, half_width), 1).astype(f32)
    angles = by_row(my_times, (8, half_width)).astype(f32) * jnp.exp(power * (-math.log(10000.0) / half_width))
    condition = dot(hot.astype(f32).astype(bf), table[...], 1, 0) + jnp.concatenate(
        [jnp.cos(angles), jnp.sin(angles)], axis=1
    )
    sigmoid = 1.0 / (1.0 + jnp.exp(-condition))
    act[...] = condition * sigmoid
    slope[...] = sigmoid * (1.0 + condition * (1.0 - sigmoid)) * cond_scale

    one.two()
    two.one()
    a_g.one()
    b_g.one()
    c_g.one()
    keeps[1].wait()
    keeps[2].wait()
    landed(tok.at[their_rows], swap_recv.at[1])
    landed(ups.at[their_rows], swap_recv.at[2])

    @pl.loop(0, blocks)
    def _(r):
        at, _ = span(r)
        values = jnp.transpose(tok[:, at])
        hid[at, :] = values
        unit, scale = norm_forward(values)
        normed[at, :] = unit
        inv[at, :] = scale
        upg[at, :] = jnp.transpose(ups[:, at])

    landed(bias_pack.at[other], swap_recv.at[0])
    bias_full[...] = jnp.concatenate([bias_pack[n, :, :width] for n in range(2)], axis=1)
    bias_up[...] = jnp.concatenate([bias_pack[n, 0:1, :] for n in range(2)], axis=1)

    one.three()
    two.two()
    one.four()
    a_g.two()
    one.five()

    def regroup(buf, places):
        @pl.loop(0, 2 * deep)
        def _(k):
            depth, pair = k // 2, k % 2
            at = pl.ds(pl.multiple_of(k * 2 * shard_rows, 16), 2 * shard_rows)
            halves = [
                jnp.concatenate([buf[n, 2 * pair + m, depth].astype(f32) for m in range(2)], axis=0)
                for n in range(2)
            ]
            for write, low, size in places:
                write(at, jnp.concatenate([half[:, low : low + size] for half in halves], axis=1).astype(bf))

    def to_square(j):
        def write(at, value):
            square[j, at, :] = value
        return write

    def to_hidden(ref):
        def write(at, value):
            ref[at, :] = value
        return write

    regroup(
        g_one,
        [(to_square(6 + j), j * width, width) for j in range(3)]
        + [(to_square(j), (3 + j) * width, width) for j in range(2)],
    )

    act_bf = act[...].astype(bf)

    def modulate(j):
        value = dot(act_bf, square[j], 1, 0) + bias_full[5 + j : 6 + j, :]
        for l in range(own):
            modv[l, j : j + 1, :] = value[l : l + 1, :]

    modulate(0)
    modulate(1)

    @pl.loop(0, blocks)
    def _(r):
        at, b = span(r)
        value = (normed[at, :] * (1.0 + modv[b, 1:2, :]) + modv[b, 0:1, :]).astype(bf)
        mod_bf[at, :] = value
        qkv[0, at, :] = (dot(value, square[6], 1, 0) + bias_full[3:4, :]).astype(bf)
        qkv[1, at, :] = dot(value, square[7], 1, 0).astype(bf)
        qkv[2, at, :] = (dot(value, square[8], 1, 0) + bias_full[4:5, :]).astype(bf)

    two.three()
    b_g.two()

    lane = lax.broadcasted_iota(jnp.int32, (1, LANES), 1)
    masks = [(lane // HD == h).astype(f32).astype(bf) for h in range(LANES // HD)]

    def split(value):
        return jnp.concatenate([value * mask for mask in masks], axis=0)

    def side_by_side(value):
        return jnp.concatenate([value[h * sequence : (h + 1) * sequence] for h in range(len(masks))], axis=1)

    def attend(b):
        at = pl.ds(b * sequence, sequence)

        @pl.loop(0, pairs)
        def _(g):
            col = pl.ds(pl.multiple_of(g * LANES, LANES), LANES)
            scores = dot(split(qkv[0, at, col]), qkv[1, at, col], 1, 1) * score_scale
            log_total = jnp.log(jnp.sum(jnp.exp(scores), axis=-1, keepdims=True))
            mix = jnp.exp(scores - log_total)
            weights[b * pairs + g] = mix
            att[at, col] = dot(side_by_side(mix.astype(bf)), split(qkv[2, at, col]), 1, 0).astype(bf)

    attend(0)
    two.four()
    a_g.three()
    c_g.two()
    for b in range(1, own):
        attend(b)
    two.five()
    regroup(
        g_two,
        [(to_square(2 + j), j * width, width) for j in range(4)] + [(to_square(9), 4 * width, width)],
    )
    for j in range(2, 6):
        modulate(j)
    a_g.four()
    b_g.three()

    @pl.loop(0, blocks)
    def _(r):
        at, b = span(r)
        result = bias_full[1:2, :] + dot(att[at, :], square[9], 1, 1)
        attention[at, :] = result
        middle = hid[at, :] + modv[b, 2:3, :] * result
        hid[at, :] = middle
        unit, scale = norm_forward(middle)
        normed_two[at, :] = unit
        inv_two[at, :] = scale
        mod_two[at, :] = (unit * (1.0 + modv[b, 4:5, :]) + modv[b, 3:4, :]).astype(bf)
        grad = modv[b, 5:6, :] * upg[at, :]
        gff[at, :] = grad.astype(bf)
        sum_down[...] += total(grad)

    def regroup_hidden(buf, c):
        @pl.loop(0, 2 * deep)
        def _(k):
            depth, pair = k // 2, k % 2
            at = pl.ds(pl.multiple_of(k * 2 * shard_rows, 16), 2 * shard_rows)
            for n in range(2):
                value = jnp.concatenate([buf[n, 2 * pair + m, depth].astype(f32) for m in range(2)], axis=0).astype(bf)
                w_up[c, n, at, :] = value[:, :chunk]
                w_down[c, n, at, :] = value[:, chunk:]

    def put(parts, n, columns, value):
        for w in range(wide):
            piece = value[w * shard_rows : (w + 1) * shard_rows].astype(bf)
            parts[n, w % 4, w // 4, :, columns] = piece

    def forward_and_back(c):
        parts = groups[c][0]

        @pl.loop(0, 2)
        def _(n):
            at = pl.ds(pl.multiple_of(n * hidden + c * chunk, chunk), chunk)
            up_at, down_at = w_up[c, n], w_down[c, n]
            pre = dot(mod_two[...], up_at, 1, 0) + bias_up[:, at]
            tangent = jnp.tanh(GELU_K * (pre + GELU_A * pre * pre * pre))
            value = (0.5 * pre * (1.0 + tangent)).astype(bf)
            steep = 0.5 * (1.0 + tangent) + 0.5 * pre * (1.0 - tangent * tangent) * GELU_K * (
                1.0 + 3.0 * GELU_A * pre * pre
            )
            feed[...] += dot(value, down_at, 1, 1)
            put(parts, n, slice(chunk, None), dot(gff[...], value, 0, 0))
            grad = dot(gff[...], down_at, 1, 0) * steep
            sum_up[:, at] = total(grad)
            grad_bf = grad.astype(bf)
            put(parts, n, slice(0, chunk), dot(mod_two[...], grad_bf, 0, 0))
            gmod[...] += dot(grad_bf, up_at, 1, 1)

    a_g.five()
    regroup_hidden(g_a, 0)
    forward_and_back(0)
    a_s.one()
    b_g.four()
    c_g.three()
    b_g.five()
    regroup_hidden(g_b, 1)
    forward_and_back(1)
    b_s.one()
    a_s.two()
    c_g.four()
    c_g.five()
    regroup_hidden(g_c, 2)
    forward_and_back(2)
    c_s.one()
    b_s.two()
    a_s.three()

    @pl.loop(0, blocks)
    def _(r):
        at, b = span(r)
        ff = feed[at, :] + bias_full[2:3, :]
        up = upg[at, :]
        bout[:, at] = jnp.transpose(hid[at, :] + modv[b, 5:6, :] * ff)
        gm[b, 5:6, :] += total(up * ff)
        grad, unit = gmod[at, :], normed_two[at, :]
        gm[b, 3:4, :] += total(grad)
        gm[b, 4:5, :] += total(grad * unit)
        middle = up + norm_backward(grad * (1.0 + modv[b, 4:5, :]), unit, inv_two[at, :])
        upg[at, :] = middle
        gm[b, 2:3, :] += total(middle * attention[at, :])
        grad_att = modv[b, 2:3, :] * middle
        sum_out[...] += total(grad_att)
        grad_bf = grad_att.astype(bf)
        gatt[at, :] = grad_bf
        gattended[at, :] = dot(grad_bf, square[9], 1, 0).astype(bf)

    def swap_out(src, dst, which):
        spot.push(src.at[their_rows], dst.at[:, mine], swap_send.at[which], swap_recv.at[which], spot.me, other)
        keep = pltpu.make_async_copy(src.at[my_rows], dst.at[:, mine], local.at[which])
        keep.start()
        keeps.append(keep)

    swap_out(bout, block_half, 3)

    def row_pieces(ref, low, value):
        for k in range(value.shape[1] // LANES):
            ref[low + k : low + k + 1, :] = value[:, k * LANES : (k + 1) * LANES]

    for l in range(own):
        for j in range(4):
            row_pieces(early_rows, (l * 4 + j) * thirds, gm[l, 2 + j : 3 + j, :])
        row_pieces(early_rows, (own * 4 + l) * thirds, act[l : l + 1, :])
        code = jnp.full((1, LANES), my_labels[l], jnp.int32)
        low = own * 5 * thirds
        early_rows[low + l : low + l + 1, :] = (code // 256).astype(f32)
        early_rows[low + own + l : low + own + l + 1, :] = (code % 256).astype(f32)
    low = own * 5 * thirds + 2 * own
    row_pieces(early_rows, low, sum_out[...])
    row_pieces(early_rows, low + thirds, sum_down[...])
    row_pieces(early_rows, low + 2 * thirds, sum_up[...])
    early[core, xy, z] = early_rows[...].astype(bf)
    early_g.one()

    value = dot(gatt[...], att[...], 0, 0)
    for n in range(2):
        put(out_parts, n, slice(None), value[:, n * width : (n + 1) * width])
    out_s.one()
    c_s.two()
    b_s.three()
    a_s.four()
    early_g.two()

    gact = jnp.zeros((8, features), f32)

    def stack_gm(j):
        return jnp.concatenate([gm[l, j : j + 1, :] for l in range(own)] * (8 // own), axis=0).astype(bf)

    def attend_back(b):
        at = pl.ds(b * sequence, sequence)

        @pl.loop(0, pairs)
        def _(g):
            col = pl.ds(pl.multiple_of(g * LANES, LANES), LANES)
            mix = weights[b * pairs + g]
            grad_out = split(gattended[at, col])
            grad_mix = dot(grad_out, qkv[2, at, col], 1, 1)
            dots = jnp.sum(mix * grad_mix, axis=-1, keepdims=True)
            grad_scores = (mix * (grad_mix - dots) * score_scale).astype(bf)
            grad_q = dot(side_by_side(grad_scores), split(qkv[1, at, col]), 1, 0)
            grad_k = dot(grad_scores, split(qkv[0, at, col]), 0, 0)
            grad_v = dot(mix.astype(bf), grad_out, 0, 0)
            gproj[0, at, col] = grad_q.astype(bf)
            gproj[1, at, col] = grad_k.astype(bf)
            gproj[2, at, col] = grad_v.astype(bf)
            sum_heads[0, :, col] += total(grad_q)
            sum_heads[1, :, col] += total(grad_v)

    attend_back(0)
    c_s.three()
    b_s.four()
    out_s.two()
    early_g.three()
    for b in range(1, own):
        attend_back(b)
    c_s.four()
    out_s.three()
    early_g.four()

    pieces = [dot(mod_bf[...], gproj[j], 0, 0) for j in range(3)]
    for n in range(2):
        value = jnp.concatenate([piece[:, n * width : (n + 1) * width] for piece in pieces], axis=1)
        put(in_parts, n, slice(None), value)
    in_s.one()
    a_s.five()
    b_s.five()
    out_s.four()
    for j in range(2, 6):
        gact += dot(stack_gm(j), square[j], 1, 1)

    @pl.loop(0, blocks)
    def _(r):
        at, b = span(r)
        grad = sum(dot(gproj[j, at, :], square[6 + j], 1, 1) for j in range(3))
        unit = normed[at, :]
        gm[b, 0:1, :] += total(grad)
        gm[b, 1:2, :] += total(grad * unit)
        back = norm_backward(grad * (1.0 + modv[b, 1:2, :]), unit, inv[at, :])
        tout[:, at] = jnp.transpose(upg[at, :] + back)

    swap_out(tout, token_half, 4)
    in_s.two()
    for j in range(2):
        gact += dot(stack_gm(j), square[j], 1, 1)
    grad_condition = gact * slope[...]
    for l in range(own):
        for j in range(2):
            row_pieces(late_rows, (l * 2 + j) * thirds, gm[l, j : j + 1, :])
        row_pieces(late_rows, (own * 2 + l) * thirds, grad_condition[l : l + 1, :])
    for which in range(2):
        row_pieces(late_rows, (own * 3 + which) * thirds, sum_heads[which])
    late[core, xy, z] = late_rows[...].astype(bf)
    late_g.one()
    in_s.three()
    late_g.two()
    c_s.five()
    early_g.five()
    out_s.five()
    in_s.four()
    late_g.three()
    late_g.four()
    late_g.five()
    in_s.five()

    for keep in keeps[3:]:
        keep.wait()
    landed(block_half.at[:, theirs], swap_recv.at[3])
    landed(token_half.at[:, theirs], swap_recv.at[4])
    for copy in spot.waits:
        copy.wait_send()


def main_pass(
    wide, sequence, own, tokens, upstream, labels, timesteps, class_table,
    mod_w, in_w, out_w, up_w, down_w, mod_b, in_b, out_b, up_b, down_b,
):
    bf, f32 = jnp.bfloat16, jnp.float32
    deep = plane(wide)[0]
    width, both = tokens.shape
    count, features = both // 2, 2 * width
    rows, hidden = up_w.shape
    vmem = pl.BlockSpec(memory_space=pltpu.VMEM)
    anywhere = pl.BlockSpec(memory_space=pl.ANY)
    smem = pl.BlockSpec(memory_space=pltpu.SMEM)
    sds, dma, ram = jax.ShapeDtypeStruct, pltpu.SemaphoreType.DMA, pltpu.VMEM
    wide_f32, wide_bf = ram((count, features), f32), ram((count, features), bf)
    flipped = ram((features, count), f32)
    column = ram((count, 1), f32)
    three = ram((3, count, features), bf)
    gathered = lambda columns: ram((2, 4, deep, rows, columns), bf)
    scratch = [
        flipped, flipped, ram(class_table.shape, bf), ram((2, ROLE_ROWS, hidden), f32),
        ram((ROLE_ROWS, features), f32), ram((1, 2 * hidden), f32),
        gathered(5 * width), gathered(5 * width), gathered(2 * hidden // 3), gathered(2 * hidden // 3),
        gathered(2 * hidden // 3), ram((10, features, features), bf),
        ram((3, 2, features, hidden // 3), bf), ram((3, 2, features, hidden // 3), bf),
        wide_f32, wide_f32, wide_f32, column, wide_bf, wide_f32, column, wide_bf, wide_bf, wide_f32,
        wide_f32, wide_f32,
        three, wide_bf, ram((own * features // LANES, sequence * LANES // HD, sequence), f32),
        wide_bf, wide_bf, three,
        ram((own, 8, features), f32), ram((own, 8, features), f32), ram((8, features), f32),
        ram((8, features), f32), ram((2, 1, features), f32), ram((1, features), f32),
        ram((1, 2 * hidden), f32), ram((1, features), f32),
        ram((EARLY_ROWS, LANES), f32), ram((LATE_ROWS, LANES), f32), flipped, flipped,
    ]
    for columns in (2 * hidden // 3,) * 3 + (width, 3 * width):
        scratch += scatter_shapes(deep, rows, columns)
    scratch += [
        dma((7, deep - 1 + 7)), dma((7, deep - 1 + 7)), dma((5, deep + 3)), dma((5, deep + 3)),
        dma((5,)), dma((5,)), dma((5,)),
    ]
    return pl.pallas_call(
        functools.partial(main_kernel, wide, sequence),
        name="everything",
        out_shape=(
            sds((width, both), f32),
            sds((width, both), f32),
            sds((2, 4, deep, EARLY_ROWS, LANES), bf),
            sds((2, 4, deep, LATE_ROWS, LANES), bf),
            sds((rows, 2 * hidden // 3), f32),
            sds((rows, 2 * hidden // 3), f32),
            sds((rows, 2 * hidden // 3), f32),
            sds((rows, width), f32),
            sds((rows, 3 * width), f32),
        ),
        in_specs=[anywhere] * 2 + [smem] * 2 + [anywhere] + [vmem] * 10,
        out_specs=(anywhere,) * 2 + (vmem,) * 7,
        scratch_shapes=scratch,
        compiler_params=pltpu.CompilerParams(
            collective_id=0, has_side_effects=True, vmem_limit_bytes=VMEM_LIMIT
        ),
    )(
        tokens, upstream, labels, timesteps, class_table,
        mod_w, in_w, out_w, up_w, down_w, mod_b, in_b, out_b, up_b, down_b,
    )


def finish_kernel(
    wide, own, weight_scale,
    block_half, token_half, early, late, tot_a, tot_b, tot_c, tot_out, tot_in,
    block_out, token_out, cond_out, table_out, mod_out, mod_bias_out, in_out, in_bias_out,
    out_out, out_bias_out, up_out, up_bias_out, down_out, down_bias_out,
    early_f, late_f, act_t, local,
):
    bf, f32 = jnp.bfloat16, jnp.float32
    deep = plane(wide)[0]
    copies = [
        pltpu.make_async_copy(block_half, block_out, local.at[0]),
        pltpu.make_async_copy(token_half, token_out, local.at[1]),
    ]
    for copy in copies:
        copy.start()
    me, core = lax.axis_index("wide"), lax.axis_index("narrow")
    rows, hidden = up_out.shape
    width = out_out.shape[1]
    features = 2 * width
    thirds = features // LANES
    devices = 2 * wide

    def dot(a, b, left, right):
        return lax.dot_general(a, b, (((left,), (right,)), ((), ())), preferred_element_type=f32)

    chunk = hidden // 3
    for c, ref in enumerate([tot_a, tot_b, tot_c]):
        up_out[:, c * chunk : (c + 1) * chunk] = ref[:, :chunk] * weight_scale
        down_out[:, c * chunk : (c + 1) * chunk] = ref[:, chunk:] * weight_scale
    out_out[...] = tot_out[...] * weight_scale
    for j in range(3):
        in_out[j] = tot_in[:, j * width : (j + 1) * width] * weight_scale

    early_f[...] = early[...].astype(f32)
    late_f[...] = late[...].astype(f32)

    def everyone(ref, size, row):
        return ref[pl.ds(row, devices, stride=size), :]

    def latents(ref, size, first, step):
        return jnp.concatenate(
            [
                jnp.concatenate(
                    [everyone(ref, size, first + l * step + k) for k in range(thirds)], axis=1
                )
                for l in range(own)
            ],
            axis=0,
        )

    def half(value):
        return jnp.where(core == 0, value[:, :width], value[:, width:])

    act_t[...] = jnp.transpose(latents(early_f, EARLY_ROWS, own * 4 * thirds, thirds))
    act_mine = act_t[pl.ds(pl.multiple_of(me * rows, 8), rows), :].astype(bf)
    for j in range(6):
        if j < 2:
            grads = latents(late_f, LATE_ROWS, j * thirds, 2 * thirds)
        else:
            grads = latents(early_f, EARLY_ROWS, (j - 2) * thirds, 4 * thirds)
        grads = half(grads)
        mod_bias_out[j : j + 1, :] = jnp.sum(grads, axis=0, keepdims=True) * weight_scale
        mod_out[j] = dot(act_mine, grads.astype(bf), 1, 0) * weight_scale

    cond = latents(late_f, LATE_ROWS, own * 2 * thirds, thirds).astype(bf)
    low = own * 5 * thirds
    code = jnp.concatenate(
        [
            everyone(early_f, EARLY_ROWS, low + l) * 256.0 + everyone(early_f, EARLY_ROWS, low + own + l)
            for l in range(own)
        ],
        axis=0,
    )
    classes = table_out.shape[0]
    for first in range(0, classes, LANES):
        size = min(LANES, classes - first)
        names = lax.broadcasted_iota(jnp.int32, code.shape, 1).astype(f32) + float(first)
        hot = jnp.where(code == names, 1.0, 0.0).astype(bf)
        table_out[first : first + size, :] = dot(hot, cond, 0, 0)[:size]

    spot_xy, spot_z = me % 4, me // 4
    for n in range(2):
        seat = (n * 4 + spot_xy) * deep + spot_z
        for l in range(own):
            first = seat * LATE_ROWS + (own * 2 + l) * thirds
            for k in range(thirds):
                cond_out[n * own + l : n * own + l + 1, k * LANES : (k + 1) * LANES] = late_f[
                    pl.ds(first + k, 1), :
                ]

    def sums(ref, size, low, many):
        return [
            jnp.sum(everyone(ref, size, low + k), axis=0, keepdims=True) * weight_scale for k in range(many)
        ]

    low = own * 5 * thirds + 2 * own
    out_bias_out[...] = half(jnp.concatenate(sums(early_f, EARLY_ROWS, low, thirds), axis=1))
    down_bias_out[...] = half(jnp.concatenate(sums(early_f, EARLY_ROWS, low + thirds, thirds), axis=1))
    pieces = sums(early_f, EARLY_ROWS, low + 2 * thirds, 2 * hidden // LANES)
    many = len(pieces) // 2
    up_bias_out[...] = jnp.concatenate(
        [jnp.where(core == 0, pieces[k], pieces[many + k]) for k in range(many)], axis=1
    ).reshape(-1)
    for which in range(2):
        pieces = sums(late_f, LATE_ROWS, (own * 3 + which) * thirds, thirds)
        in_bias_out[which : which + 1, :] = half(jnp.concatenate(pieces, axis=1))
    for copy in copies:
        copy.wait()


def finish_pass(wide, own, weight_scale, classes, results):
    f32 = jnp.float32
    block_half, token_half, early, late, tot_a, tot_b, tot_c, tot_out, tot_in = results
    rows = tot_a.shape[0]
    hidden = 3 * tot_a.shape[1] // 2
    width = tot_out.shape[1]
    vmem = pl.BlockSpec(memory_space=pltpu.VMEM)
    anywhere = pl.BlockSpec(memory_space=pl.ANY)
    sds, ram = jax.ShapeDtypeStruct, pltpu.VMEM
    early, late = early.reshape(-1, LANES), late.reshape(-1, LANES)
    return pl.pallas_call(
        functools.partial(finish_kernel, wide, own, weight_scale),
        name="finish",
        out_shape=(
            sds(block_half.shape, f32),
            sds(token_half.shape, f32),
            sds((2 * own, 2 * width), f32),
            sds((classes, 2 * width), f32),
            sds((6, rows, width), f32),
            sds((6, width), f32),
            sds((3, rows, width), f32),
            sds((2, width), f32),
            sds((rows, width), f32),
            sds((1, width), f32),
            sds((rows, hidden), f32),
            sds((hidden,), f32),
            sds((rows, hidden), f32),
            sds((1, width), f32),
        ),
        in_specs=[anywhere] * 2 + [vmem] * 7,
        out_specs=(vmem,) * 14,
        scratch_shapes=[
            ram(early.shape, f32), ram(late.shape, f32), ram((2 * width, 2 * own * wide), f32),
            pltpu.SemaphoreType.DMA((2,)),
        ],
        compiler_params=pltpu.CompilerParams(vmem_limit_bytes=VMEM_LIMIT),
    )(block_half, token_half, early, late, tot_a, tot_b, tot_c, tot_out, tot_in)


def fused_shards(
    latent_tokens, labels, timesteps, class_table, modulation_weight, modulation_bias, in_weight, in_bias,
    out_weight, out_bias, up_weight, up_bias, down_weight, down_bias, cotangent,
):
    wide = lax.axis_size("wide")
    own = labels.shape[0] // 2
    sequence = latent_tokens.shape[1] // labels.shape[0]
    weight_scale = (latent_tokens.shape[1] * wide) ** (-0.5)
    results = main_pass(
        wide, sequence, own, latent_tokens, cotangent, labels, timesteps, class_table,
        jnp.transpose(modulation_weight, (1, 0, 2)), jnp.transpose(in_weight, (1, 0, 2)),
        jnp.transpose(out_weight), up_weight, jnp.transpose(down_weight),
        modulation_bias, in_bias, out_bias.reshape(1, -1), up_bias, down_bias.reshape(1, -1),
    )
    outs = list(finish_pass(wide, own, weight_scale, class_table.shape[0], results))
    outs[4] = jnp.transpose(outs[4], (1, 0, 2))
    outs[6] = jnp.transpose(outs[6], (1, 0, 2))
    for n in (9, 13):
        outs[n] = outs[n].reshape(-1)
    outs[8] = jnp.transpose(outs[8])
    outs[12] = jnp.transpose(outs[12])
    return tuple(outs)


def fits(wide, features, latents):
    deep, side = plane(wide)
    rows = features // wide
    return side == 2 and deep > 1 and features % wide == 0 and rows % 8 == 0 and latents == 4 * wide


def pick(wide):
    def run(*args):
        chosen = fused_shards if fits(wide, args[3].shape[1], args[1].shape[0] * wide) else shards
        return chosen(*args)

    return run


def solution(mesh):
    return jax.shard_map(
        pick(mesh.shape["wide"]),
        mesh=mesh,
        in_specs=(
            P("narrow", "wide"),
            P("wide"),
            P("wide"),
            P(),
            P("wide", None, "narrow"),
            P(None, "narrow"),
            P("wide", None, "narrow"),
            P(None, "narrow"),
            P("narrow", "wide"),
            P("narrow"),
            P("wide", "narrow"),
            P("narrow"),
            P("narrow", "wide"),
            P("narrow"),
            P("narrow", "wide"),
        ),
        out_specs=(
            P("narrow", "wide"),
            P("narrow", "wide"),
            P("wide", None),
            P(),
            P("wide", None, "narrow"),
            P(None, "narrow"),
            P("wide", None, "narrow"),
            P(None, "narrow"),
            P("narrow", "wide"),
            P("narrow"),
            P("wide", "narrow"),
            P("narrow"),
            P("narrow", "wide"),
            P("narrow"),
        ),
        check_vma=False,
    )
```

```python
import functools
import math

import jax
import jax.numpy as jnp
from jax import lax
from jax.experimental import pallas as pl
from jax.experimental.pallas import tpu as pltpu
from jax.sharding import PartitionSpec as P

D = 384
HD = 64
LANES = 128
MESH = pl.DeviceIdType.MESH
VMEM_LIMIT = 60 * 1024 * 1024


EPS = 1e-06
GELU_K = 0.7978845608028654
GELU_A = 0.044715


def time_features(timesteps):
    half_width = D // 2
    frequencies = jnp.exp(
        jnp.arange(half_width, dtype=jnp.float32) * (-math.log(10000.0) / half_width)
    )
    angles = timesteps.astype(jnp.float32)[:, None] * frequencies[None, :]
    return jnp.concatenate([jnp.cos(angles), jnp.sin(angles)], axis=1)


def gelu_value(inputs):
    inner = GELU_K * (inputs + GELU_A * inputs * inputs * inputs)
    return 0.5 * inputs * (1.0 + jnp.tanh(inner))


def gelu_slope(inputs):
    inner = GELU_K * (inputs + GELU_A * inputs * inputs * inputs)
    tangent = jnp.tanh(inner)
    return 0.5 * (1.0 + tangent) + 0.5 * inputs * (1.0 - tangent * tangent) * GELU_K * (
        1.0 + 3.0 * GELU_A * inputs * inputs
    )


def silu_slope(inputs):
    sigmoid = jax.nn.sigmoid(inputs)
    return sigmoid * (1.0 + inputs * (1.0 - sigmoid))


def plane(wide):
    side = max(1, round((wide / 2) ** (1 / 3)))
    while wide % (side * side):
        side -= 1
    return wide // (side * side), side


class Place:
    def __init__(self, wide):
        self.deep, self.side = plane(wide)
        self.me = lax.axis_index("wide")
        self.core = lax.axis_index("narrow")
        self.z = self.me // (self.side * self.side)
        rest = self.me % (self.side * self.side)
        major, minor = rest // self.side, rest % self.side
        self.p = major + self.core * (minor - major)
        self.q = minor + self.core * (major - minor)
        self.p_stride = self.side + self.core * (1 - self.side)
        self.q_stride = 1 + self.core * (self.side - 1)

    def index(self, dz, dp, dq):
        return (
            ((self.z + dz) % self.deep) * (self.side * self.side)
            + ((self.p + dp) % self.side) * self.p_stride
            + ((self.q + dq) % self.side) * self.q_stride
        )

    def line_peers(self):
        return (
            [self.index(dz, 0, 0) for dz in range(1, self.deep)]
            + [self.index(0, dp, 0) for dp in range(1, self.side)]
            + [self.index(0, 0, dq) for dq in range(1, self.side)]
        )


def gather_kernel(
    wide, shard, tokens, upstream, biases,
    full, tokens_out, upstream_out, biases_out,
    send, recv, pair_send, pair_recv, swap_send, swap_recv, local,
):
    at = Place(wide)
    core, other = at.core, 1 - at.core
    barrier = pltpu.get_barrier_semaphore()
    peers = at.line_peers()
    for peer in peers:
        pl.semaphore_signal(barrier, 1, device_id=(peer, core), device_id_type=MESH)
    pl.semaphore_signal(barrier, 1, device_id=(at.me, other), device_id_type=MESH)
    pl.semaphore_wait(barrier, len(peers) + 1)
    waits = []
    count = 0

    def push(src, block, target):
        nonlocal count
        copy = pltpu.make_async_remote_copy(
            src, full.at[core, block], send.at[count], recv.at[block],
            device_id=(target, core), device_id_type=MESH,
        )
        copy.start()
        waits.append(copy)
        count += 1

    def share(src, block):
        copy = pltpu.make_async_remote_copy(
            src, full.at[core, block], pair_send.at[block], pair_recv.at[block],
            device_id=(at.me, other), device_id_type=MESH,
        )
        copy.start()
        waits.append(copy)

    def arrived(block):
        pltpu.make_async_copy(full.at[core, block], full.at[core, block], recv.at[block]).wait()

    for dz in range(1, at.deep):
        push(shard, at.me, at.index(dz, 0, 0))
    for dp in range(1, at.side):
        push(shard, at.me, at.index(0, dp, 0))
    for dq in range(1, at.side):
        push(shard, at.me, at.index(0, 0, dq))
    share(shard, at.me)
    half = tokens_out.shape[2]
    mine = pl.ds(pl.multiple_of(core * half, LANES), half)
    theirs = pl.ds(pl.multiple_of(other * half, LANES), half)
    for which, (src, dst) in enumerate(
        [(tokens.at[:, theirs], tokens_out), (upstream.at[:, theirs], upstream_out), (biases, biases_out)]
    ):
        copy = pltpu.make_async_remote_copy(
            src, dst.at[core], swap_send.at[which], swap_recv.at[which],
            device_id=(at.me, other), device_id_type=MESH,
        )
        copy.start()
        waits.append(copy)
    keeps = [
        pltpu.make_async_copy(src, dst, local.at[which])
        for which, (src, dst) in enumerate(
            [
                (tokens.at[:, mine], tokens_out.at[core]),
                (upstream.at[:, mine], upstream_out.at[core]),
                (biases, biases_out.at[core]),
                (shard, full.at[core, at.me]),
            ]
        )
    ]
    for keep in keeps:
        keep.start()
    for dz in range(1, at.deep):
        block = at.index(dz, 0, 0)
        arrived(block)
        for dp in range(1, at.side):
            push(full.at[core, block], block, at.index(0, dp, 0))
        for dq in range(1, at.side):
            push(full.at[core, block], block, at.index(0, 0, dq))
        share(full.at[core, block], block)
    for dz in range(at.deep):
        for dp in range(1, at.side):
            block = at.index(dz, dp, 0)
            arrived(block)
            for dq in range(1, at.side):
                push(full.at[core, block], block, at.index(0, 0, dq))
            share(full.at[core, block], block)
    for dz in range(at.deep):
        for dq in range(1, at.side):
            for dp in range(at.side):
                block = at.index(dz, dp, dq)
                arrived(block)
                share(full.at[core, block], block)
    for keep in keeps:
        keep.wait()
    for copy in waits:
        copy.wait_send()
    for block in range(wide):
        pltpu.make_async_copy(full.at[core, block], full.at[core, block], pair_recv.at[block]).wait()
    for which, (src, dst) in enumerate(
        [(tokens_out.at[core], None), (upstream_out.at[core], None), (biases_out.at[core], None)]
    ):
        pltpu.make_async_copy(src, src, swap_recv.at[which]).wait()


def gather_all(wide, shard, tokens, upstream, biases):
    rows, columns = shard.shape
    features, count = tokens.shape
    deep, side = plane(wide)
    sends = wide * (deep + 2 * side)
    vmem = pl.BlockSpec(memory_space=pltpu.VMEM)
    return pl.pallas_call(
        functools.partial(gather_kernel, wide),
        name="gather",
        out_shape=(
            jax.ShapeDtypeStruct((2, wide, rows, columns), shard.dtype),
            jax.ShapeDtypeStruct((2, features, count // 2), tokens.dtype),
            jax.ShapeDtypeStruct((2, features, count // 2), tokens.dtype),
            jax.ShapeDtypeStruct((2,) + biases.shape, biases.dtype),
        ),
        in_specs=[vmem] * 4,
        out_specs=(vmem,) * 4,
        scratch_shapes=[
            pltpu.SemaphoreType.DMA((sends,)),
            pltpu.SemaphoreType.DMA((wide,)),
            pltpu.SemaphoreType.DMA((wide,)),
            pltpu.SemaphoreType.DMA((wide,)),
            pltpu.SemaphoreType.DMA((3,)),
            pltpu.SemaphoreType.DMA((3,)),
            pltpu.SemaphoreType.DMA((4,)),
        ],
        compiler_params=pltpu.CompilerParams(
            collective_id=0, has_side_effects=True, vmem_limit_bytes=VMEM_LIMIT
        ),
    )(shard, tokens, upstream, biases)


def scatter_kernel(
    wide, parts, message, block_out, token_out,
    total, messages, block_half, token_half,
    from_pair, from_q, from_p, from_z, sums,
    send, pair_send, pair_recv, q_recv, p_recv, z_recv,
    note_send, note_recv, swap_send, swap_recv, local,
):
    at = Place(wide)
    core, other = at.core, 1 - at.core
    barrier = pltpu.get_barrier_semaphore()
    for step in range(wide):
        peer = (at.me + step) % wide
        if step:
            pl.semaphore_signal(barrier, 1, device_id=(peer, core), device_id_type=MESH)
        pl.semaphore_signal(barrier, 1, device_id=(peer, other), device_id_type=MESH)
    pl.semaphore_wait(barrier, 2 * wide - 1)
    waits = []

    deep, side = at.deep, at.side
    order = (
        [(dz, dp, dq) for dq in range(1, side) for dp in range(side) for dz in range(deep)]
        + [(dz, dp, 0) for dp in range(1, side) for dz in range(deep)]
        + [(dz, 0, 0) for dz in range(1, deep)]
        + [(0, 0, 0)]
    )
    for dz, dp, dq in order:
        block = at.index(dz, dp, dq)
        copy = pltpu.make_async_remote_copy(
            parts.at[other, block], from_pair.at[block], pair_send.at[block], pair_recv.at[block],
            device_id=(at.me, other), device_id_type=MESH,
        )
        copy.start()
        waits.append(copy)
    for step in range(wide):
        peer = (at.me + step) % wide
        for flip in range(2):
            if step == 0 and flip == 0:
                continue
            seat = core if flip == 0 else other
            copy = pltpu.make_async_remote_copy(
                message.at[seat], messages.at[at.me, core],
                note_send.at[step, flip], note_recv.at[at.me, core],
                device_id=(peer, seat), device_id_type=MESH,
            )
            copy.start()
            waits.append(copy)
    half = block_out.shape[0] // 2
    span = block_out.shape[1]
    columns = pl.ds(pl.multiple_of(core * span, LANES), span)
    mine = pl.ds(pl.multiple_of(core * half, 8), half)
    theirs = pl.ds(pl.multiple_of(other * half, 8), half)
    keeps = [pltpu.make_async_copy(message.at[core], messages.at[at.me, core], local.at[2])]
    for which, (src, dst) in enumerate([(block_out, block_half), (token_out, token_half)]):
        copy = pltpu.make_async_remote_copy(
            src.at[theirs], dst.at[:, columns], swap_send.at[which], swap_recv.at[which],
            device_id=(at.me, other), device_id_type=MESH,
        )
        copy.start()
        waits.append(copy)
        keeps.append(pltpu.make_async_copy(src.at[mine], dst.at[:, columns], local.at[which]))
    for keep in keeps:
        keep.start()

    def landed(ref, sem):
        pltpu.make_async_copy(ref, ref, sem).wait()

    f32 = jnp.float32
    for number, (dz, dp, dq) in enumerate(order):
        block = at.index(dz, dp, dq)
        landed(from_pair.at[block], pair_recv.at[block])
        value = parts[core, block].astype(f32) + from_pair[block].astype(f32)
        zs, ps = (at.z + dz) % deep, (at.p + dp) % side
        if dq == 0:
            for s in range(side - 1):
                landed(from_q.at[s, zs, ps], q_recv.at[s, zs, ps])
                value += from_q[s, zs, ps].astype(f32)
            if dp == 0:
                for s in range(side - 1):
                    landed(from_p.at[s, zs], p_recv.at[s, zs])
                    value += from_p[s, zs].astype(f32)
        if dq:
            target, slot, sem = (
                at.index(0, 0, dq), from_q.at[side - 1 - dq, zs, ps], q_recv.at[side - 1 - dq, zs, ps]
            )
        elif dp:
            target, slot, sem = (
                at.index(0, dp, 0), from_p.at[side - 1 - dp, zs], p_recv.at[side - 1 - dp, zs]
            )
        elif dz:
            target, slot, sem = at.index(dz, 0, 0), from_z.at[deep - 1 - dz], z_recv.at[deep - 1 - dz]
        else:
            for s in range(deep - 1):
                landed(from_z.at[s], z_recv.at[s])
                value += from_z[s].astype(f32)
            total[...] = value
            continue
        sums[block] = value.astype(jnp.bfloat16)
        copy = pltpu.make_async_remote_copy(
            sums.at[block], slot, send.at[number], sem,
            device_id=(target, core), device_id_type=MESH,
        )
        copy.start()
        waits.append(copy)
    for keep in keeps:
        keep.wait()
    for copy in waits:
        copy.wait_send()
    for step in range(wide):
        peer = (at.me + step) % wide
        if step:
            landed(messages.at[peer, core], note_recv.at[peer, core])
        landed(messages.at[peer, other], note_recv.at[peer, other])
    spare = pl.ds(pl.multiple_of(other * span, LANES), span)
    landed(block_half.at[:, spare], swap_recv.at[0])
    landed(token_half.at[:, spare], swap_recv.at[1])


def scatter_all(wide, parts, message, block_out, token_out):
    rows, columns = parts.shape[2:]
    features, count = block_out.shape
    deep, side = plane(wide)
    vmem = pl.BlockSpec(memory_space=pltpu.VMEM)
    bf, f32 = jnp.bfloat16, jnp.float32
    dma = pltpu.SemaphoreType.DMA
    return pl.pallas_call(
        functools.partial(scatter_kernel, wide),
        name="scatter",
        out_shape=(
            jax.ShapeDtypeStruct((rows, columns), f32),
            jax.ShapeDtypeStruct((wide,) + message.shape, bf),
            jax.ShapeDtypeStruct((features // 2, 2 * count), f32),
            jax.ShapeDtypeStruct((features // 2, 2 * count), f32),
        ),
        in_specs=[vmem] * 4,
        out_specs=(vmem,) * 4,
        scratch_shapes=[
            pltpu.VMEM((wide, rows, columns), bf),
            pltpu.VMEM((max(side - 1, 1), deep, side, rows, columns), bf),
            pltpu.VMEM((max(side - 1, 1), deep, rows, columns), bf),
            pltpu.VMEM((max(deep - 1, 1), rows, columns), bf),
            pltpu.VMEM((wide, rows, columns), bf),
            dma((wide,)),
            dma((wide,)),
            dma((wide,)),
            dma((max(side - 1, 1), deep, side)),
            dma((max(side - 1, 1), deep)),
            dma((max(deep - 1, 1),)),
            dma((wide, 2)),
            dma((wide, 2)),
            dma((2,)),
            dma((2,)),
            dma((3,)),
        ],
        compiler_params=pltpu.CompilerParams(
            collective_id=1, has_side_effects=True, vmem_limit_bytes=VMEM_LIMIT
        ),
    )(parts, message, block_out, token_out)


def norm_forward(values):
    average = jnp.mean(values, axis=-1, keepdims=True)
    centred = values - average
    inv_std = lax.rsqrt(jnp.mean(centred * centred, axis=-1, keepdims=True) + EPS)
    return centred * inv_std, inv_std


def norm_backward(grad_norm, normed, inv_std):
    first = jnp.mean(grad_norm, axis=-1, keepdims=True)
    second = jnp.mean(grad_norm * normed, axis=-1, keepdims=True)
    return inv_std * (grad_norm - first - normed * second)


def block_kernel(
    own, sequence, width, hidden,
    tokens, upstream, full, modulation, bias_in, bias_out, bias_up, bias_down,
    block_out, token_out, parts, grad_mod, sum_heads, sum_out, sum_up, sum_down,
    hid, upg, normed, inv, mod_bf, normed_two, inv_two, mod_two, gff, attention, feed, gmod,
    qkv, att_heads, att, weights, gatt_heads, gatt, gproj_heads, gproj,
):
    bf, f32 = jnp.bfloat16, jnp.float32
    features = 2 * width
    heads = features // HD
    per_half = heads // 2
    count = own * sequence
    score_scale = HD ** (-0.5)
    rows = LANES if sequence % LANES == 0 else sequence
    blocks = count // rows
    chunk = 256 if hidden % 256 == 0 else hidden
    chunks = hidden // chunk
    in_at, out_at = 2 * hidden, 2 * hidden + 3 * width

    def dot(a, b, left, right):
        return lax.dot_general(a, b, (((left,), (right,)), ((), ())), preferred_element_type=f32)

    def total(value):
        return jnp.sum(value, axis=0, keepdims=True)

    grad_mod[...] = jnp.zeros_like(grad_mod)
    sum_heads[...] = jnp.zeros_like(sum_heads)
    sum_out[...] = jnp.zeros_like(sum_out)
    sum_down[...] = jnp.zeros_like(sum_down)
    feed[...] = jnp.zeros_like(feed)
    gmod[...] = jnp.zeros_like(gmod)

    def span(r):
        return pl.ds(pl.multiple_of(r * rows, rows), rows), (r * rows) // sequence

    @pl.loop(0, blocks)
    def _(r):
        at, b = span(r)
        values = jnp.transpose(tokens[:, at])
        hid[at, :] = values
        unit, scale = norm_forward(values)
        normed[at, :] = unit
        inv[at, :] = scale
        mod_bf[at, :] = (unit * (1.0 + modulation[b, 1:2, :]) + modulation[b, 0:1, :]).astype(bf)
        up = jnp.transpose(upstream[:, at])
        upg[at, :] = up
        grad = modulation[b, 5:6, :] * up
        gff[at, :] = grad.astype(bf)
        sum_down[...] += total(grad)

    @pl.loop(0, blocks)
    def _(r):
        at, b = span(r)
        for n in range(2):
            out = dot(mod_bf[at, :], full[n, :, in_at:out_at], 1, 0)
            for j in range(3):
                for h in range(per_half):
                    low = j * width + h * HD
                    piece = out[:, low : low + HD]
                    if j != 1:
                        piece = piece + bias_in[j // 2, n * per_half + h]
                    qkv[j, n * per_half + h, at, :] = piece.astype(bf)

    @pl.loop(0, own * heads)
    def _(i):
        b, h = i // heads, i % heads
        at = pl.ds(pl.multiple_of(b * sequence, sequence), sequence)
        scores = dot(qkv[0, h, at, :], qkv[1, h, at, :], 1, 1) * score_scale
        log_total = jnp.log(jnp.sum(jnp.exp(scores), axis=-1, keepdims=True))
        mix = jnp.exp(scores - log_total)
        weights[i] = mix
        att_heads[h, at, :] = dot(mix.astype(bf), qkv[2, h, at, :], 1, 0).astype(bf)

    for n in range(2):
        att[n] = jnp.concatenate([att_heads[n * per_half + h] for h in range(per_half)], axis=1)

    @pl.loop(0, blocks)
    def _(r):
        at, b = span(r)
        result = bias_out[...] + sum(
            dot(att[n, at, :], full[n, :, out_at : out_at + width], 1, 1) for n in range(2)
        )
        attention[at, :] = result
        middle = hid[at, :] + modulation[b, 2:3, :] * result
        hid[at, :] = middle
        unit, scale = norm_forward(middle)
        normed_two[at, :] = unit
        inv_two[at, :] = scale
        mod_two[at, :] = (unit * (1.0 + modulation[b, 4:5, :]) + modulation[b, 3:4, :]).astype(bf)

    @pl.loop(0, 2 * chunks)
    def _(i):
        n, c = i // chunks, i % chunks
        at = pl.ds(pl.multiple_of(c * chunk, chunk), chunk)
        down_at = pl.ds(pl.multiple_of(hidden + c * chunk, chunk), chunk)
        up_w, down_w = full[n, :, at], full[n, :, down_at]
        pre = dot(mod_two[...], up_w, 1, 0) + bias_up[n, :, at]
        tangent = jnp.tanh(GELU_K * (pre + GELU_A * pre * pre * pre))
        act = (0.5 * pre * (1.0 + tangent)).astype(bf)
        slope = 0.5 * (1.0 + tangent) + 0.5 * pre * (1.0 - tangent * tangent) * GELU_K * (
            1.0 + 3.0 * GELU_A * pre * pre
        )
        feed[...] += dot(act, down_w, 1, 1)
        parts[n, :, down_at] = dot(gff[...], act, 0, 0).astype(bf)
        grad = dot(gff[...], down_w, 1, 0) * slope
        sum_up[n, :, at] = total(grad)
        grad_bf = grad.astype(bf)
        parts[n, :, at] = dot(mod_two[...], grad_bf, 0, 0).astype(bf)
        gmod[...] += dot(grad_bf, up_w, 1, 1)

    @pl.loop(0, blocks)
    def _(r):
        at, b = span(r)
        ff = feed[at, :] + bias_down[...]
        up = upg[at, :]
        block_out[:, at] = jnp.transpose(hid[at, :] + modulation[b, 5:6, :] * ff)
        grad_mod[b, 5:6, :] += total(up * ff)
        grad, unit = gmod[at, :], normed_two[at, :]
        grad_mod[b, 3:4, :] += total(grad)
        grad_mod[b, 4:5, :] += total(grad * unit)
        middle = up + norm_backward(grad * (1.0 + modulation[b, 4:5, :]), unit, inv_two[at, :])
        upg[at, :] = middle
        grad_mod[b, 2:3, :] += total(middle * attention[at, :])
        grad_att = modulation[b, 2:3, :] * middle
        sum_out[...] += total(grad_att)
        grad_bf = grad_att.astype(bf)
        gatt[at, :] = grad_bf
        for n in range(2):
            out = dot(grad_bf, full[n, :, out_at : out_at + width], 1, 0).astype(bf)
            for h in range(per_half):
                gatt_heads[n * per_half + h, at, :] = out[:, h * HD : (h + 1) * HD]

    @pl.loop(0, own * heads)
    def _(i):
        b, h = i // heads, i % heads
        at = pl.ds(pl.multiple_of(b * sequence, sequence), sequence)
        mix, grad_out = weights[i], gatt_heads[h, at, :]
        grad_mix = dot(grad_out, qkv[2, h, at, :], 1, 1)
        dots = jnp.sum(mix * grad_mix, axis=-1, keepdims=True)
        grad_scores = (mix * (grad_mix - dots) * score_scale).astype(bf)
        grad_q = dot(grad_scores, qkv[1, h, at, :], 1, 0)
        grad_k = dot(grad_scores, qkv[0, h, at, :], 0, 0)
        grad_v = dot(mix.astype(bf), grad_out, 0, 0)
        gproj_heads[0, h, at, :] = grad_q.astype(bf)
        gproj_heads[1, h, at, :] = grad_k.astype(bf)
        gproj_heads[2, h, at, :] = grad_v.astype(bf)
        sum_heads[0, h] += total(grad_q)
        sum_heads[1, h] += total(grad_v)

    for n in range(2):
        gproj[n] = jnp.concatenate(
            [gproj_heads[j, n * per_half + h] for j in range(3) for h in range(per_half)], axis=1
        )
        parts[n, :, in_at:] = jnp.concatenate(
            [dot(mod_bf[...], gproj[n], 0, 0), dot(gatt[...], att[n], 0, 0)], axis=1
        ).astype(bf)

    @pl.loop(0, blocks)
    def _(r):
        at, b = span(r)
        grad = sum(dot(gproj[n, at, :], full[n, :, in_at:out_at], 1, 1) for n in range(2))
        unit = normed[at, :]
        grad_mod[b, 0:1, :] += total(grad)
        grad_mod[b, 1:2, :] += total(grad * unit)
        back = norm_backward(grad * (1.0 + modulation[b, 1:2, :]), unit, inv[at, :])
        token_out[:, at] = jnp.transpose(upg[at, :] + back)


def block_pass(
    tokens, upstream, full, modulation, bias_in, bias_out, bias_up, bias_down, own, sequence, width, hidden
):
    bf, f32 = jnp.bfloat16, jnp.float32
    features = 2 * width
    heads = features // HD
    count = own * sequence
    bias_in = jnp.transpose(bias_in.reshape(2, 2, width), (1, 0, 2)).reshape(2, heads, 1, HD)
    vmem = pl.BlockSpec(memory_space=pltpu.VMEM)
    sds = jax.ShapeDtypeStruct
    wide_f32, wide_bf = pltpu.VMEM((count, features), f32), pltpu.VMEM((count, features), bf)
    column = pltpu.VMEM((count, 1), f32)
    by_head = pltpu.VMEM((heads, count, HD), bf)
    by_head_three = pltpu.VMEM((3, heads, count, HD), bf)
    block_out, token_out, parts, grad_mod, sum_heads, sum_out, sum_up, sum_down = pl.pallas_call(
        functools.partial(block_kernel, own, sequence, width, hidden),
        name="block",
        out_shape=(
            sds((features, count), f32),
            sds((features, count), f32),
            sds((2, features, 2 * hidden + 4 * width), bf),
            sds((own, 6, features), f32),
            sds((2, heads, 1, HD), f32),
            sds((1, features), f32),
            sds((2, 1, hidden), f32),
            sds((1, features), f32),
        ),
        in_specs=[vmem] * 8,
        out_specs=(vmem,) * 8,
        scratch_shapes=[
            wide_f32, wide_f32, wide_f32, column, wide_bf, wide_f32, column, wide_bf, wide_bf, wide_f32,
            wide_f32, wide_f32,
            by_head_three, by_head, pltpu.VMEM((2, count, width), bf),
            pltpu.VMEM((own * heads, sequence, sequence), f32),
            by_head, wide_bf, by_head_three, pltpu.VMEM((2, count, 3 * width), bf),
        ],
        compiler_params=pltpu.CompilerParams(vmem_limit_bytes=VMEM_LIMIT),
    )(
        tokens, upstream, full, modulation, bias_in, bias_out.reshape(1, -1),
        bias_up.reshape(2, 1, hidden), bias_down.reshape(1, -1),
    )
    by_half = lambda value: value.reshape(2, -1)
    bias_sums = jnp.concatenate(
        [
            by_half(sum_heads[0]), by_half(sum_heads[1]), by_half(sum_out), by_half(sum_up), by_half(sum_down),
        ],
        axis=1,
    )
    return block_out, token_out, parts, grad_mod, bias_sums


def codes(values):
    return jnp.concatenate([values // 256, values % 256]).astype(jnp.bfloat16)


def shards(
    latent_tokens,
    labels,
    timesteps,
    class_table,
    modulation_weight,
    modulation_bias,
    in_weight,
    in_bias,
    out_weight,
    out_bias,
    up_weight,
    up_bias,
    down_weight,
    down_bias,
    cotangent,
):
    bf, f32 = jnp.bfloat16, jnp.float32
    wide = lax.axis_size("wide")
    me, core = lax.axis_index("wide"), lax.axis_index("narrow")
    latent_count = labels.shape[0]
    own = latent_count // 2
    width = latent_tokens.shape[0]
    hidden = up_weight.shape[1]
    local_tokens = latent_tokens.shape[1]
    sequence = local_tokens // latent_count
    weight_scale = (local_tokens * wide) ** (-0.5)
    rows = up_weight.shape[0]

    ids = jnp.concatenate([codes(labels), codes(timesteps)])
    ids = jnp.pad(ids[None, :], ((0, rows - 1), (0, LANES - ids.shape[0])))
    shard = jnp.concatenate(
        [
            up_weight,
            jnp.transpose(down_weight),
            in_weight.reshape(rows, 3 * width),
            jnp.transpose(out_weight),
            modulation_weight.reshape(rows, 6 * width),
            ids,
        ],
        axis=1,
    )
    bias_parts = [in_bias.reshape(-1), out_bias, up_bias, down_bias, modulation_bias.reshape(-1)]
    biases = jnp.concatenate(bias_parts)
    pad = -biases.shape[0] % (8 * LANES)
    biases = jnp.pad(biases, (0, pad)).reshape(-1, LANES)
    full, tokens, upstream, both = gather_all(wide, shard, latent_tokens, cotangent, biases)
    ids_all = full[0, :, 0, -LANES:].astype(jnp.int32)
    pick = lambda n: ids_all[:, n * latent_count : (n + 1) * latent_count].reshape(-1)
    labels_all = pick(0) * 256 + pick(1)
    times_all = pick(2) * 256 + pick(3)
    class_ids = jnp.arange(class_table.shape[0], dtype=jnp.int32)
    every_hot = (labels_all[:, None] == class_ids[None, :]).astype(bf)
    condition_all = jnp.dot(every_hot, class_table, preferred_element_type=f32) + time_features(
        times_all
    )
    activated_all = jax.nn.silu(condition_all).astype(bf)
    first = me * latent_count + core * own
    condition = lax.dynamic_slice_in_dim(condition_all, first, own, 0)
    activated = lax.dynamic_slice_in_dim(activated_all, first, own, 0)

    full = full.reshape(2, rows * wide, -1)
    flat = both.reshape(2, -1)
    offset = 0
    halves = []
    for part in bias_parts:
        halves.append(flat[:, offset : offset + part.shape[0]])
        offset += part.shape[0]
    bias_in, bias_out, bias_up, bias_down, bias_mod = halves
    mod_at = 2 * hidden + 4 * width
    mod_full = full[:, :, mod_at : mod_at + 6 * width]
    modulation = jnp.einsum("bd,ndf->nbf", activated, mod_full, preferred_element_type=f32) + bias_mod[:, None]
    modulation = jnp.transpose(modulation.reshape(2, own, 6, width), (1, 2, 0, 3)).reshape(own, 6, 2 * width)

    block_output, token_grads, parts, grad_modulation, bias_sums = block_pass(
        tokens.reshape(2 * width, -1), upstream.reshape(2 * width, -1), full, modulation,
        bias_in, bias_out, bias_up, bias_down, own, sequence, width, hidden,
    )

    grad_modulation_bf = grad_modulation.astype(bf)
    by_half = jnp.transpose(grad_modulation_bf.reshape(own, 6, 2, width), (2, 0, 1, 3)).reshape(2, own, 6 * width)
    grad_activated = jnp.einsum("nbf,ndf->bd", by_half, mod_full, preferred_element_type=f32)
    condition_rows = (grad_activated * silu_slope(condition) * sequence ** (-0.5)).astype(bf)
    message = jnp.concatenate(
        [
            by_half.reshape(2, -1),
            jnp.broadcast_to(condition_rows.reshape(1, -1), (2, own * 2 * width)),
            bias_sums.astype(bf),
        ],
        axis=1,
    )
    used = message.shape[1]
    message = jnp.pad(message, ((0, 0), (0, -used % (16 * LANES)))).reshape(2, -1, LANES)
    total, messages, block_half, token_half = scatter_all(
        wide, parts.reshape(2, wide, rows, -1), message, block_output, token_grads
    )
    flat_notes = messages.reshape(wide * 2, -1)
    gm_all = flat_notes[:, : own * 6 * width].reshape(wide * latent_count, 6 * width)
    cond_all = flat_notes[:, own * 6 * width : own * 8 * width].reshape(wide * latent_count, 2 * width)
    sums = jnp.sum(flat_notes[:, own * 8 * width : used].astype(f32), axis=0) * weight_scale
    act_mine = lax.dynamic_slice_in_dim(activated_all, me * rows, rows, 1)
    mod_grads = jnp.einsum("bd,bf->df", act_mine, gm_all, preferred_element_type=f32) * weight_scale
    mod_bias_grads = jnp.sum(gm_all.astype(f32), axis=0) * weight_scale
    table_grads = jnp.einsum("bc,bd->cd", every_hot, cond_all, preferred_element_type=f32)
    condition_grads = lax.dynamic_slice_in_dim(cond_all, me * latent_count, latent_count, 0).astype(f32)
    total = total * weight_scale
    up_part = total[:, :hidden]
    down_part = jnp.transpose(total[:, hidden : 2 * hidden])
    in_part = total[:, 2 * hidden : 2 * hidden + 3 * width].reshape(rows, 3, width)
    out_part = jnp.transpose(total[:, 2 * hidden + 3 * width :])
    return (
        block_half,
        token_half,
        condition_grads,
        table_grads,
        mod_grads.reshape(rows, 6, width),
        mod_bias_grads.reshape(6, width),
        in_part,
        sums[: 2 * width].reshape(2, width),
        out_part,
        sums[2 * width : 3 * width],
        up_part,
        sums[3 * width : 3 * width + hidden],
        down_part,
        sums[3 * width + hidden :],
    )


ROLE_ROWS = 16
EARLY_ROWS, LATE_ROWS = 64, 32


class Spot:
    def __init__(self, wide):
        self.deep, self.side = plane(wide)
        self.me = lax.axis_index("wide")
        self.core = lax.axis_index("narrow")
        self.other = 1 - self.core
        self.z = self.me // 4
        rest = self.me % 4
        major, minor = rest // 2, rest % 2
        self.p = major + self.core * (minor - major)
        self.q = minor + self.core * (major - minor)
        self.xy = rest
        self.waits = []

    def line(self, dp, dq):
        p, q = (self.p + dp) % 2, (self.q + dq) % 2
        return p * (2 - self.core) + q * (1 + self.core)

    def depth(self, dz):
        return (self.z + dz) % self.deep

    def device(self, dz, dp, dq):
        return self.depth(dz) * 4 + self.line(dp, dq)

    def push(self, src, dst, send, recv, target, seat):
        copy = pltpu.make_async_remote_copy(
            src, dst, send, recv, device_id=(target, seat), device_id_type=MESH
        )
        copy.start()
        self.waits.append(copy)

    def p_peer(self):
        return self.device(0, 1, 0)

    def q_peer(self):
        return self.device(0, 0, 1)

    def enter(self):
        barrier = pltpu.get_barrier_semaphore()
        peers = [self.device(dz, 0, 0) for dz in range(1, self.deep)] + [self.p_peer(), self.q_peer(), self.device(0, 1, 1)]
        for peer in peers:
            pl.semaphore_signal(barrier, 1, device_id=(peer, self.core), device_id_type=MESH)
        pl.semaphore_signal(barrier, 1, device_id=(self.me, self.other), device_id_type=MESH)
        pl.semaphore_wait(barrier, len(peers) + 1)


def landed(ref, sem):
    pltpu.make_async_copy(ref, ref, sem).wait()


class Gather:
    def __init__(self, spot, buf, send, recv, number, direct=False):
        self.spot, self.buf, self.direct = spot, buf, direct
        self.send = lambda n: send.at[number, n]
        self.recv = lambda n: recv.at[number, n]
        self.base = spot.deep - 1

    def mine(self):
        s = self.spot
        return self.buf.at[s.core, s.xy, s.z]

    def share(self, line, send, recv, target, seat):
        ref = self.buf.at[self.spot.core, line]
        self.spot.push(ref, ref, self.send(send), self.recv(recv), target, seat)

    def one(self):
        s = self.spot
        for dz in range(1, s.deep):
            s.push(self.mine(), self.mine(), self.send(dz - 1), self.recv(dz - 1), s.device(dz, 0, 0), s.core)

    def two(self):
        s, base = self.spot, self.base
        for dz in range(1, s.deep):
            landed(self.buf.at[s.core, s.xy, s.depth(-dz)], self.recv(dz - 1))
        line = s.line(0, 0)
        self.share(line, base, base, s.p_peer(), s.core)
        self.share(line, base + 1, base + 1, s.q_peer(), s.core)
        if self.direct:
            self.share(line, base + 3, base + 2, s.device(0, 1, 1), s.core)
        self.share(line, base + 2, base + 3, s.me, s.other)

    def three(self):
        s, base = self.spot, self.base
        line = s.line(1, 0)
        landed(self.buf.at[s.core, line], self.recv(base))
        if not self.direct:
            self.share(line, base + 3, base + 2, s.q_peer(), s.core)
        self.share(line, base + 4, base + 4, s.me, s.other)

    def four(self):
        s, base = self.spot, self.base
        for dp in range(2):
            line = s.line(dp, 1)
            landed(self.buf.at[s.core, line], self.recv(base + 1 + dp))
            self.share(line, base + 5 + dp, base + 5 + dp, s.me, s.other)

    def five(self):
        s, base = self.spot, self.base
        for slot, (dp, dq) in enumerate([(0, 0), (0, 1), (1, 0), (1, 1)]):
            landed(self.buf.at[s.other, s.line(dp, dq)], self.recv(base + 3 + slot))


class Scatter:
    def __init__(self, spot, parts, bufs, send, recv, number, direct=False):
        self.spot, self.parts, self.direct = spot, parts, direct
        self.from_pair, self.to_q, self.from_q, self.to_p, self.from_p, self.to_z, self.from_z, self.total = bufs
        self.send = lambda n: send.at[number, n]
        self.recv = lambda n: recv.at[number, n]

    def pair(self, line):
        f32 = jnp.float32
        return self.parts[self.spot.core, line].astype(f32) + self.from_pair[line].astype(f32)

    def one(self):
        s = self.spot
        s.push(self.parts.at[s.other], self.from_pair, self.send(0), self.recv(0), s.me, s.other)

    def two(self):
        s, bf = self.spot, jnp.bfloat16
        landed(self.from_pair, self.recv(0))
        for dp in (1, 0):
            self.to_q[dp] = self.pair(s.line(dp, 1)).astype(bf)
            target = s.device(0, dp, 1) if self.direct else s.q_peer()
            s.push(self.to_q.at[dp], self.from_q.at[dp], self.send(1 + dp), self.recv(1 + dp), target, s.core)
        if self.direct:
            self.to_p[...] = self.pair(s.line(1, 0)).astype(bf)
            s.push(self.to_p, self.from_p, self.send(3), self.recv(3), s.p_peer(), s.core)

    def three(self):
        s = self.spot
        landed(self.from_q.at[1], self.recv(2))
        if not self.direct:
            value = self.pair(s.line(1, 0)) + self.from_q[1].astype(jnp.float32)
            self.to_p[...] = value.astype(jnp.bfloat16)
            s.push(self.to_p, self.from_p, self.send(3), self.recv(3), s.p_peer(), s.core)

    def four(self):
        s, f32 = self.spot, jnp.float32
        landed(self.from_q.at[0], self.recv(1))
        landed(self.from_p, self.recv(3))
        for dz in list(range(1, s.deep)) + [0]:
            z = s.depth(dz)
            value = self.parts[s.core, s.xy, z].astype(f32) + self.from_pair[s.xy, z].astype(f32)
            value = value + self.from_q[0, z].astype(f32) + self.from_p[z].astype(f32)
            if self.direct:
                value = value + self.from_q[1, z].astype(f32)
            if dz:
                self.to_z[dz - 1] = value.astype(jnp.bfloat16)
                s.push(
                    self.to_z.at[dz - 1], self.from_z.at[dz - 1], self.send(3 + dz), self.recv(3 + dz),
                    s.device(dz, 0, 0), s.core,
                )
            else:
                self.total[...] = value

    def five(self):
        s = self.spot
        for dz in range(1, s.deep):
            landed(self.from_z.at[dz - 1], self.recv(3 + dz))
        value = self.total[...]
        for dz in range(1, s.deep):
            value = value + self.from_z[dz - 1].astype(jnp.float32)
        self.total[...] = value


def scatter_shapes(deep, rows, columns):
    bf = jnp.bfloat16
    return [
        pltpu.VMEM((2, 4, deep, rows, columns), bf),
        pltpu.VMEM((4, deep, rows, columns), bf),
        pltpu.VMEM((2, deep, rows, columns), bf),
        pltpu.VMEM((2, deep, rows, columns), bf),
        pltpu.VMEM((deep, rows, columns), bf),
        pltpu.VMEM((deep, rows, columns), bf),
        pltpu.VMEM((deep - 1, rows, columns), bf),
        pltpu.VMEM((deep - 1, rows, columns), bf),
    ]


def main_kernel(
    wide, sequence,
    tokens, upstream, labels, timesteps, class_table,
    mod_w, in_w, out_w, up_w, down_w, mod_b, in_b, out_b, up_b, down_b,
    block_half, token_half, early, late, tot_a, tot_b, tot_c, tot_out, tot_in,
    tok, ups, table, bias_pack, bias_full, bias_up,
    g_one, g_two, g_a, g_b, g_c, square, w_up, w_down,
    hid, upg, normed, inv, mod_bf, normed_two, inv_two, mod_two, gff, attention, feed, gmod,
    qkv, att, weights, gatt, gattended, gproj,
    modv, gm, act, slope, sum_heads, sum_out, sum_up, sum_down, early_rows, late_rows, bout, tout,
    *rest,
):
    bf, f32 = jnp.bfloat16, jnp.float32
    groups = [rest[8 * n : 8 * n + 8] for n in range(5)]
    out_parts, in_parts = groups[3][0], groups[4][0]
    g_send, g_recv, s_send, s_recv, swap_send, swap_recv, local = rest[40:]
    width, hidden = in_w.shape[2], up_w.shape[1]
    features, count = tok.shape
    shard_rows = up_w.shape[0]
    own = count // sequence
    pairs = features // LANES
    spot = Spot(wide)
    core, other, deep = spot.core, spot.other, spot.deep
    score_scale = HD ** (-0.5)
    cond_scale = sequence ** (-0.5)
    rows = LANES
    blocks = count // rows
    chunks = 3
    chunk = hidden // chunks
    thirds = features // LANES

    def dot(a, b, left, right):
        return lax.dot_general(a, b, (((left,), (right,)), ((), ())), preferred_element_type=f32)

    def total(value):
        return jnp.sum(value, axis=0, keepdims=True)

    def span(r):
        return pl.ds(pl.multiple_of(r * rows, rows), rows), (r * rows) // sequence

    mine = pl.ds(pl.multiple_of(core * count, LANES), count)
    theirs = pl.ds(pl.multiple_of(other * count, LANES), count)
    my_rows = pl.ds(pl.multiple_of(core * width, 8), width)
    their_rows = pl.ds(pl.multiple_of(other * width, 8), width)
    keeps = [
        pltpu.make_async_copy(class_table, table, local.at[0]),
        pltpu.make_async_copy(tokens.at[:, mine], tok.at[my_rows], local.at[1]),
        pltpu.make_async_copy(upstream.at[:, mine], ups.at[my_rows], local.at[2]),
    ]
    for keep in keeps:
        keep.start()

    xy, z = spot.xy, spot.z
    g_one[core, xy, z] = jnp.concatenate(
        [in_w[j].astype(f32) for j in range(3)]
        + [mod_w[j].astype(f32) for j in range(2)],
        axis=1,
    ).astype(bf)
    g_two[core, xy, z] = jnp.concatenate(
        [mod_w[j].astype(f32) for j in range(2, 6)] + [out_w[...].astype(f32)], axis=1
    ).astype(bf)
    for c, buf in enumerate([g_a, g_b, g_c]):
        buf[core, xy, z, :, :chunk] = up_w[:, c * chunk : (c + 1) * chunk]
        buf[core, xy, z, :, chunk:] = down_w[:, c * chunk : (c + 1) * chunk]
    bias_pack[core] = jnp.zeros(bias_pack.shape[1:], f32)
    bias_pack[core, 0:1, :] = up_b[...].reshape(1, -1)
    bias_pack[core, 1:2, :width] = out_b[...]
    bias_pack[core, 2:3, :width] = down_b[...]
    bias_pack[core, 3:5, :width] = in_b[...]
    bias_pack[core, 5:11, :width] = mod_b[...]

    gather = [
        Gather(spot, buf, g_send, g_recv, n, direct=n > 4)
        for n, buf in enumerate([g_one, g_two, g_a, g_b, g_c, early, late])
    ]
    scatter = [
        Scatter(spot, bufs[0], tuple(bufs[1:]) + (out,), s_send, s_recv, n, direct=n == 4)
        for n, (bufs, out) in enumerate(
            zip(groups, [tot_a, tot_b, tot_c, tot_out, tot_in])
        )
    ]
    one, two, a_g, b_g, c_g, early_g, late_g = gather
    a_s, b_s, c_s, out_s, in_s = scatter

    spot.enter()
    one.one()
    spot.push(bias_pack.at[core], bias_pack.at[core], swap_send.at[0], swap_recv.at[0], spot.me, other)
    spot.push(tokens.at[:, theirs], tok.at[my_rows], swap_send.at[1], swap_recv.at[1], spot.me, other)
    spot.push(upstream.at[:, theirs], ups.at[my_rows], swap_send.at[2], swap_recv.at[2], spot.me, other)
    gm[...] = jnp.zeros_like(gm)
    sum_heads[...] = jnp.zeros_like(sum_heads)
    sum_out[...] = jnp.zeros_like(sum_out)
    sum_down[...] = jnp.zeros_like(sum_down)
    feed[...] = jnp.zeros_like(feed)
    gmod[...] = jnp.zeros_like(gmod)
    early_rows[...] = jnp.zeros_like(early_rows)
    late_rows[...] = jnp.zeros_like(late_rows)

    my_labels = [labels[core * own + l] for l in range(own)]
    my_times = [timesteps[core * own + l] for l in range(own)]

    def by_row(scalars, shape):
        row = lax.broadcasted_iota(jnp.int32, shape, 0)
        value = jnp.full(shape, -1, jnp.int32)
        for l, scalar in enumerate(scalars):
            value = jnp.where(row == l, scalar, value)
        return value

    keeps[0].wait()
    classes = class_table.shape[0]
    hot = by_row(my_labels, (8, classes)) == lax.broadcasted_iota(jnp.int32, (8, classes), 1)
    half_width = features // 2
    power = lax.broadcasted_iota(jnp.int32, (8, half_width), 1).astype(f32)
    angles = by_row(my_times, (8, half_width)).astype(f32) * jnp.exp(power * (-math.log(10000.0) / half_width))
    condition = dot(hot.astype(f32).astype(bf), table[...], 1, 0) + jnp.concatenate(
        [jnp.cos(angles), jnp.sin(angles)], axis=1
    )
    sigmoid = 1.0 / (1.0 + jnp.exp(-condition))
    act[...] = condition * sigmoid
    slope[...] = sigmoid * (1.0 + condition * (1.0 - sigmoid)) * cond_scale

    one.two()
    two.one()
    a_g.one()
    b_g.one()
    c_g.one()
    keeps[1].wait()
    keeps[2].wait()
    landed(tok.at[their_rows], swap_recv.at[1])
    landed(ups.at[their_rows], swap_recv.at[2])

    @pl.loop(0, blocks, unroll=True)
    def _(r):
        at, _ = span(r)
        values = jnp.transpose(tok[:, at])
        hid[at, :] = values
        unit, scale = norm_forward(values)
        normed[at, :] = unit
        inv[at, :] = scale
        upg[at, :] = jnp.transpose(ups[:, at])

    landed(bias_pack.at[other], swap_recv.at[0])
    bias_full[...] = jnp.concatenate([bias_pack[n, :, :width] for n in range(2)], axis=1)
    bias_up[...] = jnp.concatenate([bias_pack[n, 0:1, :] for n in range(2)], axis=1)

    one.three()
    two.two()
    one.four()
    a_g.two()
    one.five()

    def regroup(buf, places):
        @pl.loop(0, 2 * deep, unroll=4)
        def _(k):
            depth, pair = k // 2, k % 2
            at = pl.ds(pl.multiple_of(k * 2 * shard_rows, 16), 2 * shard_rows)
            halves = [
                jnp.concatenate([buf[n, 2 * pair + m, depth].astype(f32) for m in range(2)], axis=0)
                for n in range(2)
            ]
            for write, low, size in places:
                write(at, jnp.concatenate([half[:, low : low + size] for half in halves], axis=1).astype(bf))

    def to_square(j):
        def write(at, value):
            square[j, at, :] = value
        return write

    def to_hidden(ref):
        def write(at, value):
            ref[at, :] = value
        return write

    regroup(
        g_one,
        [(to_square(6 + j), j * width, width) for j in range(3)]
        + [(to_square(j), (3 + j) * width, width) for j in range(2)],
    )

    act_bf = act[...].astype(bf)

    def modulate(j):
        value = dot(act_bf, square[j], 1, 0) + bias_full[5 + j : 6 + j, :]
        for l in range(own):
            modv[l, j : j + 1, :] = value[l : l + 1, :]

    modulate(0)
    modulate(1)

    @pl.loop(0, blocks, unroll=True)
    def _(r):
        at, b = span(r)
        value = (normed[at, :] * (1.0 + modv[b, 1:2, :]) + modv[b, 0:1, :]).astype(bf)
        mod_bf[at, :] = value
        qkv[0, at, :] = (dot(value, square[6], 1, 0) + bias_full[3:4, :]).astype(bf)
        qkv[1, at, :] = dot(value, square[7], 1, 0).astype(bf)
        qkv[2, at, :] = (dot(value, square[8], 1, 0) + bias_full[4:5, :]).astype(bf)

    two.three()
    b_g.two()

    lane = lax.broadcasted_iota(jnp.int32, (1, LANES), 1)
    masks = [(lane // HD == h).astype(f32).astype(bf) for h in range(LANES // HD)]

    def split(value):
        return jnp.concatenate([value * mask for mask in masks], axis=0)

    def side_by_side(value):
        return jnp.concatenate([value[h * sequence : (h + 1) * sequence] for h in range(len(masks))], axis=1)

    def attend(b):
        at = pl.ds(b * sequence, sequence)

        @pl.loop(0, pairs)
        def _(g):
            col = pl.ds(pl.multiple_of(g * LANES, LANES), LANES)
            scores = dot(split(qkv[0, at, col]), qkv[1, at, col], 1, 1) * score_scale
            log_total = jnp.log(jnp.sum(jnp.exp(scores), axis=-1, keepdims=True))
            mix = jnp.exp(scores - log_total)
            weights[b * pairs + g] = mix
            att[at, col] = dot(side_by_side(mix.astype(bf)), split(qkv[2, at, col]), 1, 0).astype(bf)

    attend(0)
    two.four()
    a_g.three()
    c_g.two()
    for b in range(1, own):
        attend(b)
    two.five()
    regroup(
        g_two,
        [(to_square(2 + j), j * width, width) for j in range(4)] + [(to_square(9), 4 * width, width)],
    )
    for j in range(2, 6):
        modulate(j)
    a_g.four()
    b_g.three()

    @pl.loop(0, blocks, unroll=True)
    def _(r):
        at, b = span(r)
        result = bias_full[1:2, :] + dot(att[at, :], square[9], 1, 1)
        attention[at, :] = result
        middle = hid[at, :] + modv[b, 2:3, :] * result
        hid[at, :] = middle
        unit, scale = norm_forward(middle)
        normed_two[at, :] = unit
        inv_two[at, :] = scale
        mod_two[at, :] = (unit * (1.0 + modv[b, 4:5, :]) + modv[b, 3:4, :]).astype(bf)
        grad = modv[b, 5:6, :] * upg[at, :]
        gff[at, :] = grad.astype(bf)
        sum_down[...] += total(grad)

    def regroup_hidden(buf, c):
        @pl.loop(0, 2 * deep, unroll=4)
        def _(k):
            depth, pair = k // 2, k % 2
            at = pl.ds(pl.multiple_of(k * 2 * shard_rows, 16), 2 * shard_rows)
            for n in range(2):
                value = jnp.concatenate([buf[n, 2 * pair + m, depth].astype(f32) for m in range(2)], axis=0).astype(bf)
                w_up[c, n, at, :] = value[:, :chunk]
                w_down[c, n, at, :] = value[:, chunk:]

    def put(parts, n, columns, value):
        for w in range(wide):
            piece = value[w * shard_rows : (w + 1) * shard_rows].astype(bf)
            parts[n, w % 4, w // 4, :, columns] = piece

    def forward_and_back(c):
        parts = groups[c][0]

        @pl.loop(0, 2, unroll=True)
        def _(n):
            at = pl.ds(pl.multiple_of(n * hidden + c * chunk, chunk), chunk)
            up_at, down_at = w_up[c, n], w_down[c, n]
            pre = dot(mod_two[...], up_at, 1, 0) + bias_up[:, at]
            tangent = jnp.tanh(GELU_K * (pre + GELU_A * pre * pre * pre))
            value = (0.5 * pre * (1.0 + tangent)).astype(bf)
            steep = 0.5 * (1.0 + tangent) + 0.5 * pre * (1.0 - tangent * tangent) * GELU_K * (
                1.0 + 3.0 * GELU_A * pre * pre
            )
            feed[...] += dot(value, down_at, 1, 1)
            put(parts, n, slice(chunk, None), dot(gff[...], value, 0, 0))
            grad = dot(gff[...], down_at, 1, 0) * steep
            sum_up[:, at] = total(grad)
            grad_bf = grad.astype(bf)
            put(parts, n, slice(0, chunk), dot(mod_two[...], grad_bf, 0, 0))
            gmod[...] += dot(grad_bf, up_at, 1, 1)

    a_g.five()
    regroup_hidden(g_a, 0)
    forward_and_back(0)
    a_s.one()
    b_g.four()
    c_g.three()
    b_g.five()
    regroup_hidden(g_b, 1)
    forward_and_back(1)
    b_s.one()
    a_s.two()
    c_g.four()
    c_g.five()
    regroup_hidden(g_c, 2)
    forward_and_back(2)
    c_s.one()
    b_s.two()
    a_s.three()

    @pl.loop(0, blocks, unroll=True)
    def _(r):
        at, b = span(r)
        ff = feed[at, :] + bias_full[2:3, :]
        up = upg[at, :]
        bout[:, at] = jnp.transpose(hid[at, :] + modv[b, 5:6, :] * ff)
        gm[b, 5:6, :] += total(up * ff)
        grad, unit = gmod[at, :], normed_two[at, :]
        gm[b, 3:4, :] += total(grad)
        gm[b, 4:5, :] += total(grad * unit)
        middle = up + norm_backward(grad * (1.0 + modv[b, 4:5, :]), unit, inv_two[at, :])
        upg[at, :] = middle
        gm[b, 2:3, :] += total(middle * attention[at, :])
        grad_att = modv[b, 2:3, :] * middle
        sum_out[...] += total(grad_att)
        grad_bf = grad_att.astype(bf)
        gatt[at, :] = grad_bf
        gattended[at, :] = dot(grad_bf, square[9], 1, 0).astype(bf)

    def swap_out(src, dst, which):
        spot.push(src.at[their_rows], dst.at[:, mine], swap_send.at[which], swap_recv.at[which], spot.me, other)
        keep = pltpu.make_async_copy(src.at[my_rows], dst.at[:, mine], local.at[which])
        keep.start()
        keeps.append(keep)

    swap_out(bout, block_half, 3)

    def row_pieces(ref, low, value):
        for k in range(value.shape[1] // LANES):
            ref[low + k : low + k + 1, :] = value[:, k * LANES : (k + 1) * LANES]

    for l in range(own):
        for j in range(4):
            row_pieces(early_rows, (l * 4 + j) * thirds, gm[l, 2 + j : 3 + j, :])
        row_pieces(early_rows, (own * 4 + l) * thirds, act[l : l + 1, :])
        code = jnp.full((1, LANES), my_labels[l], jnp.int32)
        low = own * 5 * thirds
        early_rows[low + l : low + l + 1, :] = (code // 256).astype(f32)
        early_rows[low + own + l : low + own + l + 1, :] = (code % 256).astype(f32)
    low = own * 5 * thirds + 2 * own
    row_pieces(early_rows, low, sum_out[...])
    row_pieces(early_rows, low + thirds, sum_down[...])
    row_pieces(early_rows, low + 2 * thirds, sum_up[...])
    early[core, xy, z] = early_rows[...].astype(bf)
    early_g.one()

    value = dot(gatt[...], att[...], 0, 0)
    for n in range(2):
        put(out_parts, n, slice(None), value[:, n * width : (n + 1) * width])
    out_s.one()
    c_s.two()
    b_s.three()
    a_s.four()
    early_g.two()

    gact = jnp.zeros((8, features), f32)

    def stack_gm(j):
        return jnp.concatenate([gm[l, j : j + 1, :] for l in range(own)] * (8 // own), axis=0).astype(bf)

    def attend_back(b):
        at = pl.ds(b * sequence, sequence)

        @pl.loop(0, pairs)
        def _(g):
            col = pl.ds(pl.multiple_of(g * LANES, LANES), LANES)
            mix = weights[b * pairs + g]
            grad_out = split(gattended[at, col])
            grad_mix = dot(grad_out, qkv[2, at, col], 1, 1)
            dots = jnp.sum(mix * grad_mix, axis=-1, keepdims=True)
            grad_scores = (mix * (grad_mix - dots) * score_scale).astype(bf)
            grad_q = dot(side_by_side(grad_scores), split(qkv[1, at, col]), 1, 0)
            grad_k = dot(grad_scores, split(qkv[0, at, col]), 0, 0)
            grad_v = dot(mix.astype(bf), grad_out, 0, 0)
            gproj[0, at, col] = grad_q.astype(bf)
            gproj[1, at, col] = grad_k.astype(bf)
            gproj[2, at, col] = grad_v.astype(bf)
            sum_heads[0, :, col] += total(grad_q)
            sum_heads[1, :, col] += total(grad_v)

    attend_back(0)
    c_s.three()
    b_s.four()
    out_s.two()
    early_g.three()
    for b in range(1, own):
        attend_back(b)
    c_s.four()
    out_s.three()
    early_g.four()

    pieces = [dot(mod_bf[...], gproj[j], 0, 0) for j in range(3)]
    for n in range(2):
        value = jnp.concatenate([piece[:, n * width : (n + 1) * width] for piece in pieces], axis=1)
        put(in_parts, n, slice(None), value)
    in_s.one()
    a_s.five()
    b_s.five()
    out_s.four()
    for j in range(2, 6):
        gact += dot(stack_gm(j), square[j], 1, 1)

    @pl.loop(0, blocks, unroll=True)
    def _(r):
        at, b = span(r)
        grad = sum(dot(gproj[j, at, :], square[6 + j], 1, 1) for j in range(3))
        unit = normed[at, :]
        gm[b, 0:1, :] += total(grad)
        gm[b, 1:2, :] += total(grad * unit)
        back = norm_backward(grad * (1.0 + modv[b, 1:2, :]), unit, inv[at, :])
        tout[:, at] = jnp.transpose(upg[at, :] + back)

    swap_out(tout, token_half, 4)
    in_s.two()
    for j in range(2):
        gact += dot(stack_gm(j), square[j], 1, 1)
    grad_condition = gact * slope[...]
    for l in range(own):
        for j in range(2):
            row_pieces(late_rows, (l * 2 + j) * thirds, gm[l, j : j + 1, :])
        row_pieces(late_rows, (own * 2 + l) * thirds, grad_condition[l : l + 1, :])
    for which in range(2):
        row_pieces(late_rows, (own * 3 + which) * thirds, sum_heads[which])
    late[core, xy, z] = late_rows[...].astype(bf)
    late_g.one()
    in_s.three()
    late_g.two()
    c_s.five()
    early_g.five()
    out_s.five()
    in_s.four()
    late_g.three()
    late_g.four()
    late_g.five()
    in_s.five()

    for keep in keeps[3:]:
        keep.wait()
    landed(block_half.at[:, theirs], swap_recv.at[3])
    landed(token_half.at[:, theirs], swap_recv.at[4])
    for copy in spot.waits:
        copy.wait_send()


def main_pass(
    wide, sequence, own, tokens, upstream, labels, timesteps, class_table,
    mod_w, in_w, out_w, up_w, down_w, mod_b, in_b, out_b, up_b, down_b,
):
    bf, f32 = jnp.bfloat16, jnp.float32
    deep = plane(wide)[0]
    width, both = tokens.shape
    count, features = both // 2, 2 * width
    rows, hidden = up_w.shape
    vmem = pl.BlockSpec(memory_space=pltpu.VMEM)
    anywhere = pl.BlockSpec(memory_space=pl.ANY)
    smem = pl.BlockSpec(memory_space=pltpu.SMEM)
    sds, dma, ram = jax.ShapeDtypeStruct, pltpu.SemaphoreType.DMA, pltpu.VMEM
    wide_f32, wide_bf = ram((count, features), f32), ram((count, features), bf)
    flipped = ram((features, count), f32)
    column = ram((count, 1), f32)
    three = ram((3, count, features), bf)
    gathered = lambda columns: ram((2, 4, deep, rows, columns), bf)
    scratch = [
        flipped, flipped, ram(class_table.shape, bf), ram((2, ROLE_ROWS, hidden), f32),
        ram((ROLE_ROWS, features), f32), ram((1, 2 * hidden), f32),
        gathered(5 * width), gathered(5 * width), gathered(2 * hidden // 3), gathered(2 * hidden // 3),
        gathered(2 * hidden // 3), ram((10, features, features), bf),
        ram((3, 2, features, hidden // 3), bf), ram((3, 2, features, hidden // 3), bf),
        wide_f32, wide_f32, wide_f32, column, wide_bf, wide_f32, column, wide_bf, wide_bf, wide_f32,
        wide_f32, wide_f32,
        three, wide_bf, ram((own * features // LANES, sequence * LANES // HD, sequence), f32),
        wide_bf, wide_bf, three,
        ram((own, 8, features), f32), ram((own, 8, features), f32), ram((8, features), f32),
        ram((8, features), f32), ram((2, 1, features), f32), ram((1, features), f32),
        ram((1, 2 * hidden), f32), ram((1, features), f32),
        ram((EARLY_ROWS, LANES), f32), ram((LATE_ROWS, LANES), f32), flipped, flipped,
    ]
    for columns in (2 * hidden // 3,) * 3 + (width, 3 * width):
        scratch += scatter_shapes(deep, rows, columns)
    scratch += [
        dma((7, deep - 1 + 7)), dma((7, deep - 1 + 7)), dma((5, deep + 3)), dma((5, deep + 3)),
        dma((5,)), dma((5,)), dma((5,)),
    ]
    return pl.pallas_call(
        functools.partial(main_kernel, wide, sequence),
        name="everything",
        out_shape=(
            sds((width, both), f32),
            sds((width, both), f32),
            sds((2, 4, deep, EARLY_ROWS, LANES), bf),
            sds((2, 4, deep, LATE_ROWS, LANES), bf),
            sds((rows, 2 * hidden // 3), f32),
            sds((rows, 2 * hidden // 3), f32),
            sds((rows, 2 * hidden // 3), f32),
            sds((rows, width), f32),
            sds((rows, 3 * width), f32),
        ),
        in_specs=[anywhere] * 2 + [smem] * 2 + [anywhere] + [vmem] * 10,
        out_specs=(anywhere,) * 2 + (vmem,) * 7,
        scratch_shapes=scratch,
        compiler_params=pltpu.CompilerParams(
            collective_id=0, has_side_effects=True, vmem_limit_bytes=VMEM_LIMIT
        ),
    )(
        tokens, upstream, labels, timesteps, class_table,
        mod_w, in_w, out_w, up_w, down_w, mod_b, in_b, out_b, up_b, down_b,
    )


def finish_kernel(
    wide, own, weight_scale,
    block_half, token_half, early, late, tot_a, tot_b, tot_c, tot_out, tot_in,
    block_out, token_out, cond_out, table_out, mod_out, mod_bias_out, in_out, in_bias_out,
    out_out, out_bias_out, up_out, up_bias_out, down_out, down_bias_out,
    early_f, late_f, act_t, local,
):
    bf, f32 = jnp.bfloat16, jnp.float32
    deep = plane(wide)[0]
    copies = [
        pltpu.make_async_copy(block_half, block_out, local.at[0]),
        pltpu.make_async_copy(token_half, token_out, local.at[1]),
    ]
    for copy in copies:
        copy.start()
    me, core = lax.axis_index("wide"), lax.axis_index("narrow")
    rows, hidden = up_out.shape
    width = out_out.shape[1]
    features = 2 * width
    thirds = features // LANES
    devices = 2 * wide

    def dot(a, b, left, right):
        return lax.dot_general(a, b, (((left,), (right,)), ((), ())), preferred_element_type=f32)

    chunk = hidden // 3
    for c, ref in enumerate([tot_a, tot_b, tot_c]):
        up_out[:, c * chunk : (c + 1) * chunk] = ref[:, :chunk] * weight_scale
        down_out[:, c * chunk : (c + 1) * chunk] = ref[:, chunk:] * weight_scale
    out_out[...] = tot_out[...] * weight_scale
    for j in range(3):
        in_out[j] = tot_in[:, j * width : (j + 1) * width] * weight_scale

    early_f[...] = early[...].astype(f32)
    late_f[...] = late[...].astype(f32)

    def everyone(ref, size, row):
        return ref[pl.ds(row, devices, stride=size), :]

    def latents(ref, size, first, step):
        return jnp.concatenate(
            [
                jnp.concatenate(
                    [everyone(ref, size, first + l * step + k) for k in range(thirds)], axis=1
                )
                for l in range(own)
            ],
            axis=0,
        )

    def half(value):
        return jnp.where(core == 0, value[:, :width], value[:, width:])

    act_t[...] = jnp.transpose(latents(early_f, EARLY_ROWS, own * 4 * thirds, thirds))
    act_mine = act_t[pl.ds(pl.multiple_of(me * rows, 8), rows), :].astype(bf)
    for j in range(6):
        if j < 2:
            grads = latents(late_f, LATE_ROWS, j * thirds, 2 * thirds)
        else:
            grads = latents(early_f, EARLY_ROWS, (j - 2) * thirds, 4 * thirds)
        grads = half(grads)
        mod_bias_out[j : j + 1, :] = jnp.sum(grads, axis=0, keepdims=True) * weight_scale
        mod_out[j] = dot(act_mine, grads.astype(bf), 1, 0) * weight_scale

    cond = latents(late_f, LATE_ROWS, own * 2 * thirds, thirds).astype(bf)
    low = own * 5 * thirds
    code = jnp.concatenate(
        [
            everyone(early_f, EARLY_ROWS, low + l) * 256.0 + everyone(early_f, EARLY_ROWS, low + own + l)
            for l in range(own)
        ],
        axis=0,
    )
    classes = table_out.shape[0]
    for first in range(0, classes, LANES):
        size = min(LANES, classes - first)
        names = lax.broadcasted_iota(jnp.int32, code.shape, 1).astype(f32) + float(first)
        hot = jnp.where(code == names, 1.0, 0.0).astype(bf)
        table_out[first : first + size, :] = dot(hot, cond, 0, 0)[:size]

    spot_xy, spot_z = me % 4, me // 4
    for n in range(2):
        seat = (n * 4 + spot_xy) * deep + spot_z
        for l in range(own):
            first = seat * LATE_ROWS + (own * 2 + l) * thirds
            for k in range(thirds):
                cond_out[n * own + l : n * own + l + 1, k * LANES : (k + 1) * LANES] = late_f[
                    pl.ds(first + k, 1), :
                ]

    def sums(ref, size, low, many):
        return [
            jnp.sum(everyone(ref, size, low + k), axis=0, keepdims=True) * weight_scale for k in range(many)
        ]

    low = own * 5 * thirds + 2 * own
    out_bias_out[...] = half(jnp.concatenate(sums(early_f, EARLY_ROWS, low, thirds), axis=1))
    down_bias_out[...] = half(jnp.concatenate(sums(early_f, EARLY_ROWS, low + thirds, thirds), axis=1))
    pieces = sums(early_f, EARLY_ROWS, low + 2 * thirds, 2 * hidden // LANES)
    many = len(pieces) // 2
    up_bias_out[...] = jnp.concatenate(
        [jnp.where(core == 0, pieces[k], pieces[many + k]) for k in range(many)], axis=1
    ).reshape(-1)
    for which in range(2):
        pieces = sums(late_f, LATE_ROWS, (own * 3 + which) * thirds, thirds)
        in_bias_out[which : which + 1, :] = half(jnp.concatenate(pieces, axis=1))
    for copy in copies:
        copy.wait()


def finish_pass(wide, own, weight_scale, classes, results):
    f32 = jnp.float32
    block_half, token_half, early, late, tot_a, tot_b, tot_c, tot_out, tot_in = results
    rows = tot_a.shape[0]
    hidden = 3 * tot_a.shape[1] // 2
    width = tot_out.shape[1]
    vmem = pl.BlockSpec(memory_space=pltpu.VMEM)
    anywhere = pl.BlockSpec(memory_space=pl.ANY)
    sds, ram = jax.ShapeDtypeStruct, pltpu.VMEM
    early, late = early.reshape(-1, LANES), late.reshape(-1, LANES)
    return pl.pallas_call(
        functools.partial(finish_kernel, wide, own, weight_scale),
        name="finish",
        out_shape=(
            sds(block_half.shape, f32),
            sds(token_half.shape, f32),
            sds((2 * own, 2 * width), f32),
            sds((classes, 2 * width), f32),
            sds((6, rows, width), f32),
            sds((6, width), f32),
            sds((3, rows, width), f32),
            sds((2, width), f32),
            sds((rows, width), f32),
            sds((1, width), f32),
            sds((rows, hidden), f32),
            sds((hidden,), f32),
            sds((rows, hidden), f32),
            sds((1, width), f32),
        ),
        in_specs=[anywhere] * 2 + [vmem] * 7,
        out_specs=(vmem,) * 14,
        scratch_shapes=[
            ram(early.shape, f32), ram(late.shape, f32), ram((2 * width, 2 * own * wide), f32),
            pltpu.SemaphoreType.DMA((2,)),
        ],
        compiler_params=pltpu.CompilerParams(vmem_limit_bytes=VMEM_LIMIT),
    )(block_half, token_half, early, late, tot_a, tot_b, tot_c, tot_out, tot_in)


def fused_shards(
    latent_tokens, labels, timesteps, class_table, modulation_weight, modulation_bias, in_weight, in_bias,
    out_weight, out_bias, up_weight, up_bias, down_weight, down_bias, cotangent,
):
    wide = lax.axis_size("wide")
    own = labels.shape[0] // 2
    sequence = latent_tokens.shape[1] // labels.shape[0]
    weight_scale = (latent_tokens.shape[1] * wide) ** (-0.5)
    results = main_pass(
        wide, sequence, own, latent_tokens, cotangent, labels, timesteps, class_table,
        jnp.transpose(modulation_weight, (1, 0, 2)), jnp.transpose(in_weight, (1, 0, 2)),
        jnp.transpose(out_weight), up_weight, jnp.transpose(down_weight),
        modulation_bias, in_bias, out_bias.reshape(1, -1), up_bias, down_bias.reshape(1, -1),
    )
    outs = list(finish_pass(wide, own, weight_scale, class_table.shape[0], results))
    outs[4] = jnp.transpose(outs[4], (1, 0, 2))
    outs[6] = jnp.transpose(outs[6], (1, 0, 2))
    for n in (9, 13):
        outs[n] = outs[n].reshape(-1)
    outs[8] = jnp.transpose(outs[8])
    outs[12] = jnp.transpose(outs[12])
    return tuple(outs)


def fits(wide, features, latents):
    deep, side = plane(wide)
    rows = features // wide
    return side == 2 and deep > 1 and features % wide == 0 and rows % 8 == 0 and latents == 4 * wide


def pick(wide):
    def run(*args):
        chosen = fused_shards if fits(wide, args[3].shape[1], args[1].shape[0] * wide) else shards
        return chosen(*args)

    return run


def solution(mesh):
    return jax.shard_map(
        pick(mesh.shape["wide"]),
        mesh=mesh,
        in_specs=(
            P("narrow", "wide"),
            P("wide"),
            P("wide"),
            P(),
            P("wide", None, "narrow"),
            P(None, "narrow"),
            P("wide", None, "narrow"),
            P(None, "narrow"),
            P("narrow", "wide"),
            P("narrow"),
            P("wide", "narrow"),
            P("narrow"),
            P("narrow", "wide"),
            P("narrow"),
            P("narrow", "wide"),
        ),
        out_specs=(
            P("narrow", "wide"),
            P("narrow", "wide"),
            P("wide", None),
            P(),
            P("wide", None, "narrow"),
            P(None, "narrow"),
            P("wide", None, "narrow"),
            P(None, "narrow"),
            P("narrow", "wide"),
            P("narrow"),
            P("wide", "narrow"),
            P("narrow"),
            P("narrow", "wide"),
            P("narrow"),
        ),
        check_vma=False,
    )
```
